32 devices in a mesh: groups: 2 (over y), seq: 4 (over z), head: 2 (over x), sub: 2 (over core).
Axes of the slice: x: 2, y: 2, z: 4, core: 2. Of those that a mesh axis runs over, the one named last changes fastest.
Arguments:
- tokens: int32 [3, 4096], P(None, ('groups', 'seq')), parts along dimension 1, may hold values from 0 to 1023
- masked: int32 [4096], P(('groups', 'seq')), parts along dimension 0, may hold values 0 or 1
- used_frames: int32 [2], P('groups'), parts along dimension 0, may hold values from 1024 to 2048
- tables: bfloat16 [3, 1024, 1024], P(None, None, ('head', 'sub')), may hold values from -6 to 6
- mask_vec: bfloat16 [1024], P(('head', 'sub')), may hold values from -6 to 6
- attn_in: bfloat16 [3, 1024, 512], P(None, None, ('head', 'sub')), may hold values from -0.1875 to 0.1875
- head_temp: float32 [8], P(('head', 'sub')), may hold values from 12 to 28
- attn_out: bfloat16 [512, 1024], P(('head', 'sub')), may hold values from -0.25 to 0.25
- conv_in: bfloat16 [2, 1024, 1024], P(None, None, ('head', 'sub')), may hold values from -0.1875 to 0.1875
- conv_kernel: float32 [31, 1024], P(None, ('head', 'sub')), may hold values from -1 to 1
- conv_out: bfloat16 [1024, 1024], P(('head', 'sub')), may hold values from -0.1875 to 0.1875
- voc_in: bfloat16 [1024, 512], P(('head', 'sub')), may hold values from -0.1875 to 0.1875
- voc_kernel: float32 [7, 512], replicated, may hold values from -2 to 2
- voc_up: bfloat16 [512, 1536], P(('head', 'sub')), may hold values from -0.25 to 0.25
- voc_down: bfloat16 [1536, 512], P(('head', 'sub')), may hold values from -0.15625 to 0.15625
- voc_head: bfloat16 [512, 1282], P(('head', 'sub')), may hold values from -0.25 to 0.25
- head_bias: float32 [1282], replicated, may hold values from 0.5 to 2.5
Outputs:
- features: bfloat16 [4096, 1024], P(('groups', 'seq', 'head', 'sub')), parts along dimension 0
- waveform: float32 [1310720], P(('groups', 'seq', 'head', 'sub')), parts along dimension 0
The draws below stay inside these ranges and needn't reach their ends.
There are 2 independent parts, one for each index of `groups`. The reference program is written for one: setup_inputs(seed, part) draws one part's arguments, and reference() takes and returns one part's arrays. A program takes and returns all parts, laid end to end along the dimension named above; an argument that names none is the same for every part. Nothing has to cross between parts.
All inputs are finite; a program needn't handle non-finite values. No bound on the sum of `masked` on one device may be relied on, other than what follows from the above.
Results may differ from the reference program's by a relative error of at most 0.02.
Values may be sent and summed in bfloat16 or wider, within the bound.
A program may use at most 64 MiB of HBM per device.

```python
import math
import jax
import jax.numpy as jnp
import numpy as np
from jax import lax

D = 1024
H = 8
CODES = 1024
KW = 31
VW = 512
VF = 1536
VK = 7
NFFT = 1280
HOP = 320
HW = 512
BINS = 641
L = 2048
N_SEQ = 4
N_HEAD = 2
N_SUB = 2


def set_ends(values, key, smallest, top_value):
    extent = values.shape
    spot = [jax.random.randint(jax.random.fold_in(key, axis), (), 0, extent[axis]) for axis in range(len(extent))]
    values = values.at[tuple(spot)].set(smallest)
    longest = extent.index(max(extent))
    spot[longest] = (spot[longest] + 1) % extent[longest]
    return values.at[tuple(spot)].set(top_value)


def levels(own_key, shape, shards, smallest, high):
    level = 1.0
    for axis_at, shards_of in shards:
        draws = jax.random.uniform(jax.random.fold_in(jax.random.fold_in(own_key, 6), axis_at), (shards_of,), jnp.float32, smallest / len(shards), high / len(shards))
        level = level * jnp.repeat(jnp.exp(draws), shape[axis_at] // shards_of).reshape((-1,) + (1,) * (len(shape) - 1 - axis_at))
    return level


def cumulative_ranks(amount, lean):
    loads = [(1 << 20) // math.isqrt(rank ** lean) + 1 for rank in range(1, amount + 1)]
    spread = 1 + sum(loads) // (1 << 30)
    return np.cumsum(np.array([max(1, weight // spread) for weight in loads]))


def ranked(rng, dims, number_of, skew):
    table = cumulative_ranks(number_of, skew)
    lot = jax.random.randint(jax.random.fold_in(rng, 1), dims, 0, int(table[number_of - 1]))
    rank = jnp.searchsorted(jnp.asarray(table, jnp.int32), lot, side="right")
    return jax.random.permutation(jax.random.fold_in(rng, 2), number_of)[rank].astype(jnp.int32)


def centred(own_key, shape, scale, most, split=(), kind=jnp.bfloat16):
    array = jax.random.normal(own_key, shape, jnp.float32) * scale
    if len(split) > 0:
        array = levels(own_key, shape, split, -0.22, 0.18) * array
    return jnp.clip(array, min=-most, max=most).astype(kind)


def setup_inputs(seed: int = 0, part: int = 0) -> dict:
    keys = jax.random.split(jax.random.key(seed), 18)
    part_splits = jax.random.split(jax.random.fold_in(keys[17], part), 18)
    return {
        "tokens": set_ends(ranked(part_splits[0], (3, L), CODES, 2), jax.random.fold_in(part_splits[0], 3), 0, CODES - 1).astype(jnp.int32),
        "masked": set_ends((jax.random.randint(part_splits[1], (L,), 0, 2) < 1).astype(jnp.int32), jax.random.fold_in(part_splits[1], 1), 0, 1),
        "used_frames": jax.random.randint(part_splits[2], (1,), L // 2, L + 1).astype(jnp.int32),
        "tables": centred(keys[3], (3, CODES, D), 1.0, 6.0, ((2, 4),)),
        "mask_vec": centred(keys[4], (D,), 1.0, 6.0, ((0, 4),)),
        "attn_in": centred(keys[5], (3, D, HW), D ** -0.5, 0.1875, ((2, 4),)),
        "head_temp": jnp.clip(jnp.exp(math.log(28.0) - 0.84729786 * jax.random.uniform(keys[6], (H,), jnp.float32) ** levels(keys[6], (H,), ((0, 4),), -0.2, 0.2)), 12.0, 28.0),
        "attn_out": centred(keys[7], (HW, D), HW ** -0.5, 0.25, ((0, 4),)),
        "conv_in": centred(keys[8], (2, D, D), D ** -0.5, 0.1875, ((2, 4),)),
        "conv_kernel": centred(keys[9], (KW, D), KW ** -0.5, 1.0, ((1, 4),), jnp.float32),
        "conv_out": centred(keys[10], (D, D), D ** -0.5, 0.1875, ((0, 4),)),
        "voc_in": centred(keys[11], (D, VW), D ** -0.5, 0.1875, ((0, 4),)),
        "voc_kernel": centred(keys[12], (VK, VW), VK ** -0.5, 2.0, (), jnp.float32),
        "voc_up": centred(keys[13], (VW, VF), VW ** -0.5, 0.25, ((0, 4),)),
        "voc_down": centred(keys[14], (VF, VW), VF ** -0.5, 0.15625, ((0, 4),)),
        "voc_head": centred(keys[15], (VW, 2 * BINS), VW ** -0.5, 0.25, ((0, 4),)),
        "head_bias": jnp.clip(jax.random.uniform(keys[16], (2 * BINS,), jnp.float32, 0.5, 2.5), 0.5, 2.5),
    }


def layer_norm(values):
    average = lax.optimization_barrier(jnp.mean(values, axis=-1, keepdims=True))
    centered = values - average
    return centered * lax.rsqrt(lax.optimization_barrier(jnp.mean(centered * centered, axis=-1, keepdims=True)) + 1e-05)

def unit_heads(projected, head_count):
    row_count = projected.shape[0]
    split_heads = projected.reshape(row_count, head_count, projected.shape[1] // head_count)
    scaled = split_heads * lax.rsqrt(lax.optimization_barrier(jnp.sum(split_heads * split_heads, axis=-1, keepdims=True)) + 1e-06)
    return scaled.astype(jnp.bfloat16)

def depthwise(kernel, rows_in):
    tap_count = kernel.shape[0]
    half_taps = tap_count // 2
    padded_rows = jnp.pad(rows_in.astype(jnp.float32), ((half_taps, half_taps), (0, 0)))
    out_rows = rows_in.shape[0]
    result = jnp.zeros((out_rows, rows_in.shape[1]), jnp.float32)
    for offset in range(tap_count):
        result = result + kernel[offset].astype(jnp.float32) * padded_rows[offset:offset + out_rows]
    return result

def reference(tokens, masked, used_frames, tables, mask_vec, attn_in, head_temp, attn_out, conv_in, conv_kernel, conv_out, voc_in, voc_kernel, voc_up, voc_down, voc_head, head_bias):
    total_frames = tokens.shape[1]
    masked_rows = masked == 1
    level_two = jnp.where(masked_rows[:, None], mask_vec.astype(jnp.float32)[None, :], tables[2][tokens[2]].astype(jnp.float32))
    embedded = (tables[0][tokens[0]].astype(jnp.float32) + tables[1][tokens[1]].astype(jnp.float32) + level_two).astype(jnp.bfloat16)
    normed = layer_norm(embedded.astype(jnp.float32)).astype(jnp.bfloat16)
    head_count = head_temp.shape[0]
    query_normalized = unit_heads(jnp.dot(normed, attn_in[0], preferred_element_type=jnp.float32), head_count)
    key_unit = unit_heads(jnp.dot(normed, attn_in[1], preferred_element_type=jnp.float32), head_count)
    value_rows = jnp.dot(normed, attn_in[2], preferred_element_type=jnp.float32).astype(jnp.bfloat16)
    value_heads = value_rows.reshape(total_frames, head_count, -1)
    lookup_admissible_flags = jnp.arange(total_frames) < used_frames[0]
    block_rows = total_frames // N_SEQ

    def one_head(attender_element):
        asker_vectors_split, lookup_vectors_split, content_vectors_split, similarity_sharpness = attender_element

        def one_block(query_block):
            angular_similarity = jnp.dot(query_block, lookup_vectors_split.T, preferred_element_type=jnp.float32)
            attention_probabilities = jnp.where(lookup_admissible_flags[None, :], jnp.exp(similarity_sharpness * (angular_similarity - 1.0)), 0.0)
            normalizer = lax.optimization_barrier(jnp.sum(attention_probabilities, axis=1, keepdims=True))
            weighted = jnp.dot(attention_probabilities.astype(jnp.bfloat16), content_vectors_split, preferred_element_type=jnp.float32)
            return weighted / normalizer
        blocks_out = lax.map(one_block, asker_vectors_split.reshape(N_SEQ, block_rows, asker_vectors_split.shape[1]))
        return blocks_out.reshape(total_frames, asker_vectors_split.shape[1])
    per_head = lax.map(one_head, (jnp.transpose(query_normalized, (1, 0, 2)), jnp.transpose(key_unit, (1, 0, 2)), jnp.transpose(value_heads, (1, 0, 2)), head_temp))
    attended = jnp.transpose(per_head, (1, 0, 2)).reshape(total_frames, -1).astype(jnp.bfloat16)
    stream = embedded.astype(jnp.float32) + jnp.dot(attended, attn_out, preferred_element_type=jnp.float32)
    conv_normed = layer_norm(stream).astype(jnp.bfloat16)
    gate_value = jnp.dot(conv_normed, conv_in[0], preferred_element_type=jnp.float32)
    gate_signal = jnp.dot(conv_normed, conv_in[1], preferred_element_type=jnp.float32)
    gated_rows = (gate_value * jax.nn.sigmoid(gate_signal)).astype(jnp.bfloat16)
    depth_rows = depthwise(conv_kernel, gated_rows)
    activated = (depth_rows * jax.nn.sigmoid(depth_rows)).astype(jnp.bfloat16)
    group_count = N_HEAD * N_SUB
    channels = activated.shape[1] // group_count
    conv_sum = jnp.zeros(stream.shape, jnp.float32)
    for member in range(group_count):
        group_part = jnp.dot(activated[:, member * channels:(member + 1) * channels], conv_out[member * channels:(member + 1) * channels], preferred_element_type=jnp.float32).astype(jnp.bfloat16)
        conv_sum = conv_sum + lax.optimization_barrier(group_part).astype(jnp.float32)
    features = layer_norm(stream + conv_sum).astype(jnp.bfloat16)
    live_rows = (jnp.arange(total_frames) < used_frames[0])[:, None]
    base_rows = layer_norm(jnp.where(live_rows, jnp.dot(features, voc_in, preferred_element_type=jnp.float32), 0.0))
    vdepth = depthwise(voc_kernel, base_rows)
    inner_rows = layer_norm(vdepth).astype(jnp.bfloat16)
    hidden = jax.nn.gelu(jnp.dot(inner_rows, voc_up, preferred_element_type=jnp.float32), approximate=False).astype(jnp.bfloat16)
    refined = base_rows + jnp.dot(hidden, voc_down, preferred_element_type=jnp.float32)
    head_input = layer_norm(refined).astype(jnp.bfloat16)
    spectrum = jnp.dot(head_input, voc_head, preferred_element_type=jnp.float32) + head_bias
    bin_count = spectrum.shape[1] // 2
    magnitude = jnp.minimum(jnp.exp(spectrum[:, :bin_count]), 100.0)
    phase_rows = spectrum[:, bin_count:]
    real_part = magnitude * jnp.cos(phase_rows)
    imag_part = magnitude * jnp.sin(phase_rows)
    wave_rows = jnp.fft.irfft(lax.complex(real_part, imag_part), n=NFFT, axis=1)
    sample_ids = jnp.arange(NFFT).astype(jnp.float32)
    hann_window = 0.5 - 0.5 * jnp.cos(2.0 * math.pi / NFFT * sample_ids)
    intersection = NFFT // HOP
    framed = (wave_rows * hann_window[None, :]).reshape(total_frames, intersection, HOP)
    envelope = jnp.broadcast_to((hann_window * hann_window).reshape(1, intersection, HOP), framed.shape)
    padded_frames = jnp.pad(framed, ((intersection, intersection), (0, 0), (0, 0)))
    padded_env = jnp.pad(envelope, ((intersection, intersection), (0, 0), (0, 0)))
    audio_sum = jnp.zeros((total_frames, HOP), jnp.float32)
    energy = jnp.zeros((total_frames, HOP), jnp.float32)
    for quarter in range(intersection):
        begin = intersection + intersection // 2 - quarter
        audio_sum = audio_sum + padded_frames[begin:begin + total_frames, quarter]
        energy = energy + padded_env[begin:begin + total_frames, quarter]
    waveform = (audio_sum / energy).reshape(total_frames * HOP)
    return (features, waveform)
```

```python
import functools
import math

import jax
import jax.numpy as jnp
import numpy as np
from jax import lax
from jax.experimental import pallas as pl
from jax.experimental.pallas import tpu as pltpu
from jax.sharding import PartitionSpec as P

HOP = 320


MESH = pl.DeviceIdType.MESH
HALO = 32


def remote(src, dst, send_sem, recv_sem, **where):
    return pltpu.make_async_remote_copy(
        src_ref=src,
        dst_ref=dst,
        send_sem=send_sem,
        recv_sem=recv_sem,
        device_id=where,
        device_id_type=MESH,
    )


class Place:
    def __init__(self):
        self.group, self.seq = lax.axis_index("groups"), lax.axis_index("seq")
        self.head, self.sub = lax.axis_index("head"), lax.axis_index("sub")
        self.groups, self.seqs = lax.axis_size("groups"), lax.axis_size("seq")
        self.heads = lax.axis_size("head")
        self.me = self.head * 2 + self.sub
        self.partner = 1 - self.sub

    def head_at(self, step):
        return lax.rem(self.head + step, self.heads)

    def group_at(self, step):
        return lax.rem(self.group + step, self.groups)


def enter(at):
    barrier = pltpu.get_barrier_semaphore()

    def greet(**where):
        pl.semaphore_signal(barrier, inc=1, device_id=where, device_id_type=MESH)

    for step in range(1, at.heads):
        greet(head=at.head_at(step))
        greet(head=at.head_at(step), sub=at.partner)
    for step in range(1, at.groups):
        greet(groups=at.group_at(step))
    greet(sub=at.partner)

    @pl.when(at.seq > 0)
    def _():
        greet(seq=at.seq - 1)

    @pl.when(at.seq < at.seqs - 1)
    def _():
        greet(seq=at.seq + 1)

    count = 2 * (at.heads - 1) + at.groups
    count = count + jnp.where(at.seq > 0, 1, 0) + jnp.where(at.seq < at.seqs - 1, 1, 0)
    pl.semaphore_wait(barrier, count)


class Spread:
    def __init__(self, at, buffer, rows, sems):
        self.at, self.buffer, self.rows = at, buffer, rows
        self.send, self.recv = sems

    def part(self, block):
        return self.buffer.at[block, pl.ds(*self.rows)]

    def cross(self, step):
        block = self.part(self.at.me)
        return remote(
            block, block, self.send.at[step], self.recv.at[step], head=self.at.head_at(step)
        )

    def aside(self, step):
        block = self.part(self.at.head_at(self.at.heads - step) * 2 + self.at.sub)
        slot = self.at.heads + step
        return remote(block, block, self.send.at[slot], self.recv.at[slot], sub=self.at.partner)

    def start(self):
        for step in range(1, self.at.heads):
            self.cross(step).start()
        self.aside(0).start()

    def relay(self):
        for step in range(1, self.at.heads):
            self.cross(step).wait_recv()
            self.aside(step).start()

    def finish(self):
        for step in range(self.at.heads):
            if step > 0:
                self.cross(step).wait_send()
            self.aside(step).wait()


class Weight:
    def __init__(self, at, own, full, sems):
        self.at, self.own, self.full = at, own, full
        self.send, self.recv, self.local = sems
        self.length = own.shape[0] // at.groups

    def piece(self, block, part):
        start = pl.multiple_of(part * self.length, 16)
        return self.full.at[block, pl.ds(start, self.length)]

    def source(self, step):
        return self.at.head_at(self.at.heads - step) * 2 + self.at.sub

    def cross(self, step):
        start = pl.multiple_of(self.at.group * self.length, 16)
        return remote(
            self.own.at[pl.ds(start, self.length)],
            self.piece(self.at.me, self.at.group),
            self.send.at[step],
            self.recv.at[step],
            head=self.at.head_at(step),
        )

    def over(self, step, turn):
        block = self.piece(self.source(step), self.at.group)
        slot = self.at.heads + (step - 1) * self.at.groups + turn
        return remote(
            block, block, self.send.at[slot], self.recv.at[slot], groups=self.at.group_at(turn)
        )

    def aside(self, step, turn):
        part = self.at.group_at(self.at.groups - turn)
        block = self.piece(self.source(step), part)
        slot = self.at.heads * (1 + self.at.groups) + (step - 1) * self.at.groups + turn
        return remote(block, block, self.send.at[slot], self.recv.at[slot], sub=self.at.partner)

    def mine(self):
        return remote(
            self.own, self.full.at[self.at.me], self.send.at[0], self.recv.at[0], sub=self.at.partner
        )

    def kept(self):
        return pltpu.make_async_copy(self.own, self.full.at[self.at.me], self.local.at[0])

    def start(self):
        for step in range(1, self.at.heads):
            self.cross(step).start()
        self.mine().start()
        self.kept().start()

    def relay_cross(self):
        for step in range(1, self.at.heads):
            self.cross(step).wait_recv()
            for turn in range(1, self.at.groups):
                self.over(step, turn).start()
            self.aside(step, 0).start()

    def relay_over(self):
        for step in range(1, self.at.heads):
            for turn in range(1, self.at.groups):
                self.over(step, turn).wait_recv()
                self.aside(step, turn).start()

    def finish(self):
        self.mine().wait()
        self.kept().wait()
        for step in range(1, self.at.heads):
            self.cross(step).wait_send()
            for turn in range(1, self.at.groups):
                self.over(step, turn).wait_send()
            for turn in range(self.at.groups):
                self.aside(step, turn).wait()


def weight_sems(heads, groups):
    count = heads * (1 + 2 * groups)
    return [
        pltpu.SemaphoreType.DMA((count,)),
        pltpu.SemaphoreType.DMA((count,)),
        pltpu.SemaphoreType.DMA((1,)),
    ]


def norm_rows(values):
    average = jnp.mean(values, axis=-1, keepdims=True)
    centered = values - average
    return centered * lax.rsqrt(jnp.mean(centered * centered, axis=-1, keepdims=True) + 1e-05)


PIECES = 4
WEIGHTS = 6


def up_to(value, unit):
    return -(-value // unit) * unit


def synthesis_constants(bin_count, fft_size, padded_bins, padded_hop):
    parts = fft_size // HOP
    samples = np.arange(fft_size)
    window = 0.5 - 0.5 * np.cos(2.0 * np.pi / fft_size * samples)
    bins = np.arange(bin_count)[:, None]
    angle = 2.0 * np.pi / fft_size * (bins * samples[None, :] % fft_size)
    edge = (bins == 0) | (bins == bin_count - 1)
    factor = np.where(edge, 1.0, 2.0) / fft_size
    cosine = factor * np.cos(angle) * window
    sine = np.where(edge, 0.0, -factor * np.sin(angle) * window)

    def spread(table, rows, fill):
        result = np.full((rows, parts, padded_hop), fill)
        result[: table.shape[0], :, :HOP] = table.reshape(-1, parts, HOP)
        return result.reshape(rows, parts * padded_hop)

    tables = np.concatenate([spread(cosine, padded_bins, 0.0), spread(sine, padded_bins, 0.0)])
    energy = spread((window * window)[None, :], 1, 1.0).reshape(parts, padded_hop)
    energy = np.pad(energy, ((0, -parts % 8), (0, 0)), constant_values=1.0)
    return jnp.asarray(tables, jnp.bfloat16), jnp.asarray(energy, jnp.float32)


def sine_cosine(angle):
    turns = jnp.round(angle * (2.0 / math.pi))
    rest = angle - turns * 1.5703125
    rest = rest - turns * 4.837512969970703125e-4
    rest = rest - turns * 7.549789948768648e-8
    square = rest * rest
    sine = rest + rest * square * (
        -1.6666654611e-1 + square * (8.3321608736e-3 + square * -1.9515295891e-4)
    )
    cosine = 1.0 - 0.5 * square + square * square * (
        4.166664568298827e-2 + square * (-1.388731625493765e-3 + square * 2.443315711809948e-5)
    )
    quadrant = turns.astype(jnp.int32) & 3
    odd = (quadrant & 1) == 1
    sine, cosine = jnp.where(odd, cosine, sine), jnp.where(odd, sine, cosine)
    sine = jnp.where(quadrant >= 2, -sine, sine)
    cosine = jnp.where((quadrant == 1) | (quadrant == 2), -cosine, cosine)
    return sine, cosine


def mix(parts, full):
    if parts[0].shape[1] % 128 == 0:
        return jnp.dot(
            jnp.concatenate(parts, axis=1),
            full[...].reshape(-1, full.shape[2]),
            preferred_element_type=jnp.float32,
        )
    result = 0.0
    for block, part in enumerate(parts):
        result = result + jnp.dot(part, full[block], preferred_element_type=jnp.float32)
    return result


def block_kernel(sizes, *refs):
    (small_ref, env_ref, tables_hbm, attn_hbm, conv_in_hbm, conv_kernel_hbm, voc_kernel_hbm,
     dft_hbm) = refs[:8]
    owns_hbm = list(refs[8 : 8 + WEIGHTS])
    feat_out, wave_out = refs[8 + WEIGHTS : 10 + WEIGHTS]
    refs = refs[10 + WEIGHTS :]
    fulls = refs[:WEIGHTS]
    (tables_ref, attn_ref, conv_in, conv_kernel, voc_kernel, dft, head_raw, head_wide, head_own,
     tokh, emb, att, kvbuf, q_scr, acc, l_acc, stream, gated, win, act, audio) = refs[
        WEIGHTS : WEIGHTS + 21
    ]
    (load_sems, tok_send, tok_recv, e_send, e_recv, a_send, a_recv, r_send, r_recv, l_send,
     l_recv, s_send, s_recv) = refs[WEIGHTS + 21 : WEIGHTS + 34]
    wsems = refs[WEIGHTS + 34 :]
    local_heads, head_size, bin_count, padded_bins, fft_size = sizes
    at = Place()
    blocks, total, columns = emb.shape
    rows = total - 2 * HALO
    width = q_scr.shape[2]
    codes = tables_ref.shape[1]
    slab = rows // blocks
    padded_hop = env_ref.shape[1]
    parts = fft_size // HOP
    half_voc = voc_kernel.shape[0] // 2
    rim = half_voc + parts // 2
    taps = conv_kernel.shape[0]
    span_rows = win.shape[1]

    loads = []

    def load(source, target):
        copy = pltpu.make_async_copy(source, target, load_sems.at[len(loads)])
        copy.start()
        loads.append(copy)
        return copy

    tables_load = load(tables_hbm, tables_ref)
    joined = width % 128 == 0
    attn_loads = [
        load(attn_hbm.at[p], attn_ref.at[0, :, pl.ds(p * width, width)] if joined else attn_ref.at[p])
        for p in range(3)
    ]
    head_load = load(owns_hbm[5], head_raw)
    conv_loads = [load(conv_in_hbm, conv_in), load(conv_kernel_hbm, conv_kernel)]
    late_loads = [load(voc_kernel_hbm, voc_kernel), load(dft_hbm, dft)]

    tokh[...] = jnp.zeros_like(tokh)
    enter(at)
    first, last = at.seq == 0, at.seq == at.seqs - 1

    def tokens_up():
        return remote(small_ref.at[:, pl.ds(rows - 128, 128)], tokh.at[0],
                      tok_send.at[0], tok_recv.at[0], seq=at.seq + 1)

    def tokens_down():
        return remote(small_ref.at[:, pl.ds(0, 128)], tokh.at[1],
                      tok_send.at[1], tok_recv.at[1], seq=at.seq - 1)

    @pl.when(jnp.logical_not(last))
    def _():
        tokens_up().start()

    @pl.when(jnp.logical_not(first))
    def _():
        tokens_down().start()

    owns = owns_hbm[:5] + [head_own]
    weights = [Weight(at, owns[w], fulls[w], wsems[3 * w : 3 * w + 3]) for w in range(WEIGHTS)]

    ids = lax.broadcasted_iota(jnp.int32, (1, codes), 1).astype(jnp.float32)
    mask_row = small_ref[4:5, :columns]

    def embed(token_rows):
        result = token_rows[:, 3:4] * mask_row
        for level in range(3):
            hot = jnp.where(token_rows[:, level : level + 1] == ids, 1.0, 0.0).astype(jnp.bfloat16)
            result = result + jnp.dot(hot, tables_ref[level], preferred_element_type=jnp.float32)
        return result.astype(jnp.bfloat16)

    piece = rows // PIECES
    spans = [(p * piece, piece) for p in range(PIECES)] + [(rows, 2 * HALO)]
    spreads = [
        Spread(at, emb, span, (e_send.at[p], e_recv.at[p])) for p, span in enumerate(spans)
    ]
    token_columns = small_ref[:, :rows].T
    tables_load.wait()
    for p in range(PIECES):
        emb[at.me, pl.ds(*spans[p])] = embed(token_columns[p * piece : (p + 1) * piece])
        spreads[p].start()

    @pl.when(jnp.logical_not(last))
    def _():
        tokens_up().wait_send()

    @pl.when(jnp.logical_not(first))
    def _():
        tokens_up().wait_recv()
        tokens_down().wait_send()

    @pl.when(jnp.logical_not(last))
    def _():
        tokens_down().wait_recv()

    halo_tokens = jnp.concatenate(
        [tokh[0].T[128 - HALO :], tokh[1].T[:HALO]], axis=0
    )
    emb[at.me, pl.ds(rows, 2 * HALO)] = embed(halo_tokens)
    spreads[PIECES].start()
    for weight in weights[:4]:
        weight.start()

    lanes = lax.broadcasted_iota(jnp.int32, (1, width), 1)
    in_head = [
        (lanes >= h * head_size) & (lanes < (h + 1) * head_size) for h in range(local_heads)
    ]

    def unit(projected):
        squares = projected * projected
        scale = jnp.zeros_like(projected)
        for h in range(local_heads):
            total_h = jnp.sum(jnp.where(in_head[h], squares, 0.0), axis=-1, keepdims=True)
            scale = jnp.where(in_head[h], lax.rsqrt(total_h + 1e-06), scale)
        return projected * scale

    def send_up(block, step, part):
        view = kvbuf.at[block, part]
        return remote(view, view, r_send.at[step, part], r_recv.at[step, part], seq=at.seq + 1)

    def send_down(block, step, part):
        view = kvbuf.at[block, part]
        return remote(view, view, l_send.at[step, part], l_recv.at[step, part], seq=at.seq - 1)

    for copy in attn_loads:
        copy.wait()
    for p, spread in enumerate(spreads):
        spread.relay()
        spread.finish()
        begin, count = spread.rows
        whole = jnp.concatenate([emb[block, pl.ds(begin, count)] for block in range(blocks)], axis=1)
        normed = norm_rows(whole.astype(jnp.float32)).astype(jnp.bfloat16)
        projected = [
            jnp.dot(normed, attn_ref[part], preferred_element_type=jnp.float32)
            for part in range(attn_ref.shape[0])
        ]
        if joined:
            projected = [projected[0][:, part * width : (part + 1) * width] for part in range(3)]
        query = unit(projected[0])
        for h in range(local_heads):
            q_scr[h, pl.ds(begin, count)] = jnp.where(in_head[h], query, 0.0).astype(jnp.bfloat16)
        if p < PIECES:
            kvbuf[at.seq, p, 0] = unit(projected[1]).astype(jnp.bfloat16)
            kvbuf[at.seq, p, 1] = projected[2].astype(jnp.bfloat16)

            @pl.when(jnp.logical_not(last))
            def _():
                send_up(at.seq, 0, p).start()

            @pl.when(jnp.logical_not(first))
            def _():
                send_down(at.seq, 0, p).start()

    acc[...] = jnp.zeros_like(acc)
    l_acc[...] = jnp.zeros_like(l_acc)
    tile = total // 3
    keys = 2 * piece
    used = small_ref[7:8, 0:1]

    def attend(block, pair):
        frame = block * rows + pair * keys + lax.broadcasted_iota(jnp.int32, (1, keys), 1)
        live = frame.astype(jnp.float32) < used
        for h in range(local_heads):
            sharp = small_ref[7:8, 1 + h : 2 + h] * 1.4426950408889634
            bias = jnp.where(live, -sharp, -1e30)

            def one(index, carry):
                span = pl.ds(pl.multiple_of(index * tile, 64), tile)
                key = jnp.concatenate([kvbuf[block, 2 * pair, 0], kvbuf[block, 2 * pair + 1, 0]])
                value = jnp.concatenate([kvbuf[block, 2 * pair, 1], kvbuf[block, 2 * pair + 1, 1]])
                scores = lax.dot_general(
                    q_scr[h, span],
                    key,
                    (((1,), (1,)), ((), ())),
                    preferred_element_type=jnp.float32,
                )
                chance = jnp.exp2(scores * sharp + bias)
                part = chance[:, :128]
                for lane in range(128, keys, 128):
                    part = part + chance[:, lane : lane + 128]
                l_acc[h, span] += part
                acc[h, span] += jnp.dot(
                    chance.astype(jnp.bfloat16), value, preferred_element_type=jnp.float32
                )
                return carry

            lax.fori_loop(0, 3, one, 0)

    head_load.wait()
    head_wide[pl.ds(0, 2 * bin_count)] = head_raw[...].astype(jnp.float32)
    tail_rows = head_wide.shape[0] - 2 * bin_count
    head_wide[pl.ds(2 * bin_count, tail_rows)] = jnp.zeros((tail_rows, width), jnp.float32)
    head_own[pl.ds(0, padded_bins)] = head_wide[pl.ds(0, padded_bins)].astype(jnp.bfloat16)
    head_own[pl.ds(padded_bins, padded_bins)] = head_wide[pl.ds(bin_count, padded_bins)].astype(
        jnp.bfloat16
    )

    def relays(stage):
        if stage == 0:
            weights[1].relay_cross()
            weights[0].relay_over()
        if stage == 1:
            weights[2].relay_cross()
            weights[1].relay_over()

    attend(at.seq, 0)
    attend(at.seq, 1)
    weights[0].relay_cross()

    def exchange(step, carry):
        for part in range(PIECES):

            @pl.when(step < at.seq)
            def _():
                block = at.seq - 1 - step
                send_up(block, step, part).wait_recv()

                @pl.when(jnp.logical_not(last))
                def _():
                    send_up(block, step + 1, part).start()

            @pl.when(step < at.seqs - 1 - at.seq)
            def _():
                block = at.seq + 1 + step
                send_down(block, step, part).wait_recv()

                @pl.when(jnp.logical_not(first))
                def _():
                    send_down(block, step + 1, part).start()

            if part % 2 == 1:

                @pl.when(step < at.seq)
                def _():
                    attend(at.seq - 1 - step, part // 2)

                @pl.when(step < at.seqs - 1 - at.seq)
                def _():
                    attend(at.seq + 1 + step, part // 2)

        for stage in range(min(2, at.seqs - 1)):

            @pl.when(step == stage)
            def _():
                relays(stage)

        return carry

    lax.fori_loop(0, at.seqs - 1, exchange, 0)
    for stage in range(at.seqs - 1, 2):
        relays(stage)

    half = rows // 2
    tiles = ((0, half), (half, total - half))
    gathers = [
        Spread(at, att, span, (a_send.at[p], a_recv.at[p])) for p, span in enumerate(tiles)
    ]
    for (begin, count), gather in zip(tiles, gathers):
        value = jnp.zeros((count, width), jnp.float32)
        for h in range(local_heads):
            mean = acc[h, pl.ds(begin, count)] / jnp.sum(
                l_acc[h, pl.ds(begin, count)], axis=-1, keepdims=True
            )
            value = jnp.where(in_head[h], mean, value)
        att[at.me, pl.ds(begin, count)] = value.astype(jnp.bfloat16)
        gather.start()
    for weight in weights[4:]:
        weight.start()
    weights[3].relay_cross()
    weights[2].relay_over()

    def drain(step, carry):
        @pl.when(jnp.logical_not(last) & (step <= at.seq))
        def _():
            for part in range(PIECES):
                send_up(at.seq - step, step, part).wait_send()

        @pl.when(jnp.logical_not(first) & (step <= at.seqs - 1 - at.seq))
        def _():
            for part in range(PIECES):
                send_down(at.seq + step, step, part).wait_send()

        return carry

    lax.fori_loop(0, at.seqs - 1, drain, 0)
    for copy in conv_loads:
        copy.wait()
    weights[0].finish()
    channel_tiles = gated.shape[0]
    gated[:, pl.ds(total, gated.shape[1] - total)] = jnp.zeros(
        (channel_tiles, gated.shape[1] - total, 128), jnp.float32
    )
    zero_first = jnp.where(first, 0.0, 1.0)
    zero_last = jnp.where(last, 0.0, 1.0)
    for (begin, count), gather in zip(tiles, gathers):
        gather.relay()
        gather.finish()
        span = pl.ds(begin, count)
        base = jnp.concatenate([emb[block, span] for block in range(blocks)], axis=1)
        summed = base.astype(jnp.float32) + mix([att[block, span] for block in range(blocks)], fulls[0])
        if begin + count > rows:
            kept = rows - begin
            summed = jnp.concatenate(
                [
                    summed[:kept],
                    summed[kept : kept + HALO] * zero_first,
                    summed[kept + HALO :] * zero_last,
                ]
            )
        normed = norm_rows(summed).astype(jnp.bfloat16)
        value = jnp.dot(normed, conv_in[0], preferred_element_type=jnp.float32)
        signal = jnp.dot(normed, conv_in[1], preferred_element_type=jnp.float32)
        gate = (value * jax.nn.sigmoid(signal)).astype(jnp.bfloat16).astype(jnp.float32)
        for low, high, shift in (
            (0, rows, HALO), (rows, rows + HALO, -rows), (rows + HALO, total, 0)
        ):
            low, high = max(low, begin), min(high, begin + count)
            if low < high:
                target = pl.ds(low + shift, high - low)
                stream[target] = summed[low - begin : high - begin]
                for c in range(channel_tiles):
                    gated[c, target] = gate[
                        low - begin : high - begin, c * 128 : (c + 1) * 128
                    ]

    first_tap = HALO - rim - taps // 2
    lead = first_tap % 8
    chunk = span_rows // 2

    def convolve(member):
        base_row = pl.multiple_of(member * slab + first_tap - lead, 8)
        outs = []
        for part in range(2):
            line = []
            for c in range(channel_tiles):
                kernel = conv_kernel[:, c * 128 : (c + 1) * 128]
                reach = up_to(chunk + taps + lead, 8)
                source = gated[c, pl.ds(base_row + part * chunk, reach)]
                result = jnp.zeros((chunk, 128), jnp.float32)
                for turn in range(8):
                    shifted = source[turn:] if turn else source
                    for k in range(taps):
                        offset = lead + k - turn
                        if offset % 8 == 0 and offset >= 0:
                            result = result + kernel[k : k + 1] * shifted[offset : offset + chunk]
                line.append((result * jax.nn.sigmoid(result)).astype(jnp.bfloat16))
            outs.append(jnp.concatenate(line, axis=1))
        return jnp.concatenate(outs)

    def swap(slot, step, other, source):
        head, sub = at.head_at(step), lax.rem(at.sub + other, 2)
        if source is None:
            block = at.head_at(at.heads - step) * 2 + sub
            view = win.at[head * 2 + sub], act.at[block]
        else:
            view = win.at[head * 2 + sub], act.at[source]
        return remote(*view, s_send.at[slot], s_recv.at[slot], head=head, sub=sub)

    peers = [(step, other) for step in range(1, at.heads) for other in range(2)] + [(0, 1)]
    for slot, (step, other) in enumerate(peers):
        member = at.head_at(step) * 2 + lax.rem(at.sub + other, 2)
        win[member] = convolve(member)
        swap(slot, step, other, at.me).start()
    act[at.me] = convolve(at.me)

    weights[4].relay_cross()
    weights[3].relay_over()
    weights[5].relay_cross()
    weights[1].finish()
    for slot, (step, other) in enumerate(peers):
        swap(slot, step, other, at.me).wait_send()
        swap(slot, step, other, None).wait_recv()
    weights[4].relay_over()
    weights[5].relay_over()

    conv_sum = mix([act[block] for block in range(blocks)], fulls[1])
    window_at = HALO - rim
    slack = window_at % 8
    around = stream[pl.ds(pl.multiple_of(at.me * slab + window_at - slack, 8), span_rows + 8)]
    features = norm_rows(around[slack : slack + span_rows] + conv_sum)
    feat_out[...] = features[rim : rim + slab].astype(jnp.bfloat16)
    first_frame = at.seq * rows + at.me * slab - rim
    frames = (first_frame + lax.broadcasted_iota(jnp.int32, (span_rows, 1), 0)).astype(jnp.float32)
    weights[2].finish()
    base_rows = jnp.dot(
        features.astype(jnp.bfloat16),
        fulls[2][...].reshape(-1, fulls[2].shape[2]),
        preferred_element_type=jnp.float32,
    )
    base_rows = norm_rows(jnp.where((frames >= 0.0) & (frames < used), base_rows, 0.0))
    for copy in late_loads:
        copy.wait()
    voc_rows = up_to(slab + parts, 8)
    vdepth = jnp.zeros((voc_rows, base_rows.shape[1]), jnp.float32)
    for k in range(2 * half_voc + 1):
        vdepth = vdepth + voc_kernel[k : k + 1] * base_rows[k : k + voc_rows]
    inner = norm_rows(vdepth).astype(jnp.bfloat16)
    weights[3].finish()
    hidden = jnp.dot(
        inner, fulls[3][...].reshape(-1, fulls[3].shape[2]), preferred_element_type=jnp.float32
    )
    hidden = (0.5 * hidden * (1.0 + lax.erf(hidden * math.sqrt(0.5)))).astype(jnp.bfloat16)
    weights[4].finish()
    refined = base_rows[half_voc : half_voc + voc_rows] + jnp.dot(
        hidden, fulls[4][...].reshape(-1, fulls[4].shape[2]), preferred_element_type=jnp.float32
    )
    head_input = norm_rows(refined).astype(jnp.bfloat16)
    weights[5].finish()

    def spectrum(index):
        parts_of = [
            fulls[5][block, pl.ds(index * padded_bins, padded_bins)] for block in range(blocks)
        ]
        inputs = [head_input]
        if width % 128 == 0:
            parts_of = [jnp.concatenate(parts_of, axis=1)]
        else:
            inputs = [head_input[:, block * width : (block + 1) * width] for block in range(blocks)]
        result = 0.0
        for one_input, part in zip(inputs, parts_of):
            result = result + lax.dot_general(
                one_input, part, (((1,), (1,)), ((), ())), preferred_element_type=jnp.float32
            )
        return result + small_ref[5 + index : 6 + index, :padded_bins]

    magnitude = jnp.minimum(jnp.exp(spectrum(0)), 100.0)
    sine, cosine = sine_cosine(spectrum(1))
    wave_frames = first_frame + half_voc + lax.broadcasted_iota(jnp.int32, (voc_rows, 1), 0)
    exists = (wave_frames >= 0) & (wave_frames < at.seqs * rows)
    magnitude = jnp.where(exists, magnitude, 0.0)
    waves = jnp.dot(
        (magnitude * cosine).astype(jnp.bfloat16),
        dft[pl.ds(0, padded_bins)],
        preferred_element_type=jnp.float32,
    ) + jnp.dot(
        (magnitude * sine).astype(jnp.bfloat16),
        dft[pl.ds(padded_bins, padded_bins)],
        preferred_element_type=jnp.float32,
    )
    there = jnp.where(exists, 1.0, 0.0)
    total_audio = jnp.zeros((slab, padded_hop), jnp.float32)
    energy = jnp.zeros((slab, padded_hop), jnp.float32)
    for quarter in range(parts):
        begin = parts - quarter
        total_audio = total_audio + waves[
            begin : begin + slab, quarter * padded_hop : (quarter + 1) * padded_hop
        ]
        energy = energy + there[begin : begin + slab] * env_ref[quarter : quarter + 1]
    total_audio = total_audio / energy
    for c in range(padded_hop // 128):
        audio[c] = total_audio[:, c * 128 : (c + 1) * 128]
    pairs = slab // 2
    group = 2 * HOP // 128
    low_lanes = lax.broadcasted_iota(jnp.int32, (1, 128), 1) < HOP % 128
    even = [audio[c, pl.ds(0, pairs, stride=2)] for c in range(padded_hop // 128)]
    odd = [
        pltpu.roll(audio[c, pl.ds(1, pairs, stride=2)], HOP % 128, 1)
        for c in range(padded_hop // 128)
    ]
    full_tiles = HOP // 128
    lines = even[:full_tiles] + [jnp.where(low_lanes, even[full_tiles], odd[0])]
    for c in range(full_tiles):
        lines.append(jnp.where(low_lanes, odd[c], odd[c + 1]))
    for index in range(group):
        wave_out[pl.ds(index, pairs, stride=group)] = lines[index]


def local(
    tokens,
    masked,
    used_frames,
    tables,
    mask_vec,
    attn_in,
    head_temp,
    attn_out,
    conv_in,
    conv_kernel,
    conv_out,
    voc_in,
    voc_kernel,
    voc_up,
    voc_down,
    voc_head,
    head_bias,
):
    groups, heads, seqs = (lax.axis_size(name) for name in ("groups", "head", "seq"))
    blocks = lax.axis_size(("head", "sub"))
    rows = tokens.shape[1]
    total = rows + 2 * HALO
    slab = rows // blocks
    columns = tables.shape[2]
    width = attn_in.shape[2]
    local_heads = head_temp.shape[0]
    bin_count = head_bias.shape[0] // 2
    fft_size = 2 * (bin_count - 1)
    parts = fft_size // HOP
    padded_bins = up_to(bin_count, 16)
    padded_hop = up_to(HOP, 128)
    rim = voc_kernel.shape[0] // 2 + parts // 2
    window_rows = up_to(slab + 2 * rim, 16)
    channels = conv_kernel.shape[1]
    dft, env = synthesis_constants(bin_count, fft_size, padded_bins, padded_hop)
    across = up_to(max(rows, padded_bins, columns), 128)

    def line(values):
        values = values.astype(jnp.float32)
        return jnp.pad(values, (0, across - values.shape[0]))

    small = jnp.stack(
        [
            line(tokens[0]),
            line(tokens[1]),
            line(jnp.where(masked == 1, -1, tokens[2])),
            line(masked == 1),
            line(mask_vec),
            line(head_bias[:bin_count]),
            line(head_bias[bin_count:]),
            line(jnp.concatenate([used_frames.astype(jnp.float32), head_temp])),
        ]
    )
    head_rows = voc_head.T
    owns = (attn_out, conv_out, voc_in, voc_up, voc_down, head_rows)
    vmem = pl.BlockSpec(memory_space=pltpu.VMEM)
    anywhere = pl.BlockSpec(memory_space=pl.ANY)
    dma = pltpu.SemaphoreType.DMA
    bf16, f32 = jnp.bfloat16, jnp.float32
    full_shapes = [(blocks,) + own.shape for own in owns[:5]] + [(blocks, 2 * padded_bins, width)]
    scratch = [pltpu.VMEM(shape, bf16) for shape in full_shapes]
    scratch += [
        pltpu.VMEM(tables.shape, bf16),
        pltpu.VMEM((1, attn_in.shape[1], 3 * width) if width % 128 == 0 else attn_in.shape, bf16),
        pltpu.VMEM(conv_in.shape, bf16),
        pltpu.VMEM(conv_kernel.shape, f32),
        pltpu.VMEM(voc_kernel.shape, f32),
        pltpu.VMEM(dft.shape, bf16),
        pltpu.VMEM(head_rows.shape, bf16),
        pltpu.VMEM((up_to(bin_count + padded_bins, 8), width), f32),
        pltpu.VMEM((2 * padded_bins, width), bf16),
        pltpu.VMEM((2, 8, 128), f32),
        pltpu.VMEM((blocks, total, columns), bf16),
        pltpu.VMEM((blocks, total, width), bf16),
        pltpu.VMEM((seqs, PIECES, 2, rows // PIECES, width), bf16),
        pltpu.VMEM((local_heads, total, width), bf16),
        pltpu.VMEM((local_heads, total, width), f32),
        pltpu.VMEM((local_heads, total, 128), f32),
        pltpu.VMEM((total, columns * blocks), f32),
        pltpu.VMEM((channels // 128, total + 64, 128), f32),
        pltpu.VMEM((blocks, window_rows, channels), bf16),
        pltpu.VMEM((blocks, window_rows, channels), bf16),
        pltpu.VMEM((padded_hop // 128, slab, 128), f32),
        dma((9,)),
        dma((2,)),
        dma((2,)),
        dma((PIECES + 1, 2 * heads)),
        dma((PIECES + 1, 2 * heads)),
        dma((2, 2 * heads)),
        dma((2, 2 * heads)),
        dma((seqs, PIECES)),
        dma((seqs, PIECES)),
        dma((seqs, PIECES)),
        dma((seqs, PIECES)),
        dma((blocks,)),
        dma((blocks,)),
    ]
    for _ in owns:
        scratch += weight_sems(heads, groups)
    sizes = (local_heads, width // local_heads, bin_count, padded_bins, fft_size)
    features, wave = pl.pallas_call(
        functools.partial(block_kernel, sizes),
        out_shape=[
            jax.ShapeDtypeStruct((slab, columns * blocks), bf16),
            jax.ShapeDtypeStruct((slab * HOP // 128, 128), f32),
        ],
        in_specs=[vmem] * 2 + [anywhere] * (6 + WEIGHTS),
        out_specs=[vmem, vmem],
        scratch_shapes=scratch,
        compiler_params=pltpu.CompilerParams(
            collective_id=0, has_side_effects=True, vmem_limit_bytes=60 * 1024 * 1024
        ),
    )(small, env, tables, attn_in, conv_in, conv_kernel, voc_kernel, dft, *owns)
    return features, wave.reshape(slab * HOP)


def solution(mesh):
    in_specs = (
        P(None, ("groups", "seq")),
        P(("groups", "seq")),
        P("groups"),
        P(None, None, ("head", "sub")),
        P(("head", "sub")),
        P(None, None, ("head", "sub")),
        P(("head", "sub")),
        P(("head", "sub"), None),
        P(None, None, ("head", "sub")),
        P(None, ("head", "sub")),
        P(("head", "sub"), None),
        P(("head", "sub"), None),
        P(),
        P(("head", "sub"), None),
        P(("head", "sub"), None),
        P(("head", "sub"), None),
        P(),
    )
    out_specs = (P(("groups", "seq", "head", "sub"), None), P(("groups", "seq", "head", "sub")))
    return jax.shard_map(local, mesh=mesh, in_specs=in_specs, out_specs=out_specs, check_vma=False)
```

```python
import functools
import math

import jax
import jax.numpy as jnp
import numpy as np
from jax import lax
from jax.experimental import pallas as pl
from jax.experimental.pallas import tpu as pltpu
from jax.sharding import PartitionSpec as P

HOP = 320


MESH = pl.DeviceIdType.MESH
HALO = 32


def remote(src, dst, send_sem, recv_sem, **where):
    return pltpu.make_async_remote_copy(
        src_ref=src,
        dst_ref=dst,
        send_sem=send_sem,
        recv_sem=recv_sem,
        device_id=where,
        device_id_type=MESH,
    )


class Place:
    def __init__(self):
        self.group, self.seq = lax.axis_index("groups"), lax.axis_index("seq")
        self.head, self.sub = lax.axis_index("head"), lax.axis_index("sub")
        self.groups, self.seqs = lax.axis_size("groups"), lax.axis_size("seq")
        self.heads = lax.axis_size("head")
        self.me = self.head * 2 + self.sub
        self.partner = 1 - self.sub

    def head_at(self, step):
        return lax.rem(self.head + step, self.heads)

    def group_at(self, step):
        return lax.rem(self.group + step, self.groups)


def enter(at):
    barrier = pltpu.get_barrier_semaphore()

    def greet(**where):
        pl.semaphore_signal(barrier, inc=1, device_id=where, device_id_type=MESH)

    for step in range(1, at.heads):
        greet(head=at.head_at(step))
        greet(head=at.head_at(step), sub=at.partner)
    for step in range(1, at.groups):
        greet(groups=at.group_at(step))
    greet(sub=at.partner)

    @pl.when(at.seq > 0)
    def _():
        greet(seq=at.seq - 1)

    @pl.when(at.seq < at.seqs - 1)
    def _():
        greet(seq=at.seq + 1)

    count = 2 * (at.heads - 1) + at.groups
    count = count + jnp.where(at.seq > 0, 1, 0) + jnp.where(at.seq < at.seqs - 1, 1, 0)
    return lambda: pl.semaphore_wait(barrier, count)


class Spread:
    def __init__(self, at, buffer, rows, sems):
        self.at, self.buffer, self.rows = at, buffer, rows
        self.send, self.recv = sems

    def part(self, block):
        return self.buffer.at[block, pl.ds(*self.rows)]

    def cross(self, step):
        block = self.part(self.at.me)
        return remote(
            block, block, self.send.at[step], self.recv.at[step], head=self.at.head_at(step)
        )

    def aside(self, step):
        block = self.part(self.at.head_at(self.at.heads - step) * 2 + self.at.sub)
        slot = self.at.heads + step
        return remote(block, block, self.send.at[slot], self.recv.at[slot], sub=self.at.partner)

    def start(self):
        for step in range(1, self.at.heads):
            self.cross(step).start()
        self.aside(0).start()

    def relay(self):
        for step in range(1, self.at.heads):
            self.cross(step).wait_recv()
            self.aside(step).start()

    def finish(self):
        for step in range(self.at.heads):
            if step > 0:
                self.cross(step).wait_send()
            self.aside(step).wait()


class Weight:
    def __init__(self, at, own, full, sems):
        self.at, self.own, self.full = at, own, full
        self.send, self.recv, self.local = sems
        self.length = own.shape[0] // at.groups

    def piece(self, block, part):
        start = pl.multiple_of(part * self.length, 16)
        return self.full.at[block, pl.ds(start, self.length)]

    def source(self, step):
        return self.at.head_at(self.at.heads - step) * 2 + self.at.sub

    def cross(self, step):
        start = pl.multiple_of(self.at.group * self.length, 16)
        return remote(
            self.own.at[pl.ds(start, self.length)],
            self.piece(self.at.me, self.at.group),
            self.send.at[step],
            self.recv.at[step],
            head=self.at.head_at(step),
        )

    def over(self, step, turn):
        block = self.piece(self.source(step), self.at.group)
        slot = self.at.heads + (step - 1) * self.at.groups + turn
        return remote(
            block, block, self.send.at[slot], self.recv.at[slot], groups=self.at.group_at(turn)
        )

    def aside(self, step, turn):
        part = self.at.group_at(self.at.groups - turn)
        block = self.piece(self.source(step), part)
        slot = self.at.heads * (1 + self.at.groups) + (step - 1) * self.at.groups + turn
        return remote(block, block, self.send.at[slot], self.recv.at[slot], sub=self.at.partner)

    def mine(self):
        return remote(
            self.own, self.full.at[self.at.me], self.send.at[0], self.recv.at[0], sub=self.at.partner
        )

    def kept(self):
        return pltpu.make_async_copy(self.own, self.full.at[self.at.me], self.local.at[0])

    def start(self):
        for step in range(1, self.at.heads):
            self.cross(step).start()
        self.mine().start()
        self.kept().start()

    def relay_cross(self):
        for step in range(1, self.at.heads):
            self.cross(step).wait_recv()
            for turn in range(1, self.at.groups):
                self.over(step, turn).start()
            self.aside(step, 0).start()

    def relay_over(self):
        for step in range(1, self.at.heads):
            for turn in range(1, self.at.groups):
                self.over(step, turn).wait_recv()
                self.aside(step, turn).start()

    def finish(self):
        self.mine().wait()
        self.kept().wait()
        for step in range(1, self.at.heads):
            self.cross(step).wait_send()
            for turn in range(1, self.at.groups):
                self.over(step, turn).wait_send()
            for turn in range(self.at.groups):
                self.aside(step, turn).wait()


def weight_sems(heads, groups):
    count = heads * (1 + 2 * groups)
    return [
        pltpu.SemaphoreType.DMA((count,)),
        pltpu.SemaphoreType.DMA((count,)),
        pltpu.SemaphoreType.DMA((1,)),
    ]


def norm_rows(values):
    average = jnp.mean(values, axis=-1, keepdims=True)
    centered = values - average
    return centered * lax.rsqrt(jnp.mean(centered * centered, axis=-1, keepdims=True) + 1e-05)


PIECES = 4
WEIGHTS = 6


def up_to(value, unit):
    return -(-value // unit) * unit


def synthesis_constants(bin_count, fft_size, padded_bins, padded_hop):
    parts = fft_size // HOP
    samples = np.arange(fft_size)
    window = 0.5 - 0.5 * np.cos(2.0 * np.pi / fft_size * samples)
    bins = np.arange(bin_count)[:, None]
    angle = 2.0 * np.pi / fft_size * (bins * samples[None, :] % fft_size)
    edge = (bins == 0) | (bins == bin_count - 1)
    factor = np.where(edge, 1.0, 2.0) / fft_size
    cosine = factor * np.cos(angle) * window
    sine = np.where(edge, 0.0, -factor * np.sin(angle) * window)

    def spread(table, rows, fill):
        result = np.full((rows, parts, padded_hop), fill)
        result[: table.shape[0], :, :HOP] = table.reshape(-1, parts, HOP)
        return result.reshape(rows, parts * padded_hop)

    tables = np.concatenate([spread(cosine, padded_bins, 0.0), spread(sine, padded_bins, 0.0)])
    energy = spread((window * window)[None, :], 1, 1.0).reshape(parts, padded_hop)
    energy = np.pad(energy, ((0, -parts % 8), (0, 0)), constant_values=1.0)
    return jnp.asarray(tables, jnp.bfloat16), jnp.asarray(energy, jnp.float32)


def sine_cosine(angle):
    turns = jnp.round(angle * (2.0 / math.pi))
    rest = angle - turns * 1.5703125
    rest = rest - turns * 4.837512969970703125e-4
    rest = rest - turns * 7.549789948768648e-8
    square = rest * rest
    sine = rest + rest * square * (
        -1.6666654611e-1 + square * (8.3321608736e-3 + square * -1.9515295891e-4)
    )
    cosine = 1.0 - 0.5 * square + square * square * (
        4.166664568298827e-2 + square * (-1.388731625493765e-3 + square * 2.443315711809948e-5)
    )
    quadrant = turns.astype(jnp.int32) & 3
    odd = (quadrant & 1) == 1
    sine, cosine = jnp.where(odd, cosine, sine), jnp.where(odd, sine, cosine)
    sine = jnp.where(quadrant >= 2, -sine, sine)
    cosine = jnp.where((quadrant == 1) | (quadrant == 2), -cosine, cosine)
    return sine, cosine


def mix(parts, full):
    if parts[0].shape[1] % 128 == 0:
        return jnp.dot(
            jnp.concatenate(parts, axis=1),
            full[...].reshape(-1, full.shape[2]),
            preferred_element_type=jnp.float32,
        )
    result = 0.0
    for block, part in enumerate(parts):
        result = result + jnp.dot(part, full[block], preferred_element_type=jnp.float32)
    return result


def block_kernel(sizes, *refs):
    (used_ref, temp_ref, tokens_ref, masked_ref, mask_ref, bias_ref, env_ref, tables_hbm, attn_hbm,
     conv_in_hbm, conv_kernel_hbm, voc_kernel_hbm, dft_hbm) = refs[:13]
    owns_hbm = list(refs[13 : 13 + WEIGHTS])
    feat_out, wave_out = refs[13 + WEIGHTS : 15 + WEIGHTS]
    refs = refs[15 + WEIGHTS :]
    fulls = refs[:WEIGHTS]
    (tables_ref, attn_ref, conv_in, conv_kernel, voc_kernel, dft, head_raw, head_wide, head_own,
     tok, tokh, emb, att, kvbuf, q_scr, acc, l_acc, stream, gated, win, act, audio) = refs[
        WEIGHTS : WEIGHTS + 22
    ]
    (load_sems, tok_send, tok_recv, e_send, e_recv, a_send, a_recv, r_send, r_recv, l_send,
     l_recv, s_send, s_recv) = refs[WEIGHTS + 22 : WEIGHTS + 35]
    wsems = refs[WEIGHTS + 35 :]
    local_heads, head_size, bin_count, padded_bins, fft_size = sizes
    at = Place()
    blocks, total, columns = emb.shape
    rows = total - 2 * HALO
    width = q_scr.shape[2]
    codes = tables_ref.shape[1]
    slab = rows // blocks
    padded_hop = env_ref.shape[1]
    parts = fft_size // HOP
    half_voc = voc_kernel.shape[0] // 2
    rim = half_voc + parts // 2
    taps = conv_kernel.shape[0]
    span_rows = win.shape[1]

    tokh[...] = jnp.zeros_like(tokh)
    wait_for_peers = enter(at)
    loads = []

    def load(source, target):
        copy = pltpu.make_async_copy(source, target, load_sems.at[len(loads)])
        copy.start()
        loads.append(copy)
        return copy

    tables_load = load(tables_hbm, tables_ref)
    joined = width % 128 == 0
    attn_loads = [
        load(attn_hbm.at[p], attn_ref.at[0, :, pl.ds(p * width, width)] if joined else attn_ref.at[p])
        for p in range(3)
    ]
    head_load = load(owns_hbm[5], head_raw)
    conv_loads = [load(conv_in_hbm, conv_in), load(conv_kernel_hbm, conv_kernel)]
    late_loads = [load(voc_kernel_hbm, voc_kernel), load(dft_hbm, dft)]

    first, last = at.seq == 0, at.seq == at.seqs - 1

    def tokens_up():
        return remote(tok.at[:, pl.ds(rows - 128, 128)], tokh.at[0],
                      tok_send.at[0], tok_recv.at[0], seq=at.seq + 1)

    def tokens_down():
        return remote(tok.at[:, pl.ds(0, 128)], tokh.at[1],
                      tok_send.at[1], tok_recv.at[1], seq=at.seq - 1)

    owns = owns_hbm[:5] + [head_own]
    weights = [Weight(at, owns[w], fulls[w], wsems[3 * w : 3 * w + 3]) for w in range(WEIGHTS)]

    ids = lax.broadcasted_iota(jnp.int32, (1, codes), 1).astype(jnp.float32)
    mask_row = mask_ref[...].astype(jnp.float32).reshape(1, columns)

    def embed(token_rows):
        result = token_rows[:, 3:4] * mask_row
        for level in range(3):
            hot = jnp.where(token_rows[:, level : level + 1] == ids, 1.0, 0.0).astype(jnp.bfloat16)
            result = result + jnp.dot(hot, tables_ref[level], preferred_element_type=jnp.float32)
        return result.astype(jnp.bfloat16)

    piece = rows // PIECES
    spans = [(p * piece, piece) for p in range(PIECES)] + [(rows, 2 * HALO)]
    spreads = [
        Spread(at, emb, span, (e_send.at[p], e_recv.at[p])) for p, span in enumerate(spans)
    ]
    is_masked = masked_ref[...].reshape(1, rows)
    tok[0:2] = tokens_ref[0:2].astype(jnp.float32)
    tok[2:3] = jnp.where(is_masked == 1, -1, tokens_ref[2:3]).astype(jnp.float32)
    tok[3:4] = is_masked.astype(jnp.float32)
    tok[4:8] = jnp.zeros((4, rows), jnp.float32)
    token_columns = tok[...].T
    tables_load.wait()
    for p in range(PIECES):
        emb[at.me, pl.ds(*spans[p])] = embed(token_columns[p * piece : (p + 1) * piece])
        if p == 0:
            wait_for_peers()
        spreads[p].start()
        if p == 0:

            @pl.when(jnp.logical_not(last))
            def _():
                tokens_up().start()

            @pl.when(jnp.logical_not(first))
            def _():
                tokens_down().start()

    @pl.when(jnp.logical_not(last))
    def _():
        tokens_up().wait_send()

    @pl.when(jnp.logical_not(first))
    def _():
        tokens_up().wait_recv()
        tokens_down().wait_send()

    @pl.when(jnp.logical_not(last))
    def _():
        tokens_down().wait_recv()

    halo_tokens = jnp.concatenate(
        [tokh[0].T[128 - HALO :], tokh[1].T[:HALO]], axis=0
    )
    emb[at.me, pl.ds(rows, 2 * HALO)] = embed(halo_tokens)
    spreads[PIECES].start()
    lanes = lax.broadcasted_iota(jnp.int32, (1, width), 1)
    in_head = [
        (lanes >= h * head_size) & (lanes < (h + 1) * head_size) for h in range(local_heads)
    ]

    def unit(projected):
        squares = projected * projected
        scale = jnp.zeros_like(projected)
        for h in range(local_heads):
            total_h = jnp.sum(jnp.where(in_head[h], squares, 0.0), axis=-1, keepdims=True)
            scale = jnp.where(in_head[h], lax.rsqrt(total_h + 1e-06), scale)
        return projected * scale

    def send_up(block, step, part):
        view = kvbuf.at[block, part]
        return remote(view, view, r_send.at[step, part], r_recv.at[step, part], seq=at.seq + 1)

    def send_down(block, step, part):
        view = kvbuf.at[block, part]
        return remote(view, view, l_send.at[step, part], l_recv.at[step, part], seq=at.seq - 1)

    for copy in attn_loads:
        copy.wait()
    for p, spread in enumerate(spreads):
        spread.relay()
        spread.finish()
        begin, count = spread.rows
        whole = jnp.concatenate([emb[block, pl.ds(begin, count)] for block in range(blocks)], axis=1)
        normed = norm_rows(whole.astype(jnp.float32)).astype(jnp.bfloat16)
        projected = [
            jnp.dot(normed, attn_ref[part], preferred_element_type=jnp.float32)
            for part in range(attn_ref.shape[0])
        ]
        if joined:
            projected = [projected[0][:, part * width : (part + 1) * width] for part in range(3)]
        query = unit(projected[0])
        for h in range(local_heads):
            q_scr[h, pl.ds(begin, count)] = jnp.where(in_head[h], query, 0.0).astype(jnp.bfloat16)
        if p < PIECES:
            kvbuf[at.seq, p, 0] = unit(projected[1]).astype(jnp.bfloat16)
            kvbuf[at.seq, p, 1] = projected[2].astype(jnp.bfloat16)

            @pl.when(jnp.logical_not(last))
            def _():
                send_up(at.seq, 0, p).start()

            @pl.when(jnp.logical_not(first))
            def _():
                send_down(at.seq, 0, p).start()

    for weight in weights[:4]:
        weight.start()
    acc[...] = jnp.zeros_like(acc)
    l_acc[...] = jnp.zeros_like(l_acc)
    tile = total // 3
    keys = 2 * piece

    def attend(block, pair):
        frame = block * rows + pair * keys + lax.broadcasted_iota(jnp.int32, (1, keys), 1)
        live = frame < used_ref[0]
        sharps = [temp_ref[h] * 1.4426950408889634 for h in range(local_heads)]
        biases = [jnp.where(live, -sharp, -1e30) for sharp in sharps]
        key = jnp.concatenate([kvbuf[block, 2 * pair, 0], kvbuf[block, 2 * pair + 1, 0]])
        value = jnp.concatenate([kvbuf[block, 2 * pair, 1], kvbuf[block, 2 * pair + 1, 1]])
        for index in range(3):
            span = pl.ds(index * tile, tile)
            scores = lax.dot_general(
                jnp.concatenate([q_scr[h, span] for h in range(local_heads)]),
                key,
                (((1,), (1,)), ((), ())),
                preferred_element_type=jnp.float32,
            )
            chances = []
            for h in range(local_heads):
                chance = jnp.exp2(scores[h * tile : (h + 1) * tile] * sharps[h] + biases[h])
                part = chance[:, :128]
                for lane in range(128, keys, 128):
                    part = part + chance[:, lane : lane + 128]
                l_acc[h, span] += part
                chances.append(chance.astype(jnp.bfloat16))
            summed = jnp.dot(
                jnp.concatenate(chances), value, preferred_element_type=jnp.float32
            )
            for h in range(local_heads):
                acc[h, span] += summed[h * tile : (h + 1) * tile]

    head_load.wait()
    head_wide[pl.ds(0, 2 * bin_count)] = head_raw[...].astype(jnp.float32)
    tail_rows = head_wide.shape[0] - 2 * bin_count
    head_wide[pl.ds(2 * bin_count, tail_rows)] = jnp.zeros((tail_rows, width), jnp.float32)
    head_own[pl.ds(0, padded_bins)] = head_wide[pl.ds(0, padded_bins)].astype(jnp.bfloat16)
    head_own[pl.ds(padded_bins, padded_bins)] = head_wide[pl.ds(bin_count, padded_bins)].astype(
        jnp.bfloat16
    )

    def relays(stage):
        weights[stage].relay_cross()
        if stage:
            weights[stage - 1].relay_over()

    pairs_of = PIECES // 2

    def exchange(index, carry):
        step, pair = index // pairs_of, lax.rem(index, pairs_of)
        before = jnp.maximum(index - 1, 0)
        old_step, old_pair = before // pairs_of, lax.rem(before, pairs_of)
        arriving = index < pairs_of * (at.seqs - 1)

        @pl.when(index < pairs_of)
        def _():
            attend(at.seq, index)

        for turn in range(2):
            part = 2 * pair + turn

            @pl.when(arriving & (step < at.seq))
            def _():
                block = at.seq - 1 - step
                send_up(block, step, part).wait_recv()

                @pl.when(jnp.logical_not(last))
                def _():
                    send_up(block, step + 1, part).start()

            @pl.when(arriving & (step < at.seqs - 1 - at.seq))
            def _():
                block = at.seq + 1 + step
                send_down(block, step, part).wait_recv()

                @pl.when(jnp.logical_not(first))
                def _():
                    send_down(block, step + 1, part).start()

            if turn == 0:

                @pl.when((index > 0) & (old_step < at.seq))
                def _():
                    attend(at.seq - 1 - old_step, old_pair)

            else:

                @pl.when((index > 0) & (old_step < at.seqs - 1 - at.seq))
                def _():
                    attend(at.seq + 1 + old_step, old_pair)

        for stage in range(3):

            @pl.when(index == 2 * stage)
            def _():
                relays(stage)

        return carry

    lax.fori_loop(0, pairs_of * (at.seqs - 1) + 1, exchange, 0)
    for stage in range((pairs_of * (at.seqs - 1) + 2) // 2, 3):
        relays(stage)

    half = rows // 2
    tiles = ((0, half), (half, total - half))
    gathers = [
        Spread(at, att, span, (a_send.at[p], a_recv.at[p])) for p, span in enumerate(tiles)
    ]
    for (begin, count), gather in zip(tiles, gathers):
        value = jnp.zeros((count, width), jnp.float32)
        for h in range(local_heads):
            mean = acc[h, pl.ds(begin, count)] / jnp.sum(
                l_acc[h, pl.ds(begin, count)], axis=-1, keepdims=True
            )
            value = jnp.where(in_head[h], mean, value)
        att[at.me, pl.ds(begin, count)] = value.astype(jnp.bfloat16)
        gather.start()
    for weight in weights[4:]:
        weight.start()
    weights[3].relay_cross()
    weights[2].relay_over()

    def drain(step, carry):
        @pl.when(jnp.logical_not(last) & (step <= at.seq))
        def _():
            for part in range(PIECES):
                send_up(at.seq - step, step, part).wait_send()

        @pl.when(jnp.logical_not(first) & (step <= at.seqs - 1 - at.seq))
        def _():
            for part in range(PIECES):
                send_down(at.seq + step, step, part).wait_send()

        return carry

    lax.fori_loop(0, at.seqs - 1, drain, 0)
    for copy in conv_loads:
        copy.wait()
    weights[0].finish()
    channel_tiles = gated.shape[0]
    gated[:, pl.ds(total, gated.shape[1] - total)] = jnp.zeros(
        (channel_tiles, gated.shape[1] - total, 128), jnp.float32
    )
    zero_first = jnp.where(first, 0.0, 1.0)
    zero_last = jnp.where(last, 0.0, 1.0)
    for (begin, count), gather in zip(tiles, gathers):
        gather.relay()
        gather.finish()
        span = pl.ds(begin, count)
        base = jnp.concatenate([emb[block, span] for block in range(blocks)], axis=1)
        summed = base.astype(jnp.float32) + mix([att[block, span] for block in range(blocks)], fulls[0])
        if begin + count > rows:
            kept = rows - begin
            summed = jnp.concatenate(
                [
                    summed[:kept],
                    summed[kept : kept + HALO] * zero_first,
                    summed[kept + HALO :] * zero_last,
                ]
            )
        normed = norm_rows(summed).astype(jnp.bfloat16)
        value = jnp.dot(normed, conv_in[0], preferred_element_type=jnp.float32)
        signal = jnp.dot(normed, conv_in[1], preferred_element_type=jnp.float32)
        gate = (value * jax.nn.sigmoid(signal)).astype(jnp.bfloat16).astype(jnp.float32)
        for low, high, shift in (
            (0, rows, HALO), (rows, rows + HALO, -rows), (rows + HALO, total, 0)
        ):
            low, high = max(low, begin), min(high, begin + count)
            if low < high:
                target = pl.ds(low + shift, high - low)
                stream[target] = summed[low - begin : high - begin]
                for c in range(channel_tiles):
                    gated[c, target] = gate[
                        low - begin : high - begin, c * 128 : (c + 1) * 128
                    ]

    first_tap = HALO - rim - taps // 2
    lead = first_tap % 8
    chunk = span_rows // 2

    def convolve(member):
        base_row = pl.multiple_of(member * slab + first_tap - lead, 8)
        outs = []
        for part in range(2):
            line = []
            for c in range(channel_tiles):
                kernel = conv_kernel[:, c * 128 : (c + 1) * 128]
                reach = up_to(chunk + taps + lead, 8)
                source = gated[c, pl.ds(base_row + part * chunk, reach)]
                result = jnp.zeros((chunk, 128), jnp.float32)
                for turn in range(8):
                    shifted = source[turn:] if turn else source
                    for k in range(taps):
                        offset = lead + k - turn
                        if offset % 8 == 0 and offset >= 0:
                            result = result + kernel[k : k + 1] * shifted[offset : offset + chunk]
                line.append((result * jax.nn.sigmoid(result)).astype(jnp.bfloat16))
            outs.append(jnp.concatenate(line, axis=1))
        return jnp.concatenate(outs)

    def swap(slot, step, other, source):
        head, sub = at.head_at(step), lax.rem(at.sub + other, 2)
        if source is None:
            block = at.head_at(at.heads - step) * 2 + sub
            view = win.at[head * 2 + sub], act.at[block]
        else:
            view = win.at[head * 2 + sub], act.at[source]
        return remote(*view, s_send.at[slot], s_recv.at[slot], head=head, sub=sub)

    peers = [(step, other) for step in range(1, at.heads) for other in range(2)] + [(0, 1)]
    for slot, (step, other) in enumerate(peers):
        member = at.head_at(step) * 2 + lax.rem(at.sub + other, 2)
        win[member] = convolve(member)
        swap(slot, step, other, at.me).start()
    act[at.me] = convolve(at.me)

    weights[4].relay_cross()
    weights[3].relay_over()
    weights[5].relay_cross()
    weights[1].finish()
    for slot, (step, other) in enumerate(peers):
        swap(slot, step, other, at.me).wait_send()
        swap(slot, step, other, None).wait_recv()
    weights[4].relay_over()
    weights[5].relay_over()

    conv_sum = mix([act[block] for block in range(blocks)], fulls[1])
    window_at = HALO - rim
    slack = window_at % 8
    around = stream[pl.ds(pl.multiple_of(at.me * slab + window_at - slack, 8), span_rows + 8)]
    features = norm_rows(around[slack : slack + span_rows] + conv_sum)
    feat_out[...] = features[rim : rim + slab].astype(jnp.bfloat16)
    first_frame = at.seq * rows + at.me * slab - rim
    frames = first_frame + lax.broadcasted_iota(jnp.int32, (span_rows, 1), 0)
    weights[2].finish()
    base_rows = jnp.dot(
        features.astype(jnp.bfloat16),
        fulls[2][...].reshape(-1, fulls[2].shape[2]),
        preferred_element_type=jnp.float32,
    )
    base_rows = norm_rows(jnp.where((frames >= 0) & (frames < used_ref[0]), base_rows, 0.0))
    for copy in late_loads:
        copy.wait()
    voc_rows = up_to(slab + parts, 8)
    vdepth = jnp.zeros((voc_rows, base_rows.shape[1]), jnp.float32)
    for k in range(2 * half_voc + 1):
        vdepth = vdepth + voc_kernel[k : k + 1] * base_rows[k : k + voc_rows]
    inner = norm_rows(vdepth).astype(jnp.bfloat16)
    weights[3].finish()
    hidden = jnp.dot(
        inner, fulls[3][...].reshape(-1, fulls[3].shape[2]), preferred_element_type=jnp.float32
    )
    hidden = (0.5 * hidden * (1.0 + lax.erf(hidden * math.sqrt(0.5)))).astype(jnp.bfloat16)
    weights[4].finish()
    refined = base_rows[half_voc : half_voc + voc_rows] + jnp.dot(
        hidden, fulls[4][...].reshape(-1, fulls[4].shape[2]), preferred_element_type=jnp.float32
    )
    head_input = norm_rows(refined).astype(jnp.bfloat16)
    weights[5].finish()

    bias_row = bias_ref[...].reshape(1, 2 * bin_count)
    biases = [
        bias_row[:, :padded_bins],
        jnp.concatenate(
            [bias_row[:, bin_count:], jnp.zeros((1, padded_bins - bin_count), jnp.float32)], axis=1
        ),
    ]

    def spectrum(index):
        parts_of = [
            fulls[5][block, pl.ds(index * padded_bins, padded_bins)] for block in range(blocks)
        ]
        inputs = [head_input]
        if width % 128 == 0:
            parts_of = [jnp.concatenate(parts_of, axis=1)]
        else:
            inputs = [head_input[:, block * width : (block + 1) * width] for block in range(blocks)]
        result = 0.0
        for one_input, part in zip(inputs, parts_of):
            result = result + lax.dot_general(
                one_input, part, (((1,), (1,)), ((), ())), preferred_element_type=jnp.float32
            )
        return result + biases[index]

    magnitude = jnp.minimum(jnp.exp(spectrum(0)), 100.0)
    sine, cosine = sine_cosine(spectrum(1))
    wave_frames = first_frame + half_voc + lax.broadcasted_iota(jnp.int32, (voc_rows, 1), 0)
    exists = (wave_frames >= 0) & (wave_frames < at.seqs * rows)
    magnitude = jnp.where(exists, magnitude, 0.0)
    waves = jnp.dot(
        (magnitude * cosine).astype(jnp.bfloat16),
        dft[pl.ds(0, padded_bins)],
        preferred_element_type=jnp.float32,
    ) + jnp.dot(
        (magnitude * sine).astype(jnp.bfloat16),
        dft[pl.ds(padded_bins, padded_bins)],
        preferred_element_type=jnp.float32,
    )
    there = jnp.where(exists, 1.0, 0.0)
    total_audio = jnp.zeros((slab, padded_hop), jnp.float32)
    energy = jnp.zeros((slab, padded_hop), jnp.float32)
    for quarter in range(parts):
        begin = parts - quarter
        total_audio = total_audio + waves[
            begin : begin + slab, quarter * padded_hop : (quarter + 1) * padded_hop
        ]
        energy = energy + there[begin : begin + slab] * env_ref[quarter : quarter + 1]
    total_audio = total_audio / energy
    for c in range(padded_hop // 128):
        audio[c] = total_audio[:, c * 128 : (c + 1) * 128]
    pairs = slab // 2
    group = 2 * HOP // 128
    low_lanes = lax.broadcasted_iota(jnp.int32, (1, 128), 1) < HOP % 128
    even = [audio[c, pl.ds(0, pairs, stride=2)] for c in range(padded_hop // 128)]
    odd = [
        pltpu.roll(audio[c, pl.ds(1, pairs, stride=2)], HOP % 128, 1)
        for c in range(padded_hop // 128)
    ]
    full_tiles = HOP // 128
    lines = even[:full_tiles] + [jnp.where(low_lanes, even[full_tiles], odd[0])]
    for c in range(full_tiles):
        lines.append(jnp.where(low_lanes, odd[c], odd[c + 1]))
    for index in range(group):
        wave_out[pl.ds(index, pairs, stride=group)] = lines[index]


def hand_over(features, wave, features_out, wave_out, sems):
    copies = [
        pltpu.make_async_copy(features, features_out, sems.at[0]),
        pltpu.make_async_copy(wave, wave_out, sems.at[1]),
    ]
    for copy in copies:
        copy.start()
    for copy in copies:
        copy.wait()


def local(
    tokens,
    masked,
    used_frames,
    tables,
    mask_vec,
    attn_in,
    head_temp,
    attn_out,
    conv_in,
    conv_kernel,
    conv_out,
    voc_in,
    voc_kernel,
    voc_up,
    voc_down,
    voc_head,
    head_bias,
):
    groups, heads, seqs = (lax.axis_size(name) for name in ("groups", "head", "seq"))
    blocks = lax.axis_size(("head", "sub"))
    rows = tokens.shape[1]
    total = rows + 2 * HALO
    slab = rows // blocks
    columns = tables.shape[2]
    width = attn_in.shape[2]
    local_heads = head_temp.shape[0]
    bin_count = head_bias.shape[0] // 2
    fft_size = 2 * (bin_count - 1)
    parts = fft_size // HOP
    padded_bins = up_to(bin_count, 16)
    padded_hop = up_to(HOP, 128)
    rim = voc_kernel.shape[0] // 2 + parts // 2
    window_rows = up_to(slab + 2 * rim, 16)
    channels = conv_kernel.shape[1]
    dft, env = synthesis_constants(bin_count, fft_size, padded_bins, padded_hop)
    head_rows = voc_head.T
    owns = (attn_out, conv_out, voc_in, voc_up, voc_down, head_rows)
    vmem = pl.BlockSpec(memory_space=pltpu.VMEM)
    smem = pl.BlockSpec(memory_space=pltpu.SMEM)
    anywhere = pl.BlockSpec(memory_space=pl.ANY)
    dma = pltpu.SemaphoreType.DMA
    bf16, f32 = jnp.bfloat16, jnp.float32
    full_shapes = [(blocks,) + own.shape for own in owns[:5]] + [(blocks, 2 * padded_bins, width)]
    scratch = [pltpu.VMEM(shape, bf16) for shape in full_shapes]
    scratch += [
        pltpu.VMEM(tables.shape, bf16),
        pltpu.VMEM((1, attn_in.shape[1], 3 * width) if width % 128 == 0 else attn_in.shape, bf16),
        pltpu.VMEM(conv_in.shape, bf16),
        pltpu.VMEM(conv_kernel.shape, f32),
        pltpu.VMEM(voc_kernel.shape, f32),
        pltpu.VMEM(dft.shape, bf16),
        pltpu.VMEM(head_rows.shape, bf16),
        pltpu.VMEM((up_to(bin_count + padded_bins, 8), width), f32),
        pltpu.VMEM((2 * padded_bins, width), bf16),
        pltpu.VMEM((8, rows), f32),
        pltpu.VMEM((2, 8, 128), f32),
        pltpu.VMEM((blocks, total, columns), bf16),
        pltpu.VMEM((blocks, total, width), bf16),
        pltpu.VMEM((seqs, PIECES, 2, rows // PIECES, width), bf16),
        pltpu.VMEM((local_heads, total, width), bf16),
        pltpu.VMEM((local_heads, total, width), f32),
        pltpu.VMEM((local_heads, total, 128), f32),
        pltpu.VMEM((total, columns * blocks), f32),
        pltpu.VMEM((channels // 128, total + 64, 128), f32),
        pltpu.VMEM((blocks, window_rows, channels), bf16),
        pltpu.VMEM((blocks, window_rows, channels), bf16),
        pltpu.VMEM((padded_hop // 128, slab, 128), f32),
        dma((9,)),
        dma((2,)),
        dma((2,)),
        dma((PIECES + 1, 2 * heads)),
        dma((PIECES + 1, 2 * heads)),
        dma((2, 2 * heads)),
        dma((2, 2 * heads)),
        dma((seqs, PIECES)),
        dma((seqs, PIECES)),
        dma((seqs, PIECES)),
        dma((seqs, PIECES)),
        dma((blocks,)),
        dma((blocks,)),
    ]
    for _ in owns:
        scratch += weight_sems(heads, groups)
    sizes = (local_heads, width // local_heads, bin_count, padded_bins, fft_size)
    features, wave = pl.pallas_call(
        functools.partial(block_kernel, sizes),
        out_shape=[
            jax.ShapeDtypeStruct((slab, columns * blocks), bf16),
            jax.ShapeDtypeStruct((slab * HOP // 128, 128), f32),
        ],
        in_specs=[smem] * 2 + [vmem] * 5 + [anywhere] * (6 + WEIGHTS),
        out_specs=[vmem, vmem],
        scratch_shapes=scratch,
        compiler_params=pltpu.CompilerParams(
            collective_id=0, has_side_effects=True, vmem_limit_bytes=60 * 1024 * 1024
        ),
    )(
        used_frames, head_temp, tokens, masked, mask_vec, head_bias, env, tables, attn_in, conv_in, conv_kernel, voc_kernel, dft, *owns)
    features, wave = pl.pallas_call(
        hand_over,
        out_shape=[jax.ShapeDtypeStruct(out.shape, out.dtype) for out in (features, wave)],
        in_specs=[vmem] * 2,
        out_specs=[anywhere] * 2,
        scratch_shapes=[dma((2,))],
    )(features, wave)
    return features, wave.reshape(slab * HOP)


def solution(mesh):
    in_specs = (
        P(None, ("groups", "seq")),
        P(("groups", "seq")),
        P("groups"),
        P(None, None, ("head", "sub")),
        P(("head", "sub")),
        P(None, None, ("head", "sub")),
        P(("head", "sub")),
        P(("head", "sub"), None),
        P(None, None, ("head", "sub")),
        P(None, ("head", "sub")),
        P(("head", "sub"), None),
        P(("head", "sub"), None),
        P(),
        P(("head", "sub"), None),
        P(("head", "sub"), None),
        P(("head", "sub"), None),
        P(),
    )
    out_specs = (P(("groups", "seq", "head", "sub"), None), P(("groups", "seq", "head", "sub")))
    return jax.shard_map(local, mesh=mesh, in_specs=in_specs, out_specs=out_specs, check_vma=False)
```

```python
import functools
import math

import jax
import jax.numpy as jnp
import numpy as np
from jax import lax
from jax.experimental import pallas as pl
from jax.experimental.pallas import tpu as pltpu
from jax.sharding import PartitionSpec as P

HOP = 320


MESH = pl.DeviceIdType.MESH
HALO = 32


def remote(src, dst, send_sem, recv_sem, **where):
    return pltpu.make_async_remote_copy(
        src_ref=src,
        dst_ref=dst,
        send_sem=send_sem,
        recv_sem=recv_sem,
        device_id=where,
        device_id_type=MESH,
    )


class Place:
    def __init__(self):
        self.group, self.seq = lax.axis_index("groups"), lax.axis_index("seq")
        self.head, self.sub = lax.axis_index("head"), lax.axis_index("sub")
        self.groups, self.seqs = lax.axis_size("groups"), lax.axis_size("seq")
        self.heads = lax.axis_size("head")
        self.me = self.head * 2 + self.sub
        self.partner = 1 - self.sub

    def head_at(self, step):
        return lax.rem(self.head + step, self.heads)

    def group_at(self, step):
        return lax.rem(self.group + step, self.groups)


def enter(at):
    barrier = pltpu.get_barrier_semaphore()

    def greet(**where):
        pl.semaphore_signal(barrier, inc=1, device_id=where, device_id_type=MESH)

    for step in range(1, at.heads):
        greet(head=at.head_at(step))
        greet(head=at.head_at(step), sub=at.partner)
    for step in range(1, at.groups):
        greet(groups=at.group_at(step))
    greet(sub=at.partner)

    @pl.when(at.seq > 0)
    def _():
        greet(seq=at.seq - 1)

    @pl.when(at.seq < at.seqs - 1)
    def _():
        greet(seq=at.seq + 1)

    count = 2 * (at.heads - 1) + at.groups
    count = count + jnp.where(at.seq > 0, 1, 0) + jnp.where(at.seq < at.seqs - 1, 1, 0)
    return lambda: pl.semaphore_wait(barrier, count)


class Spread:
    def __init__(self, at, buffer, rows, sems):
        self.at, self.buffer, self.rows = at, buffer, rows
        self.send, self.recv = sems

    def part(self, block):
        return self.buffer.at[block, pl.ds(*self.rows)]

    def cross(self, step):
        block = self.part(self.at.me)
        return remote(
            block, block, self.send.at[step], self.recv.at[step], head=self.at.head_at(step)
        )

    def aside(self, step):
        block = self.part(self.at.head_at(self.at.heads - step) * 2 + self.at.sub)
        slot = self.at.heads + step
        return remote(block, block, self.send.at[slot], self.recv.at[slot], sub=self.at.partner)

    def start(self):
        for step in range(1, self.at.heads):
            self.cross(step).start()
        self.aside(0).start()

    def relay(self):
        for step in range(1, self.at.heads):
            self.cross(step).wait_recv()
            self.aside(step).start()

    def finish(self):
        for step in range(self.at.heads):
            if step > 0:
                self.cross(step).wait_send()
            self.aside(step).wait()


class Weight:
    def __init__(self, at, own, full, sems):
        self.at, self.own, self.full = at, own, full
        self.send, self.recv, self.local = sems
        self.length = own.shape[0] // at.groups

    def piece(self, block, part):
        start = pl.multiple_of(part * self.length, 16)
        return self.full.at[block, pl.ds(start, self.length)]

    def source(self, step):
        return self.at.head_at(self.at.heads - step) * 2 + self.at.sub

    def cross(self, step):
        start = pl.multiple_of(self.at.group * self.length, 16)
        return remote(
            self.own.at[pl.ds(start, self.length)],
            self.piece(self.at.me, self.at.group),
            self.send.at[step],
            self.recv.at[step],
            head=self.at.head_at(step),
        )

    def over(self, step, turn):
        block = self.piece(self.source(step), self.at.group)
        slot = self.at.heads + (step - 1) * self.at.groups + turn
        return remote(
            block, block, self.send.at[slot], self.recv.at[slot], groups=self.at.group_at(turn)
        )

    def aside(self, step, turn):
        part = self.at.group_at(self.at.groups - turn)
        block = self.piece(self.source(step), part)
        slot = self.at.heads * (1 + self.at.groups) + (step - 1) * self.at.groups + turn
        return remote(block, block, self.send.at[slot], self.recv.at[slot], sub=self.at.partner)

    def mine(self):
        return remote(
            self.own, self.full.at[self.at.me], self.send.at[0], self.recv.at[0], sub=self.at.partner
        )

    def kept(self):
        return pltpu.make_async_copy(self.own, self.full.at[self.at.me], self.local.at[0])

    def start(self):
        for step in range(1, self.at.heads):
            self.cross(step).start()
        self.mine().start()
        self.kept().start()

    def relay_cross(self):
        for step in range(1, self.at.heads):
            self.cross(step).wait_recv()
            for turn in range(1, self.at.groups):
                self.over(step, turn).start()
            self.aside(step, 0).start()

    def relay_over(self):
        for step in range(1, self.at.heads):
            for turn in range(1, self.at.groups):
                self.over(step, turn).wait_recv()
                self.aside(step, turn).start()

    def finish(self):
        self.mine().wait()
        self.kept().wait()
        for step in range(1, self.at.heads):
            self.cross(step).wait_send()
            for turn in range(1, self.at.groups):
                self.over(step, turn).wait_send()
            for turn in range(self.at.groups):
                self.aside(step, turn).wait()


def weight_sems(heads, groups):
    count = heads * (1 + 2 * groups)
    return [
        pltpu.SemaphoreType.DMA((count,)),
        pltpu.SemaphoreType.DMA((count,)),
        pltpu.SemaphoreType.DMA((1,)),
    ]


def norm_rows(values):
    average = jnp.mean(values, axis=-1, keepdims=True)
    centered = values - average
    return centered * lax.rsqrt(jnp.mean(centered * centered, axis=-1, keepdims=True) + 1e-05)


PIECES = 4
WEIGHTS = 6


def up_to(value, unit):
    return -(-value // unit) * unit


def synthesis_constants(bin_count, fft_size, padded_bins, padded_hop):
    parts = fft_size // HOP
    samples = np.arange(fft_size)
    window = 0.5 - 0.5 * np.cos(2.0 * np.pi / fft_size * samples)
    bins = np.arange(bin_count)[:, None]
    angle = 2.0 * np.pi / fft_size * (bins * samples[None, :] % fft_size)
    edge = (bins == 0) | (bins == bin_count - 1)
    factor = np.where(edge, 1.0, 2.0) / fft_size
    cosine = factor * np.cos(angle) * window
    sine = np.where(edge, 0.0, -factor * np.sin(angle) * window)

    def spread(table, rows, fill):
        result = np.full((rows, parts, padded_hop), fill)
        result[: table.shape[0], :, :HOP] = table.reshape(-1, parts, HOP)
        return result.reshape(rows, parts * padded_hop)

    tables = np.concatenate([spread(cosine, padded_bins, 0.0), spread(sine, padded_bins, 0.0)])
    energy = spread((window * window)[None, :], 1, 1.0).reshape(parts, padded_hop)
    energy = np.pad(energy, ((0, -parts % 8), (0, 0)), constant_values=1.0)
    return jnp.asarray(tables, jnp.bfloat16), jnp.asarray(energy, jnp.float32)


def sine_cosine(angle):
    turns = jnp.round(angle * (2.0 / math.pi))
    rest = angle - turns * 1.5703125
    rest = rest - turns * 4.837512969970703125e-4
    rest = rest - turns * 7.549789948768648e-8
    square = rest * rest
    sine = rest + rest * square * (
        -1.6666654611e-1 + square * (8.3321608736e-3 + square * -1.9515295891e-4)
    )
    cosine = 1.0 - 0.5 * square + square * square * (
        4.166664568298827e-2 + square * (-1.388731625493765e-3 + square * 2.443315711809948e-5)
    )
    quadrant = turns.astype(jnp.int32) & 3
    odd = (quadrant & 1) == 1
    sine, cosine = jnp.where(odd, cosine, sine), jnp.where(odd, sine, cosine)
    sine = jnp.where(quadrant >= 2, -sine, sine)
    cosine = jnp.where((quadrant == 1) | (quadrant == 2), -cosine, cosine)
    return sine, cosine


def mix(parts, full):
    if parts[0].shape[1] % 128 == 0:
        return jnp.dot(
            jnp.concatenate(parts, axis=1),
            full[...].reshape(-1, full.shape[2]),
            preferred_element_type=jnp.float32,
        )
    result = 0.0
    for block, part in enumerate(parts):
        result = result + jnp.dot(part, full[block], preferred_element_type=jnp.float32)
    return result


def block_kernel(sizes, *refs):
    (used_ref, temp_ref, tokens_ref, masked_ref, mask_ref, bias_ref, env_ref, tables_hbm, attn_hbm,
     conv_in_hbm, conv_kernel_hbm, voc_kernel_hbm, dft_hbm) = refs[:13]
    owns_hbm = list(refs[13 : 13 + WEIGHTS])
    feat_out, wave_out = refs[13 + WEIGHTS : 15 + WEIGHTS]
    refs = refs[15 + WEIGHTS :]
    fulls = refs[:WEIGHTS]
    (tables_ref, attn_ref, conv_in, conv_kernel, voc_kernel, dft, head_raw, head_wide, head_own,
     tok, tokh, emb, att, kvbuf, q_scr, acc, l_acc, stream, gated, win, act, audio) = refs[
        WEIGHTS : WEIGHTS + 22
    ]
    (load_sems, tok_send, tok_recv, e_send, e_recv, a_send, a_recv, r_send, r_recv, l_send,
     l_recv, s_send, s_recv) = refs[WEIGHTS + 22 : WEIGHTS + 35]
    wsems = refs[WEIGHTS + 35 :]
    local_heads, head_size, bin_count, padded_bins, fft_size = sizes
    at = Place()
    blocks, total, columns = emb.shape
    rows = total - 2 * HALO
    width = q_scr.shape[2]
    codes = tables_ref.shape[1]
    slab = rows // blocks
    padded_hop = env_ref.shape[1]
    parts = fft_size // HOP
    half_voc = voc_kernel.shape[0] // 2
    rim = half_voc + parts // 2
    taps = conv_kernel.shape[0]
    span_rows = win.shape[1]

    tokh[...] = jnp.zeros_like(tokh)
    wait_for_peers = enter(at)
    loads = []

    def load(source, target):
        copy = pltpu.make_async_copy(source, target, load_sems.at[len(loads)])
        copy.start()
        loads.append(copy)
        return copy

    tables_load = load(tables_hbm, tables_ref)
    joined = width % 128 == 0
    attn_loads = [
        load(attn_hbm.at[p], attn_ref.at[0, :, pl.ds(p * width, width)] if joined else attn_ref.at[p])
        for p in range(3)
    ]
    head_load = load(owns_hbm[5], head_raw)
    conv_loads = [load(conv_in_hbm, conv_in), load(conv_kernel_hbm, conv_kernel)]
    late_loads = [load(voc_kernel_hbm, voc_kernel), load(dft_hbm, dft)]

    first, last = at.seq == 0, at.seq == at.seqs - 1

    def tokens_up():
        return remote(tok.at[:, pl.ds(rows - 128, 128)], tokh.at[0],
                      tok_send.at[0], tok_recv.at[0], seq=at.seq + 1)

    def tokens_down():
        return remote(tok.at[:, pl.ds(0, 128)], tokh.at[1],
                      tok_send.at[1], tok_recv.at[1], seq=at.seq - 1)

    owns = owns_hbm[:5] + [head_own]
    weights = [Weight(at, owns[w], fulls[w], wsems[3 * w : 3 * w + 3]) for w in range(WEIGHTS)]

    ids = lax.broadcasted_iota(jnp.int32, (1, codes), 1).astype(jnp.float32)
    mask_row = mask_ref[...].astype(jnp.float32).reshape(1, columns)

    def embed(token_rows):
        result = token_rows[:, 3:4] * mask_row
        for level in range(3):
            hot = jnp.where(token_rows[:, level : level + 1] == ids, 1.0, 0.0).astype(jnp.bfloat16)
            result = result + jnp.dot(hot, tables_ref[level], preferred_element_type=jnp.float32)
        return result.astype(jnp.bfloat16)

    piece = rows // PIECES
    spans = [(p * piece, piece) for p in range(PIECES)] + [(rows, 2 * HALO)]
    spreads = [
        Spread(at, emb, span, (e_send.at[p], e_recv.at[p])) for p, span in enumerate(spans)
    ]
    is_masked = masked_ref[...].reshape(1, rows)
    tok[0:2] = tokens_ref[0:2].astype(jnp.float32)
    tok[2:3] = jnp.where(is_masked == 1, -1, tokens_ref[2:3]).astype(jnp.float32)
    tok[3:4] = is_masked.astype(jnp.float32)
    tok[4:8] = jnp.zeros((4, rows), jnp.float32)
    token_columns = tok[...].T
    tables_load.wait()
    for p in range(PIECES):
        emb[at.me, pl.ds(*spans[p])] = embed(token_columns[p * piece : (p + 1) * piece])
        if p == 0:
            wait_for_peers()
        spreads[p].start()
        if p == 0:

            @pl.when(jnp.logical_not(last))
            def _():
                tokens_up().start()

            @pl.when(jnp.logical_not(first))
            def _():
                tokens_down().start()

    @pl.when(jnp.logical_not(last))
    def _():
        tokens_up().wait_send()

    @pl.when(jnp.logical_not(first))
    def _():
        tokens_up().wait_recv()
        tokens_down().wait_send()

    @pl.when(jnp.logical_not(last))
    def _():
        tokens_down().wait_recv()

    halo_tokens = jnp.concatenate(
        [tokh[0].T[128 - HALO :], tokh[1].T[:HALO]], axis=0
    )
    emb[at.me, pl.ds(rows, 2 * HALO)] = embed(halo_tokens)
    spreads[PIECES].start()
    for weight in weights[:5]:
        weight.start()
    lanes = lax.broadcasted_iota(jnp.int32, (1, width), 1)
    in_head = [
        (lanes >= h * head_size) & (lanes < (h + 1) * head_size) for h in range(local_heads)
    ]

    def unit(projected):
        squares = projected * projected
        scale = jnp.zeros_like(projected)
        for h in range(local_heads):
            total_h = jnp.sum(jnp.where(in_head[h], squares, 0.0), axis=-1, keepdims=True)
            scale = jnp.where(in_head[h], lax.rsqrt(total_h + 1e-06), scale)
        return projected * scale

    def send_up(block, step, part):
        view = kvbuf.at[block, part]
        return remote(view, view, r_send.at[step, part], r_recv.at[step, part], seq=at.seq + 1)

    def send_down(block, step, part):
        view = kvbuf.at[block, part]
        return remote(view, view, l_send.at[step, part], l_recv.at[step, part], seq=at.seq - 1)

    for copy in attn_loads:
        copy.wait()
    for p, spread in enumerate(spreads):
        spread.relay()
        spread.finish()
        begin, count = spread.rows
        whole = jnp.concatenate([emb[block, pl.ds(begin, count)] for block in range(blocks)], axis=1)
        normed = norm_rows(whole.astype(jnp.float32)).astype(jnp.bfloat16)
        projected = [
            jnp.dot(normed, attn_ref[part], preferred_element_type=jnp.float32)
            for part in range(attn_ref.shape[0])
        ]
        if joined:
            projected = [projected[0][:, part * width : (part + 1) * width] for part in range(3)]
        query = unit(projected[0])
        for h in range(local_heads):
            q_scr[h, pl.ds(begin, count)] = jnp.where(in_head[h], query, 0.0).astype(jnp.bfloat16)
        if p < PIECES:
            kvbuf[at.seq, p, 0] = unit(projected[1]).astype(jnp.bfloat16)
            kvbuf[at.seq, p, 1] = projected[2].astype(jnp.bfloat16)

            @pl.when(jnp.logical_not(last))
            def _():
                send_up(at.seq, 0, p).start()

            @pl.when(jnp.logical_not(first))
            def _():
                send_down(at.seq, 0, p).start()

    head_load.wait()
    head_wide[pl.ds(0, 2 * bin_count)] = head_raw[...].astype(jnp.float32)
    tail_rows = head_wide.shape[0] - 2 * bin_count
    head_wide[pl.ds(2 * bin_count, tail_rows)] = jnp.zeros((tail_rows, width), jnp.float32)
    head_own[pl.ds(0, padded_bins)] = head_wide[pl.ds(0, padded_bins)].astype(jnp.bfloat16)
    head_own[pl.ds(padded_bins, padded_bins)] = head_wide[pl.ds(bin_count, padded_bins)].astype(
        jnp.bfloat16
    )

    weights[5].start()
    acc[...] = jnp.zeros_like(acc)
    l_acc[...] = jnp.zeros_like(l_acc)
    tile = total // 3
    keys = 2 * piece

    def attend(block, pair):
        frame = block * rows + pair * keys + lax.broadcasted_iota(jnp.int32, (1, keys), 1)
        live = frame < used_ref[0]
        sharps = [temp_ref[h] * 1.4426950408889634 for h in range(local_heads)]
        biases = [jnp.where(live, -sharp, -1e30) for sharp in sharps]
        key = jnp.concatenate([kvbuf[block, 2 * pair, 0], kvbuf[block, 2 * pair + 1, 0]])
        value = jnp.concatenate([kvbuf[block, 2 * pair, 1], kvbuf[block, 2 * pair + 1, 1]])
        for index in range(3):
            span = pl.ds(index * tile, tile)
            scores = lax.dot_general(
                jnp.concatenate([q_scr[h, span] for h in range(local_heads)]),
                key,
                (((1,), (1,)), ((), ())),
                preferred_element_type=jnp.float32,
            )
            chances = []
            for h in range(local_heads):
                chance = jnp.exp2(scores[h * tile : (h + 1) * tile] * sharps[h] + biases[h])
                part = chance[:, :128]
                for lane in range(128, keys, 128):
                    part = part + chance[:, lane : lane + 128]
                l_acc[h, span] += part
                chances.append(chance.astype(jnp.bfloat16))
            summed = jnp.dot(
                jnp.concatenate(chances), value, preferred_element_type=jnp.float32
            )
            for h in range(local_heads):
                acc[h, span] += summed[h * tile : (h + 1) * tile]

    order = [("cross", 0), ("cross", 1), ("cross", 2), ("over", 0), ("cross", 3), ("over", 1),
             ("cross", 4), ("over", 2)]
    stages = [0, 1, 2, 2, 4, 4, 5, 5]

    def relays(stage, later=False):
        for (kind, index), own_stage in zip(order, stages):
            if own_stage == stage or (later and own_stage > stage):
                if kind == "cross":
                    weights[index].relay_cross()
                else:
                    weights[index].relay_over()

    pairs_of = PIECES // 2
    rounds = pairs_of * (at.seqs - 1)

    def exchange(index, carry):
        step, pair = index // pairs_of, lax.rem(index, pairs_of)
        before = jnp.maximum(index - 1, 0)
        old_step, old_pair = before // pairs_of, lax.rem(before, pairs_of)
        arriving = index < rounds

        @pl.when(index < pairs_of)
        def _():
            attend(at.seq, index)

        for turn in range(2):
            part = 2 * pair + turn

            @pl.when(arriving & (step < at.seq))
            def _():
                block = at.seq - 1 - step
                send_up(block, step, part).wait_recv()

                @pl.when(jnp.logical_not(last))
                def _():
                    send_up(block, step + 1, part).start()

            @pl.when(arriving & (step < at.seqs - 1 - at.seq))
            def _():
                block = at.seq + 1 + step
                send_down(block, step, part).wait_recv()

                @pl.when(jnp.logical_not(first))
                def _():
                    send_down(block, step + 1, part).start()

            if turn == 0:

                @pl.when((index > 0) & (old_step < at.seq))
                def _():
                    attend(at.seq - 1 - old_step, old_pair)

            else:

                @pl.when((index > 0) & (old_step < at.seqs - 1 - at.seq))
                def _():
                    attend(at.seq + 1 + old_step, old_pair)

        for stage in range(min(6, rounds)):

            @pl.when(index == stage)
            def _():
                relays(stage)

        return carry

    lax.fori_loop(0, rounds + 1, exchange, 0)
    if rounds < 6:
        relays(rounds, later=True)

    part_rows = rows // 2
    tiles = [(0, part_rows), (part_rows, total - part_rows)]
    gathers = [
        Spread(at, att, span, (a_send.at[p], a_recv.at[p])) for p, span in enumerate(tiles)
    ]
    for (begin, count), gather in zip(tiles, gathers):
        value = jnp.zeros((count, width), jnp.float32)
        for h in range(local_heads):
            mean = acc[h, pl.ds(begin, count)] / jnp.sum(
                l_acc[h, pl.ds(begin, count)], axis=-1, keepdims=True
            )
            value = jnp.where(in_head[h], mean, value)
        att[at.me, pl.ds(begin, count)] = value.astype(jnp.bfloat16)
        gather.start()
    weights[5].relay_cross()

    def drain(step, carry):
        @pl.when(jnp.logical_not(last) & (step <= at.seq))
        def _():
            for part in range(PIECES):
                send_up(at.seq - step, step, part).wait_send()

        @pl.when(jnp.logical_not(first) & (step <= at.seqs - 1 - at.seq))
        def _():
            for part in range(PIECES):
                send_down(at.seq + step, step, part).wait_send()

        return carry

    lax.fori_loop(0, at.seqs - 1, drain, 0)
    for copy in conv_loads:
        copy.wait()
    weights[0].finish()
    weights[3].relay_over()
    channel_tiles = gated.shape[0]
    gated[:, pl.ds(total, gated.shape[1] - total)] = jnp.zeros(
        (channel_tiles, gated.shape[1] - total, 128), jnp.float32
    )
    zero_first = jnp.where(first, 0.0, 1.0)
    zero_last = jnp.where(last, 0.0, 1.0)
    for (begin, count), gather in zip(tiles, gathers):
        gather.relay()
        gather.finish()
        span = pl.ds(begin, count)
        base = jnp.concatenate([emb[block, span] for block in range(blocks)], axis=1)
        summed = base.astype(jnp.float32) + mix([att[block, span] for block in range(blocks)], fulls[0])
        if begin + count > rows:
            kept = rows - begin
            summed = jnp.concatenate(
                [
                    summed[:kept],
                    summed[kept : kept + HALO] * zero_first,
                    summed[kept + HALO :] * zero_last,
                ]
            )
        normed = norm_rows(summed).astype(jnp.bfloat16)
        value = jnp.dot(normed, conv_in[0], preferred_element_type=jnp.float32)
        signal = jnp.dot(normed, conv_in[1], preferred_element_type=jnp.float32)
        gate = (value * jax.nn.sigmoid(signal)).astype(jnp.bfloat16).astype(jnp.float32)
        for low, high, shift in (
            (0, rows, HALO), (rows, rows + HALO, -rows), (rows + HALO, total, 0)
        ):
            low, high = max(low, begin), min(high, begin + count)
            if low < high:
                target = pl.ds(low + shift, high - low)
                stream[target] = summed[low - begin : high - begin]
                for c in range(channel_tiles):
                    gated[c, target] = gate[
                        low - begin : high - begin, c * 128 : (c + 1) * 128
                    ]

    first_tap = HALO - rim - taps // 2
    lead = first_tap % 8
    chunk = span_rows // 2

    def convolve(member):
        base_row = pl.multiple_of(member * slab + first_tap - lead, 8)
        outs = []
        for part in range(2):
            line = []
            for c in range(channel_tiles):
                kernel = conv_kernel[:, c * 128 : (c + 1) * 128]
                reach = up_to(chunk + taps + lead, 8)
                source = gated[c, pl.ds(base_row + part * chunk, reach)]
                result = jnp.zeros((chunk, 128), jnp.float32)
                for turn in range(8):
                    shifted = source[turn:] if turn else source
                    for k in range(taps):
                        offset = lead + k - turn
                        if offset % 8 == 0 and offset >= 0:
                            result = result + kernel[k : k + 1] * shifted[offset : offset + chunk]
                line.append((result * jax.nn.sigmoid(result)).astype(jnp.bfloat16))
            outs.append(jnp.concatenate(line, axis=1))
        return jnp.concatenate(outs)

    def swap(slot, step, other, source):
        head, sub = at.head_at(step), lax.rem(at.sub + other, 2)
        if source is None:
            block = at.head_at(at.heads - step) * 2 + sub
            view = win.at[head * 2 + sub], act.at[block]
        else:
            view = win.at[head * 2 + sub], act.at[source]
        return remote(*view, s_send.at[slot], s_recv.at[slot], head=head, sub=sub)

    peers = [(step, other) for step in range(1, at.heads) for other in range(2)] + [(0, 1)]
    for slot, (step, other) in enumerate(peers):
        member = at.head_at(step) * 2 + lax.rem(at.sub + other, 2)
        win[member] = convolve(member)
        swap(slot, step, other, at.me).start()
    act[at.me] = convolve(at.me)

    weights[4].relay_over()
    weights[1].finish()
    for slot, (step, other) in enumerate(peers):
        swap(slot, step, other, at.me).wait_send()
        swap(slot, step, other, None).wait_recv()

    conv_sum = mix([act[block] for block in range(blocks)], fulls[1])
    window_at = HALO - rim
    slack = window_at % 8
    around = stream[pl.ds(pl.multiple_of(at.me * slab + window_at - slack, 8), span_rows + 8)]
    features = norm_rows(around[slack : slack + span_rows] + conv_sum)
    feat_out[...] = features[rim : rim + slab].astype(jnp.bfloat16)
    first_frame = at.seq * rows + at.me * slab - rim
    frames = first_frame + lax.broadcasted_iota(jnp.int32, (span_rows, 1), 0)
    weights[5].relay_over()
    weights[2].finish()
    base_rows = jnp.dot(
        features.astype(jnp.bfloat16),
        fulls[2][...].reshape(-1, fulls[2].shape[2]),
        preferred_element_type=jnp.float32,
    )
    base_rows = norm_rows(jnp.where((frames >= 0) & (frames < used_ref[0]), base_rows, 0.0))
    for copy in late_loads:
        copy.wait()
    voc_rows = up_to(slab + parts, 8)
    vdepth = jnp.zeros((voc_rows, base_rows.shape[1]), jnp.float32)
    for k in range(2 * half_voc + 1):
        vdepth = vdepth + voc_kernel[k : k + 1] * base_rows[k : k + voc_rows]
    inner = norm_rows(vdepth).astype(jnp.bfloat16)
    weights[3].finish()
    hidden = jnp.dot(
        inner, fulls[3][...].reshape(-1, fulls[3].shape[2]), preferred_element_type=jnp.float32
    )
    hidden = (0.5 * hidden * (1.0 + lax.erf(hidden * math.sqrt(0.5)))).astype(jnp.bfloat16)
    weights[4].finish()
    refined = base_rows[half_voc : half_voc + voc_rows] + jnp.dot(
        hidden, fulls[4][...].reshape(-1, fulls[4].shape[2]), preferred_element_type=jnp.float32
    )
    head_input = norm_rows(refined).astype(jnp.bfloat16)
    weights[5].finish()

    bias_row = bias_ref[...].reshape(1, 2 * bin_count)
    biases = [
        bias_row[:, :padded_bins],
        jnp.concatenate(
            [bias_row[:, bin_count:], jnp.zeros((1, padded_bins - bin_count), jnp.float32)], axis=1
        ),
    ]

    def spectrum(index):
        parts_of = [
            fulls[5][block, pl.ds(index * padded_bins, padded_bins)] for block in range(blocks)
        ]
        inputs = [head_input]
        if width % 128 == 0:
            parts_of = [jnp.concatenate(parts_of, axis=1)]
        else:
            inputs = [head_input[:, block * width : (block + 1) * width] for block in range(blocks)]
        result = 0.0
        for one_input, part in zip(inputs, parts_of):
            result = result + lax.dot_general(
                one_input, part, (((1,), (1,)), ((), ())), preferred_element_type=jnp.float32
            )
        return result + biases[index]

    magnitude = jnp.minimum(jnp.exp(spectrum(0)), 100.0)
    sine, cosine = sine_cosine(spectrum(1))
    wave_frames = first_frame + half_voc + lax.broadcasted_iota(jnp.int32, (voc_rows, 1), 0)
    exists = (wave_frames >= 0) & (wave_frames < at.seqs * rows)
    magnitude = jnp.where(exists, magnitude, 0.0)
    waves = jnp.dot(
        (magnitude * cosine).astype(jnp.bfloat16),
        dft[pl.ds(0, padded_bins)],
        preferred_element_type=jnp.float32,
    ) + jnp.dot(
        (magnitude * sine).astype(jnp.bfloat16),
        dft[pl.ds(padded_bins, padded_bins)],
        preferred_element_type=jnp.float32,
    )
    there = jnp.where(exists, 1.0, 0.0)
    total_audio = jnp.zeros((slab, padded_hop), jnp.float32)
    energy = jnp.zeros((slab, padded_hop), jnp.float32)
    for quarter in range(parts):
        begin = parts - quarter
        total_audio = total_audio + waves[
            begin : begin + slab, quarter * padded_hop : (quarter + 1) * padded_hop
        ]
        energy = energy + there[begin : begin + slab] * env_ref[quarter : quarter + 1]
    total_audio = total_audio / energy
    for c in range(padded_hop // 128):
        audio[c] = total_audio[:, c * 128 : (c + 1) * 128]
    pairs = slab // 2
    group = 2 * HOP // 128
    low_lanes = lax.broadcasted_iota(jnp.int32, (1, 128), 1) < HOP % 128
    even = [audio[c, pl.ds(0, pairs, stride=2)] for c in range(padded_hop // 128)]
    odd = [
        pltpu.roll(audio[c, pl.ds(1, pairs, stride=2)], HOP % 128, 1)
        for c in range(padded_hop // 128)
    ]
    full_tiles = HOP // 128
    lines = even[:full_tiles] + [jnp.where(low_lanes, even[full_tiles], odd[0])]
    for c in range(full_tiles):
        lines.append(jnp.where(low_lanes, odd[c], odd[c + 1]))
    for index in range(group):
        wave_out[pl.ds(index, pairs, stride=group)] = lines[index]


def hand_over(features, wave, features_out, wave_out, sems):
    copies = [
        pltpu.make_async_copy(features, features_out, sems.at[0]),
        pltpu.make_async_copy(wave, wave_out, sems.at[1]),
    ]
    for copy in copies:
        copy.start()
    for copy in copies:
        copy.wait()


def local(
    tokens,
    masked,
    used_frames,
    tables,
    mask_vec,
    attn_in,
    head_temp,
    attn_out,
    conv_in,
    conv_kernel,
    conv_out,
    voc_in,
    voc_kernel,
    voc_up,
    voc_down,
    voc_head,
    head_bias,
):
    groups, heads, seqs = (lax.axis_size(name) for name in ("groups", "head", "seq"))
    blocks = lax.axis_size(("head", "sub"))
    rows = tokens.shape[1]
    total = rows + 2 * HALO
    slab = rows // blocks
    columns = tables.shape[2]
    width = attn_in.shape[2]
    local_heads = head_temp.shape[0]
    bin_count = head_bias.shape[0] // 2
    fft_size = 2 * (bin_count - 1)
    parts = fft_size // HOP
    padded_bins = up_to(bin_count, 16)
    padded_hop = up_to(HOP, 128)
    rim = voc_kernel.shape[0] // 2 + parts // 2
    window_rows = up_to(slab + 2 * rim, 16)
    channels = conv_kernel.shape[1]
    dft, env = synthesis_constants(bin_count, fft_size, padded_bins, padded_hop)
    head_rows = voc_head.T
    owns = (attn_out, conv_out, voc_in, voc_up, voc_down, head_rows)
    vmem = pl.BlockSpec(memory_space=pltpu.VMEM)
    smem = pl.BlockSpec(memory_space=pltpu.SMEM)
    anywhere = pl.BlockSpec(memory_space=pl.ANY)
    dma = pltpu.SemaphoreType.DMA
    bf16, f32 = jnp.bfloat16, jnp.float32
    full_shapes = [(blocks,) + own.shape for own in owns[:5]] + [(blocks, 2 * padded_bins, width)]
    scratch = [pltpu.VMEM(shape, bf16) for shape in full_shapes]
    scratch += [
        pltpu.VMEM(tables.shape, bf16),
        pltpu.VMEM((1, attn_in.shape[1], 3 * width) if width % 128 == 0 else attn_in.shape, bf16),
        pltpu.VMEM(conv_in.shape, bf16),
        pltpu.VMEM(conv_kernel.shape, f32),
        pltpu.VMEM(voc_kernel.shape, f32),
        pltpu.VMEM(dft.shape, bf16),
        pltpu.VMEM(head_rows.shape, bf16),
        pltpu.VMEM((up_to(bin_count + padded_bins, 8), width), f32),
        pltpu.VMEM((2 * padded_bins, width), bf16),
        pltpu.VMEM((8, rows), f32),
        pltpu.VMEM((2, 8, 128), f32),
        pltpu.VMEM((blocks, total, columns), bf16),
        pltpu.VMEM((blocks, total, width), bf16),
        pltpu.VMEM((seqs, PIECES, 2, rows // PIECES, width), bf16),
        pltpu.VMEM((local_heads, total, width), bf16),
        pltpu.VMEM((local_heads, total, width), f32),
        pltpu.VMEM((local_heads, total, 128), f32),
        pltpu.VMEM((total, columns * blocks), f32),
        pltpu.VMEM((channels // 128, total + 64, 128), f32),
        pltpu.VMEM((blocks, window_rows, channels), bf16),
        pltpu.VMEM((blocks, window_rows, channels), bf16),
        pltpu.VMEM((padded_hop // 128, slab, 128), f32),
        dma((9,)),
        dma((2,)),
        dma((2,)),
        dma((PIECES + 1, 2 * heads)),
        dma((PIECES + 1, 2 * heads)),
        dma((2, 2 * heads)),
        dma((2, 2 * heads)),
        dma((seqs, PIECES)),
        dma((seqs, PIECES)),
        dma((seqs, PIECES)),
        dma((seqs, PIECES)),
        dma((blocks,)),
        dma((blocks,)),
    ]
    for _ in owns:
        scratch += weight_sems(heads, groups)
    sizes = (local_heads, width // local_heads, bin_count, padded_bins, fft_size)
    features, wave = pl.pallas_call(
        functools.partial(block_kernel, sizes),
        out_shape=[
            jax.ShapeDtypeStruct((slab, columns * blocks), bf16),
            jax.ShapeDtypeStruct((slab * HOP // 128, 128), f32),
        ],
        in_specs=[smem] * 2 + [vmem] * 5 + [anywhere] * (6 + WEIGHTS),
        out_specs=[vmem, vmem],
        scratch_shapes=scratch,
        compiler_params=pltpu.CompilerParams(
            collective_id=0, has_side_effects=True, vmem_limit_bytes=60 * 1024 * 1024
        ),
    )(
        used_frames, head_temp, tokens, masked, mask_vec, head_bias, env, tables, attn_in, conv_in, conv_kernel, voc_kernel, dft, *owns)
    features, wave = pl.pallas_call(
        hand_over,
        out_shape=[jax.ShapeDtypeStruct(out.shape, out.dtype) for out in (features, wave)],
        in_specs=[vmem] * 2,
        out_specs=[anywhere] * 2,
        scratch_shapes=[dma((2,))],
    )(features, wave)
    return features, wave.reshape(slab * HOP)


def solution(mesh):
    in_specs = (
        P(None, ("groups", "seq")),
        P(("groups", "seq")),
        P("groups"),
        P(None, None, ("head", "sub")),
        P(("head", "sub")),
        P(None, None, ("head", "sub")),
        P(("head", "sub")),
        P(("head", "sub"), None),
        P(None, None, ("head", "sub")),
        P(None, ("head", "sub")),
        P(("head", "sub"), None),
        P(("head", "sub"), None),
        P(),
        P(("head", "sub"), None),
        P(("head", "sub"), None),
        P(("head", "sub"), None),
        P(),
    )
    out_specs = (P(("groups", "seq", "head", "sub"), None), P(("groups", "seq", "head", "sub")))
    return jax.shard_map(local, mesh=mesh, in_specs=in_specs, out_specs=out_specs, check_vma=False)
```

```python
import functools
import math

import jax
import jax.numpy as jnp
import numpy as np
from jax import lax
from jax.experimental import pallas as pl
from jax.experimental.pallas import tpu as pltpu
from jax.sharding import PartitionSpec as P

HOP = 320


MESH = pl.DeviceIdType.MESH
HALO = 32


def remote(src, dst, send_sem, recv_sem, **where):
    return pltpu.make_async_remote_copy(
        src_ref=src,
        dst_ref=dst,
        send_sem=send_sem,
        recv_sem=recv_sem,
        device_id=where,
        device_id_type=MESH,
    )


class Place:
    def __init__(self):
        self.group, self.seq = lax.axis_index("groups"), lax.axis_index("seq")
        self.head, self.sub = lax.axis_index("head"), lax.axis_index("sub")
        self.groups, self.seqs = lax.axis_size("groups"), lax.axis_size("seq")
        self.heads = lax.axis_size("head")
        self.me = self.head * 2 + self.sub
        self.partner = 1 - self.sub

    def head_at(self, step):
        return lax.rem(self.head + step, self.heads)

    def group_at(self, step):
        return lax.rem(self.group + step, self.groups)


def enter(at):
    barrier = pltpu.get_barrier_semaphore()

    def greet(**where):
        pl.semaphore_signal(barrier, inc=1, device_id=where, device_id_type=MESH)

    for step in range(1, at.heads):
        greet(head=at.head_at(step))
        greet(head=at.head_at(step), sub=at.partner)
    for step in range(1, at.groups):
        greet(groups=at.group_at(step))
    greet(sub=at.partner)

    @pl.when(at.seq > 0)
    def _():
        greet(seq=at.seq - 1)

    @pl.when(at.seq < at.seqs - 1)
    def _():
        greet(seq=at.seq + 1)

    count = 2 * (at.heads - 1) + at.groups
    count = count + jnp.where(at.seq > 0, 1, 0) + jnp.where(at.seq < at.seqs - 1, 1, 0)
    return lambda: pl.semaphore_wait(barrier, count)


class Spread:
    def __init__(self, at, buffer, rows, sems):
        self.at, self.buffer, self.rows = at, buffer, rows
        self.send, self.recv = sems

    def part(self, block, head):
        begin, count = self.rows
        if callable(begin):
            begin = begin(head)
        return self.buffer.at[block, pl.ds(begin, count)]

    def cross(self, step):
        block = self.part(self.at.me, self.at.head_at(step))
        return remote(
            block, block, self.send.at[step], self.recv.at[step], head=self.at.head_at(step)
        )

    def aside(self, step):
        source = self.at.head_at(self.at.heads - step) * 2 + self.at.sub
        block = self.part(source, self.at.head)
        slot = self.at.heads + step
        return remote(block, block, self.send.at[slot], self.recv.at[slot], sub=self.at.partner)

    def start(self):
        for step in range(1, self.at.heads):
            self.cross(step).start()
        self.aside(0).start()

    def relay(self):
        for step in range(1, self.at.heads):
            self.cross(step).wait_recv()
            self.aside(step).start()

    def finish(self):
        for step in range(self.at.heads):
            if step > 0:
                self.cross(step).wait_send()
            self.aside(step).wait()


class Weight:
    def __init__(self, at, own, full, sems):
        self.at, self.own, self.full = at, own, full
        self.send, self.recv, self.local = sems
        self.length = own.shape[0] // at.groups

    def piece(self, block, part):
        start = pl.multiple_of(part * self.length, 16)
        return self.full.at[block, pl.ds(start, self.length)]

    def source(self, step):
        return self.at.head_at(self.at.heads - step) * 2 + self.at.sub

    def cross(self, step):
        start = pl.multiple_of(self.at.group * self.length, 16)
        return remote(
            self.own.at[pl.ds(start, self.length)],
            self.piece(self.at.me, self.at.group),
            self.send.at[step],
            self.recv.at[step],
            head=self.at.head_at(step),
        )

    def over(self, step, turn):
        block = self.piece(self.source(step), self.at.group)
        slot = self.at.heads + (step - 1) * self.at.groups + turn
        return remote(
            block, block, self.send.at[slot], self.recv.at[slot], groups=self.at.group_at(turn)
        )

    def aside(self, step, turn):
        part = self.at.group_at(self.at.groups - turn)
        block = self.piece(self.source(step), part)
        slot = self.at.heads * (1 + self.at.groups) + (step - 1) * self.at.groups + turn
        return remote(block, block, self.send.at[slot], self.recv.at[slot], sub=self.at.partner)

    def mine(self):
        return remote(
            self.own, self.full.at[self.at.me], self.send.at[0], self.recv.at[0], sub=self.at.partner
        )

    def kept(self):
        return pltpu.make_async_copy(self.own, self.full.at[self.at.me], self.local.at[0])

    def start(self):
        for step in range(1, self.at.heads):
            self.cross(step).start()
        self.mine().start()
        self.kept().start()

    def relay_cross(self):
        for step in range(1, self.at.heads):
            self.cross(step).wait_recv()
            for turn in range(1, self.at.groups):
                self.over(step, turn).start()
            self.aside(step, 0).start()

    def relay_over(self):
        for step in range(1, self.at.heads):
            for turn in range(1, self.at.groups):
                self.over(step, turn).wait_recv()
                self.aside(step, turn).start()

    def finish(self):
        self.mine().wait()
        self.kept().wait()
        for step in range(1, self.at.heads):
            self.cross(step).wait_send()
            for turn in range(1, self.at.groups):
                self.over(step, turn).wait_send()
            for turn in range(self.at.groups):
                self.aside(step, turn).wait()


def weight_sems(heads, groups):
    count = heads * (1 + 2 * groups)
    return [
        pltpu.SemaphoreType.DMA((count,)),
        pltpu.SemaphoreType.DMA((count,)),
        pltpu.SemaphoreType.DMA((1,)),
    ]


def norm_rows(values):
    average = jnp.mean(values, axis=-1, keepdims=True)
    centered = values - average
    return centered * lax.rsqrt(jnp.mean(centered * centered, axis=-1, keepdims=True) + 1e-05)


PIECES = 4
WEIGHTS = 6


def up_to(value, unit):
    return -(-value // unit) * unit


def synthesis_constants(bin_count, fft_size, padded_bins, padded_hop):
    parts = fft_size // HOP
    samples = np.arange(fft_size)
    window = 0.5 - 0.5 * np.cos(2.0 * np.pi / fft_size * samples)
    bins = np.arange(bin_count)[:, None]
    angle = 2.0 * np.pi / fft_size * (bins * samples[None, :] % fft_size)
    edge = (bins == 0) | (bins == bin_count - 1)
    factor = np.where(edge, 1.0, 2.0) / fft_size
    cosine = factor * np.cos(angle) * window
    sine = np.where(edge, 0.0, -factor * np.sin(angle) * window)

    def spread(table, rows, fill):
        result = np.full((rows, parts, padded_hop), fill)
        result[: table.shape[0], :, :HOP] = table.reshape(-1, parts, HOP)
        return result.reshape(rows, parts * padded_hop)

    tables = np.concatenate([spread(cosine, padded_bins, 0.0), spread(sine, padded_bins, 0.0)])
    energy = spread((window * window)[None, :], 1, 1.0).reshape(parts, padded_hop)
    energy = np.pad(energy, ((0, -parts % 8), (0, 0)), constant_values=1.0)
    return jnp.asarray(tables, jnp.bfloat16), jnp.asarray(energy, jnp.float32)


def sine_cosine(angle):
    turns = jnp.round(angle * (2.0 / math.pi))
    rest = angle - turns * 1.5703125
    rest = rest - turns * 4.837512969970703125e-4
    rest = rest - turns * 7.549789948768648e-8
    square = rest * rest
    sine = rest + rest * square * (
        -1.6666654611e-1 + square * (8.3321608736e-3 + square * -1.9515295891e-4)
    )
    cosine = 1.0 - 0.5 * square + square * square * (
        4.166664568298827e-2 + square * (-1.388731625493765e-3 + square * 2.443315711809948e-5)
    )
    quadrant = turns.astype(jnp.int32) & 3
    odd = (quadrant & 1) == 1
    sine, cosine = jnp.where(odd, cosine, sine), jnp.where(odd, sine, cosine)
    sine = jnp.where(quadrant >= 2, -sine, sine)
    cosine = jnp.where((quadrant == 1) | (quadrant == 2), -cosine, cosine)
    return sine, cosine


def mix(parts, full):
    if parts[0].shape[1] % 128 == 0:
        return jnp.dot(
            jnp.concatenate(parts, axis=1),
            full[...].reshape(-1, full.shape[2]),
            preferred_element_type=jnp.float32,
        )
    result = 0.0
    for block, part in enumerate(parts):
        result = result + jnp.dot(part, full[block], preferred_element_type=jnp.float32)
    return result


def block_kernel(sizes, *refs):
    (used_ref, temp_ref, tokens_ref, masked_ref, mask_ref, bias_ref, env_ref, tables_hbm, attn_hbm,
     conv_in_hbm, conv_kernel_hbm, voc_kernel_hbm, dft_hbm) = refs[:13]
    owns_hbm = list(refs[13 : 13 + WEIGHTS])
    feat_hbm, wave_hbm = refs[13 + WEIGHTS : 15 + WEIGHTS]
    refs = refs[15 + WEIGHTS :]
    fulls = refs[:WEIGHTS]
    (tables_ref, attn_ref, conv_in, conv_kernel, voc_kernel, dft, head_raw, head_wide, head_own,
     tok, tokh, emb, att, kvbuf, q_scr, acc, l_acc, stream, gated, win, act, audio,
     feat_out, wave_out) = refs[
        WEIGHTS : WEIGHTS + 24
    ]
    (load_sems, tok_send, tok_recv, e_send, e_recv, a_send, a_recv, r_send, r_recv, l_send,
     l_recv, s_send, s_recv) = refs[WEIGHTS + 24 : WEIGHTS + 37]
    wsems = refs[WEIGHTS + 37 :]
    local_heads, head_size, bin_count, padded_bins, fft_size = sizes
    at = Place()
    blocks, total, columns = emb.shape
    rows = total - 2 * HALO
    width = q_scr.shape[2]
    codes = tables_ref.shape[1]
    slab = rows // blocks
    padded_hop = env_ref.shape[1]
    parts = fft_size // HOP
    half_voc = voc_kernel.shape[0] // 2
    rim = half_voc + parts // 2
    taps = conv_kernel.shape[0]
    span_rows = win.shape[1]

    tokh[...] = jnp.zeros_like(tokh)
    wait_for_peers = enter(at)
    loads = []

    def load(source, target):
        copy = pltpu.make_async_copy(source, target, load_sems.at[len(loads)])
        copy.start()
        loads.append(copy)
        return copy

    tables_load = load(tables_hbm, tables_ref)
    joined = width % 128 == 0
    attn_loads = [
        load(attn_hbm.at[p], attn_ref.at[0, :, pl.ds(p * width, width)] if joined else attn_ref.at[p])
        for p in range(3)
    ]
    head_load = load(owns_hbm[5], head_raw)
    conv_loads = [load(conv_in_hbm, conv_in), load(conv_kernel_hbm, conv_kernel)]
    late_loads = [load(voc_kernel_hbm, voc_kernel), load(dft_hbm, dft)]

    first, last = at.seq == 0, at.seq == at.seqs - 1

    def tokens_up():
        return remote(tok.at[:, pl.ds(rows - 128, 128)], tokh.at[0],
                      tok_send.at[0], tok_recv.at[0], seq=at.seq + 1)

    def tokens_down():
        return remote(tok.at[:, pl.ds(0, 128)], tokh.at[1],
                      tok_send.at[1], tok_recv.at[1], seq=at.seq - 1)

    owns = owns_hbm[:5] + [head_own]
    weights = [Weight(at, owns[w], fulls[w], wsems[3 * w : 3 * w + 3]) for w in range(WEIGHTS)]

    ids = lax.broadcasted_iota(jnp.int32, (1, codes), 1).astype(jnp.float32)
    mask_row = mask_ref[...].astype(jnp.float32).reshape(1, columns)

    def embed(token_rows):
        result = token_rows[:, 3:4] * mask_row
        for level in range(3):
            hot = jnp.where(token_rows[:, level : level + 1] == ids, 1.0, 0.0).astype(jnp.bfloat16)
            result = result + jnp.dot(hot, tables_ref[level], preferred_element_type=jnp.float32)
        return result.astype(jnp.bfloat16)

    piece = rows // PIECES
    spans = [(p * piece, piece) for p in range(PIECES)] + [(rows, 2 * HALO)]
    spreads = [
        Spread(at, emb, span, (e_send.at[p], e_recv.at[p])) for p, span in enumerate(spans)
    ]
    is_masked = masked_ref[...].reshape(1, rows)
    tok[0:2] = tokens_ref[0:2].astype(jnp.float32)
    tok[2:3] = jnp.where(is_masked == 1, -1, tokens_ref[2:3]).astype(jnp.float32)
    tok[3:4] = is_masked.astype(jnp.float32)
    tok[4:8] = jnp.zeros((4, rows), jnp.float32)
    token_columns = tok[...].T
    tables_load.wait()
    for p in range(PIECES):
        emb[at.me, pl.ds(*spans[p])] = embed(token_columns[p * piece : (p + 1) * piece])
        if p == 0:
            wait_for_peers()
        spreads[p].start()
        if p == 0:

            @pl.when(jnp.logical_not(last))
            def _():
                tokens_up().start()

            @pl.when(jnp.logical_not(first))
            def _():
                tokens_down().start()

    @pl.when(jnp.logical_not(last))
    def _():
        tokens_up().wait_send()

    @pl.when(jnp.logical_not(first))
    def _():
        tokens_up().wait_recv()
        tokens_down().wait_send()

    @pl.when(jnp.logical_not(last))
    def _():
        tokens_down().wait_recv()

    halo_tokens = jnp.concatenate(
        [tokh[0].T[128 - HALO :], tokh[1].T[:HALO]], axis=0
    )
    emb[at.me, pl.ds(rows, 2 * HALO)] = embed(halo_tokens)
    spreads[PIECES].start()
    for weight in weights[:5]:
        weight.start()
    lanes = lax.broadcasted_iota(jnp.int32, (1, width), 1)
    in_head = [
        (lanes >= h * head_size) & (lanes < (h + 1) * head_size) for h in range(local_heads)
    ]

    def unit(projected):
        squares = projected * projected
        scale = jnp.zeros_like(projected)
        for h in range(local_heads):
            total_h = jnp.sum(jnp.where(in_head[h], squares, 0.0), axis=-1, keepdims=True)
            scale = jnp.where(in_head[h], lax.rsqrt(total_h + 1e-06), scale)
        return projected * scale

    def send_up(block, step, part):
        view = kvbuf.at[block, part]
        return remote(view, view, r_send.at[step, part], r_recv.at[step, part], seq=at.seq + 1)

    def send_down(block, step, part):
        view = kvbuf.at[block, part]
        return remote(view, view, l_send.at[step, part], l_recv.at[step, part], seq=at.seq - 1)

    for copy in attn_loads:
        copy.wait()
    for p, spread in enumerate(spreads):
        spread.relay()
        spread.finish()
        begin, count = spread.rows
        whole = jnp.concatenate([emb[block, pl.ds(begin, count)] for block in range(blocks)], axis=1)
        normed = norm_rows(whole.astype(jnp.float32)).astype(jnp.bfloat16)
        projected = [
            jnp.dot(normed, attn_ref[part], preferred_element_type=jnp.float32)
            for part in range(attn_ref.shape[0])
        ]
        if joined:
            projected = [projected[0][:, part * width : (part + 1) * width] for part in range(3)]
        query = unit(projected[0])
        for h in range(local_heads):
            q_scr[h, pl.ds(begin, count)] = jnp.where(in_head[h], query, 0.0).astype(jnp.bfloat16)
        if p < PIECES:
            kvbuf[at.seq, p, 0] = unit(projected[1]).astype(jnp.bfloat16)
            kvbuf[at.seq, p, 1] = projected[2].astype(jnp.bfloat16)

            @pl.when(jnp.logical_not(last))
            def _():
                send_up(at.seq, 0, p).start()

            @pl.when(jnp.logical_not(first))
            def _():
                send_down(at.seq, 0, p).start()

    head_load.wait()
    head_wide[pl.ds(0, 2 * bin_count)] = head_raw[...].astype(jnp.float32)
    tail_rows = head_wide.shape[0] - 2 * bin_count
    head_wide[pl.ds(2 * bin_count, tail_rows)] = jnp.zeros((tail_rows, width), jnp.float32)
    head_own[pl.ds(0, padded_bins)] = head_wide[pl.ds(0, padded_bins)].astype(jnp.bfloat16)
    head_own[pl.ds(padded_bins, padded_bins)] = head_wide[pl.ds(bin_count, padded_bins)].astype(
        jnp.bfloat16
    )

    weights[5].start()
    acc[...] = jnp.zeros_like(acc)
    l_acc[...] = jnp.zeros_like(l_acc)
    tile = total // 3
    keys = 2 * piece

    def attend(block, pair):
        frame = block * rows + pair * keys + lax.broadcasted_iota(jnp.int32, (1, keys), 1)
        live = frame < used_ref[0]
        sharps = [temp_ref[h] * 1.4426950408889634 for h in range(local_heads)]
        biases = [jnp.where(live, -sharp, -1e30) for sharp in sharps]
        key = jnp.concatenate([kvbuf[block, 2 * pair, 0], kvbuf[block, 2 * pair + 1, 0]])
        value = jnp.concatenate([kvbuf[block, 2 * pair, 1], kvbuf[block, 2 * pair + 1, 1]])
        for index in range(3):
            span = pl.ds(index * tile, tile)
            scores = lax.dot_general(
                jnp.concatenate([q_scr[h, span] for h in range(local_heads)]),
                key,
                (((1,), (1,)), ((), ())),
                preferred_element_type=jnp.float32,
            )
            chances = []
            for h in range(local_heads):
                chance = jnp.exp2(scores[h * tile : (h + 1) * tile] * sharps[h] + biases[h])
                part = chance[:, :128]
                for lane in range(128, keys, 128):
                    part = part + chance[:, lane : lane + 128]
                l_acc[h, span] += part
                chances.append(chance.astype(jnp.bfloat16))
            summed = jnp.dot(
                jnp.concatenate(chances), value, preferred_element_type=jnp.float32
            )
            for h in range(local_heads):
                acc[h, span] += summed[h * tile : (h + 1) * tile]

    order = [("cross", 0), ("cross", 1), ("cross", 2), ("over", 0), ("cross", 3), ("over", 1),
             ("cross", 4), ("over", 2)]
    stages = [0, 1, 2, 2, 4, 4, 5, 5]

    def relays(stage, later=False):
        for (kind, index), own_stage in zip(order, stages):
            if own_stage == stage or (later and own_stage > stage):
                if kind == "cross":
                    weights[index].relay_cross()
                else:
                    weights[index].relay_over()

    pairs_of = PIECES // 2
    rounds = pairs_of * (at.seqs - 1)

    def exchange(index, carry):
        step, pair = index // pairs_of, lax.rem(index, pairs_of)
        before = jnp.maximum(index - 1, 0)
        old_step, old_pair = before // pairs_of, lax.rem(before, pairs_of)
        arriving = index < rounds

        @pl.when(index < pairs_of)
        def _():
            attend(at.seq, index)

        for turn in range(2):
            part = 2 * pair + turn

            @pl.when(arriving & (step < at.seq))
            def _():
                block = at.seq - 1 - step
                send_up(block, step, part).wait_recv()

                @pl.when(jnp.logical_not(last))
                def _():
                    send_up(block, step + 1, part).start()

            @pl.when(arriving & (step < at.seqs - 1 - at.seq))
            def _():
                block = at.seq + 1 + step
                send_down(block, step, part).wait_recv()

                @pl.when(jnp.logical_not(first))
                def _():
                    send_down(block, step + 1, part).start()

            if turn == 0:

                @pl.when((index > 0) & (old_step < at.seq))
                def _():
                    attend(at.seq - 1 - old_step, old_pair)

            else:

                @pl.when((index > 0) & (old_step < at.seqs - 1 - at.seq))
                def _():
                    attend(at.seq + 1 + old_step, old_pair)

        for stage in range(min(6, rounds)):

            @pl.when(index == stage)
            def _():
                relays(stage)

        return carry

    lax.fori_loop(0, rounds + 1, exchange, 0)
    if rounds < 6:
        relays(rounds, later=True)

    early = at.heads == 2
    near = rows // 2 + HALO
    far = rows - near

    def near_at(head):
        return pl.multiple_of(jnp.where(head == 0, far, 0), HALO) if early else 0

    def far_at(head):
        return pl.multiple_of(jnp.where(head == 0, 0, near), HALO) if early else near

    tiles = [(near_at, near), (rows, 2 * HALO), (far_at, far)]
    gathers = [
        Spread(at, att, span, (a_send.at[p], a_recv.at[p])) for p, span in enumerate(tiles)
    ]
    value = jnp.zeros((total, width), jnp.float32)
    for h in range(local_heads):
        mean = acc[h] / jnp.sum(l_acc[h], axis=-1, keepdims=True)
        value = jnp.where(in_head[h], mean, value)
    att[at.me] = value.astype(jnp.bfloat16)
    for gather in gathers:
        gather.start()
    weights[5].relay_cross()

    def drain(step, carry):
        @pl.when(jnp.logical_not(last) & (step <= at.seq))
        def _():
            for part in range(PIECES):
                send_up(at.seq - step, step, part).wait_send()

        @pl.when(jnp.logical_not(first) & (step <= at.seqs - 1 - at.seq))
        def _():
            for part in range(PIECES):
                send_down(at.seq + step, step, part).wait_send()

        return carry

    lax.fori_loop(0, at.seqs - 1, drain, 0)
    for copy in conv_loads:
        copy.wait()
    weights[0].finish()
    weights[3].relay_over()
    channel_tiles = gated.shape[0]
    gated[:, pl.ds(total, gated.shape[1] - total)] = jnp.zeros(
        (channel_tiles, gated.shape[1] - total, 128), jnp.float32
    )
    zero_first = jnp.where(first, 0.0, 1.0)
    zero_last = jnp.where(last, 0.0, 1.0)

    def convolution_input(pieces):
        for piece_at in pieces:
            gathers[piece_at].relay()
            gathers[piece_at].finish()
        spans = [
            pl.ds(tiles[p][0](at.head) if callable(tiles[p][0]) else tiles[p][0], tiles[p][1])
            for p in pieces
        ]

        def gathered(buffer, block):
            return jnp.concatenate([buffer[block, span] for span in spans])

        base = jnp.concatenate([gathered(emb, block) for block in range(blocks)], axis=1)
        summed = base.astype(jnp.float32) + mix(
            [gathered(att, block) for block in range(blocks)], fulls[0]
        )
        body_rows = tiles[pieces[0]][1]
        targets = [(0, body_rows, pl.multiple_of(spans[0].start + HALO, HALO))]
        if len(pieces) > 1:
            summed = jnp.concatenate(
                [
                    summed[:body_rows],
                    summed[body_rows : body_rows + HALO] * zero_first,
                    summed[body_rows + HALO :] * zero_last,
                ]
            )
            targets += [(body_rows, HALO, 0), (body_rows + HALO, HALO, total - HALO)]
        normed = norm_rows(summed).astype(jnp.bfloat16)
        value = jnp.dot(normed, conv_in[0], preferred_element_type=jnp.float32)
        signal = jnp.dot(normed, conv_in[1], preferred_element_type=jnp.float32)
        gate = (value * jax.nn.sigmoid(signal)).astype(jnp.bfloat16).astype(jnp.float32)
        for low, length, start in targets:
            target = pl.ds(start, length)
            stream[target] = summed[low : low + length]
            for c in range(channel_tiles):
                gated[c, target] = gate[low : low + length, c * 128 : (c + 1) * 128]

    convolution_input([0, 1])
    if not early:
        convolution_input([2])
    first_tap = HALO - rim - taps // 2
    lead = first_tap % 8
    chunk = span_rows // 2

    def convolve(member):
        base_row = pl.multiple_of(member * slab + first_tap - lead, 8)
        outs = []
        for part in range(2):
            line = []
            for c in range(channel_tiles):
                kernel = conv_kernel[:, c * 128 : (c + 1) * 128]
                reach = up_to(chunk + taps + lead, 8)
                source = gated[c, pl.ds(base_row + part * chunk, reach)]
                result = jnp.zeros((chunk, 128), jnp.float32)
                for turn in range(8):
                    shifted = source[turn:] if turn else source
                    for k in range(taps):
                        offset = lead + k - turn
                        if offset % 8 == 0 and offset >= 0:
                            result = result + kernel[k : k + 1] * shifted[offset : offset + chunk]
                line.append((result * jax.nn.sigmoid(result)).astype(jnp.bfloat16))
            outs.append(jnp.concatenate(line, axis=1))
        return jnp.concatenate(outs)

    def swap(slot, step, other, source):
        head, sub = at.head_at(step), lax.rem(at.sub + other, 2)
        if source is None:
            block = at.head_at(at.heads - step) * 2 + sub
            view = win.at[head * 2 + sub], act.at[block]
        else:
            view = win.at[head * 2 + sub], act.at[source]
        return remote(*view, s_send.at[slot], s_recv.at[slot], head=head, sub=sub)

    peers = [(step, other) for step in range(1, at.heads) for other in range(2)] + [(0, 1)]
    for slot, (step, other) in enumerate(peers):
        if step == 0 and early:
            convolution_input([2])
        member = at.head_at(step) * 2 + lax.rem(at.sub + other, 2)
        win[member] = convolve(member)
        swap(slot, step, other, at.me).start()
    act[at.me] = convolve(at.me)

    weights[4].relay_over()
    weights[1].finish()
    for slot, (step, other) in enumerate(peers):
        swap(slot, step, other, at.me).wait_send()
        swap(slot, step, other, None).wait_recv()

    conv_sum = mix([act[block] for block in range(blocks)], fulls[1])
    window_at = HALO - rim
    slack = window_at % 8
    around = stream[pl.ds(pl.multiple_of(at.me * slab + window_at - slack, 8), span_rows + 8)]
    features = norm_rows(around[slack : slack + span_rows] + conv_sum)
    feat_out[...] = features[rim : rim + slab].astype(jnp.bfloat16)
    feat_store = load(feat_out, feat_hbm)
    first_frame = at.seq * rows + at.me * slab - rim
    frames = first_frame + lax.broadcasted_iota(jnp.int32, (span_rows, 1), 0)
    weights[5].relay_over()
    weights[2].finish()
    base_rows = jnp.dot(
        features.astype(jnp.bfloat16),
        fulls[2][...].reshape(-1, fulls[2].shape[2]),
        preferred_element_type=jnp.float32,
    )
    base_rows = norm_rows(jnp.where((frames >= 0) & (frames < used_ref[0]), base_rows, 0.0))
    for copy in late_loads:
        copy.wait()
    voc_rows = up_to(slab + parts, 8)
    vdepth = jnp.zeros((voc_rows, base_rows.shape[1]), jnp.float32)
    for k in range(2 * half_voc + 1):
        vdepth = vdepth + voc_kernel[k : k + 1] * base_rows[k : k + voc_rows]
    inner = norm_rows(vdepth).astype(jnp.bfloat16)
    weights[3].finish()
    hidden = jnp.dot(
        inner, fulls[3][...].reshape(-1, fulls[3].shape[2]), preferred_element_type=jnp.float32
    )
    hidden = (0.5 * hidden * (1.0 + lax.erf(hidden * math.sqrt(0.5)))).astype(jnp.bfloat16)
    weights[4].finish()
    refined = base_rows[half_voc : half_voc + voc_rows] + jnp.dot(
        hidden, fulls[4][...].reshape(-1, fulls[4].shape[2]), preferred_element_type=jnp.float32
    )
    head_input = norm_rows(refined).astype(jnp.bfloat16)
    weights[5].finish()

    bias_row = bias_ref[...].reshape(1, 2 * bin_count)
    biases = [
        bias_row[:, :padded_bins],
        jnp.concatenate(
            [bias_row[:, bin_count:], jnp.zeros((1, padded_bins - bin_count), jnp.float32)], axis=1
        ),
    ]

    def spectrum(index):
        parts_of = [
            fulls[5][block, pl.ds(index * padded_bins, padded_bins)] for block in range(blocks)
        ]
        inputs = [head_input]
        if width % 128 == 0:
            parts_of = [jnp.concatenate(parts_of, axis=1)]
        else:
            inputs = [head_input[:, block * width : (block + 1) * width] for block in range(blocks)]
        result = 0.0
        for one_input, part in zip(inputs, parts_of):
            result = result + lax.dot_general(
                one_input, part, (((1,), (1,)), ((), ())), preferred_element_type=jnp.float32
            )
        return result + biases[index]

    magnitude = jnp.minimum(jnp.exp(spectrum(0)), 100.0)
    sine, cosine = sine_cosine(spectrum(1))
    wave_frames = first_frame + half_voc + lax.broadcasted_iota(jnp.int32, (voc_rows, 1), 0)
    exists = (wave_frames >= 0) & (wave_frames < at.seqs * rows)
    magnitude = jnp.where(exists, magnitude, 0.0)
    waves = jnp.dot(
        (magnitude * cosine).astype(jnp.bfloat16),
        dft[pl.ds(0, padded_bins)],
        preferred_element_type=jnp.float32,
    ) + jnp.dot(
        (magnitude * sine).astype(jnp.bfloat16),
        dft[pl.ds(padded_bins, padded_bins)],
        preferred_element_type=jnp.float32,
    )
    there = jnp.where(exists, 1.0, 0.0)
    total_audio = jnp.zeros((slab, padded_hop), jnp.float32)
    energy = jnp.zeros((slab, padded_hop), jnp.float32)
    for quarter in range(parts):
        begin = parts - quarter
        total_audio = total_audio + waves[
            begin : begin + slab, quarter * padded_hop : (quarter + 1) * padded_hop
        ]
        energy = energy + there[begin : begin + slab] * env_ref[quarter : quarter + 1]
    total_audio = total_audio / energy
    for c in range(padded_hop // 128):
        audio[c] = total_audio[:, c * 128 : (c + 1) * 128]
    pairs = slab // 2
    group = 2 * HOP // 128
    low_lanes = lax.broadcasted_iota(jnp.int32, (1, 128), 1) < HOP % 128
    even = [audio[c, pl.ds(0, pairs, stride=2)] for c in range(padded_hop // 128)]
    odd = [
        pltpu.roll(audio[c, pl.ds(1, pairs, stride=2)], HOP % 128, 1)
        for c in range(padded_hop // 128)
    ]
    full_tiles = HOP // 128
    lines = even[:full_tiles] + [jnp.where(low_lanes, even[full_tiles], odd[0])]
    for c in range(full_tiles):
        lines.append(jnp.where(low_lanes, odd[c], odd[c + 1]))
    for index in range(group):
        wave_out[pl.ds(index, pairs, stride=group)] = lines[index]
    load(wave_out, wave_hbm).wait()
    feat_store.wait()


def hand_over(features, wave, features_out, wave_out, sems):
    copies = [
        pltpu.make_async_copy(features, features_out, sems.at[0]),
        pltpu.make_async_copy(wave, wave_out, sems.at[1]),
    ]
    for copy in copies:
        copy.start()
    for copy in copies:
        copy.wait()


def local(
    tokens,
    masked,
    used_frames,
    tables,
    mask_vec,
    attn_in,
    head_temp,
    attn_out,
    conv_in,
    conv_kernel,
    conv_out,
    voc_in,
    voc_kernel,
    voc_up,
    voc_down,
    voc_head,
    head_bias,
):
    groups, heads, seqs = (lax.axis_size(name) for name in ("groups", "head", "seq"))
    blocks = lax.axis_size(("head", "sub"))
    rows = tokens.shape[1]
    total = rows + 2 * HALO
    slab = rows // blocks
    columns = tables.shape[2]
    width = attn_in.shape[2]
    local_heads = head_temp.shape[0]
    bin_count = head_bias.shape[0] // 2
    fft_size = 2 * (bin_count - 1)
    parts = fft_size // HOP
    padded_bins = up_to(bin_count, 16)
    padded_hop = up_to(HOP, 128)
    rim = voc_kernel.shape[0] // 2 + parts // 2
    window_rows = up_to(slab + 2 * rim, 16)
    channels = conv_kernel.shape[1]
    dft, env = synthesis_constants(bin_count, fft_size, padded_bins, padded_hop)
    head_rows = voc_head.T
    owns = (attn_out, conv_out, voc_in, voc_up, voc_down, head_rows)
    vmem = pl.BlockSpec(memory_space=pltpu.VMEM)
    smem = pl.BlockSpec(memory_space=pltpu.SMEM)
    anywhere = pl.BlockSpec(memory_space=pl.ANY)
    dma = pltpu.SemaphoreType.DMA
    bf16, f32 = jnp.bfloat16, jnp.float32
    full_shapes = [(blocks,) + own.shape for own in owns[:5]] + [(blocks, 2 * padded_bins, width)]
    scratch = [pltpu.VMEM(shape, bf16) for shape in full_shapes]
    scratch += [
        pltpu.VMEM(tables.shape, bf16),
        pltpu.VMEM((1, attn_in.shape[1], 3 * width) if width % 128 == 0 else attn_in.shape, bf16),
        pltpu.VMEM(conv_in.shape, bf16),
        pltpu.VMEM(conv_kernel.shape, f32),
        pltpu.VMEM(voc_kernel.shape, f32),
        pltpu.VMEM(dft.shape, bf16),
        pltpu.VMEM(head_rows.shape, bf16),
        pltpu.VMEM((up_to(bin_count + padded_bins, 8), width), f32),
        pltpu.VMEM((2 * padded_bins, width), bf16),
        pltpu.VMEM((8, rows), f32),
        pltpu.VMEM((2, 8, 128), f32),
        pltpu.VMEM((blocks, total, columns), bf16),
        pltpu.VMEM((blocks, total, width), bf16),
        pltpu.VMEM((seqs, PIECES, 2, rows // PIECES, width), bf16),
        pltpu.VMEM((local_heads, total, width), bf16),
        pltpu.VMEM((local_heads, total, width), f32),
        pltpu.VMEM((local_heads, total, 128), f32),
        pltpu.VMEM((total, columns * blocks), f32),
        pltpu.VMEM((channels // 128, total + 64, 128), f32),
        pltpu.VMEM((blocks, window_rows, channels), bf16),
        pltpu.VMEM((blocks, window_rows, channels), bf16),
        pltpu.VMEM((padded_hop // 128, slab, 128), f32),
        pltpu.VMEM((slab, columns * blocks), bf16),
        pltpu.VMEM((slab * HOP // 128, 128), f32),
        dma((11,)),
        dma((2,)),
        dma((2,)),
        dma((PIECES + 1, 2 * heads)),
        dma((PIECES + 1, 2 * heads)),
        dma((3, 2 * heads)),
        dma((3, 2 * heads)),
        dma((seqs, PIECES)),
        dma((seqs, PIECES)),
        dma((seqs, PIECES)),
        dma((seqs, PIECES)),
        dma((blocks,)),
        dma((blocks,)),
    ]
    for _ in owns:
        scratch += weight_sems(heads, groups)
    sizes = (local_heads, width // local_heads, bin_count, padded_bins, fft_size)
    features, wave = pl.pallas_call(
        functools.partial(block_kernel, sizes),
        out_shape=[
            jax.ShapeDtypeStruct((slab, columns * blocks), bf16),
            jax.ShapeDtypeStruct((slab * HOP // 128, 128), f32),
        ],
        in_specs=[smem] * 2 + [vmem] * 5 + [anywhere] * (6 + WEIGHTS),
        out_specs=[anywhere, anywhere],
        scratch_shapes=scratch,
        compiler_params=pltpu.CompilerParams(
            collective_id=0, has_side_effects=True, vmem_limit_bytes=60 * 1024 * 1024
        ),
    )(
        used_frames, head_temp, tokens, masked, mask_vec, head_bias, env, tables, attn_in, conv_in, conv_kernel, voc_kernel, dft, *owns)
    features, wave = pl.pallas_call(
        hand_over,
        out_shape=[jax.ShapeDtypeStruct(out.shape, out.dtype) for out in (features, wave)],
        in_specs=[vmem] * 2,
        out_specs=[anywhere] * 2,
        scratch_shapes=[dma((2,))],
    )(features, wave)
    return features, wave.reshape(slab * HOP)


def solution(mesh):
    in_specs = (
        P(None, ("groups", "seq")),
        P(("groups", "seq")),
        P("groups"),
        P(None, None, ("head", "sub")),
        P(("head", "sub")),
        P(None, None, ("head", "sub")),
        P(("head", "sub")),
        P(("head", "sub"), None),
        P(None, None, ("head", "sub")),
        P(None, ("head", "sub")),
        P(("head", "sub"), None),
        P(("head", "sub"), None),
        P(),
        P(("head", "sub"), None),
        P(("head", "sub"), None),
        P(("head", "sub"), None),
        P(),
    )
    out_specs = (P(("groups", "seq", "head", "sub"), None), P(("groups", "seq", "head", "sub")))
    return jax.shard_map(local, mesh=mesh, in_specs=in_specs, out_specs=out_specs, check_vma=False)
```

```python
import functools
import math

import jax
import jax.numpy as jnp
import numpy as np
from jax import lax
from jax.experimental import pallas as pl
from jax.experimental.pallas import tpu as pltpu
from jax.sharding import PartitionSpec as P

HOP = 320


MESH = pl.DeviceIdType.MESH
HALO = 32


def remote(src, dst, send_sem, recv_sem, **where):
    return pltpu.make_async_remote_copy(
        src_ref=src,
        dst_ref=dst,
        send_sem=send_sem,
        recv_sem=recv_sem,
        device_id=where,
        device_id_type=MESH,
    )


class Place:
    def __init__(self):
        self.group, self.seq = lax.axis_index("groups"), lax.axis_index("seq")
        self.head, self.sub = lax.axis_index("head"), lax.axis_index("sub")
        self.groups, self.seqs = lax.axis_size("groups"), lax.axis_size("seq")
        self.heads = lax.axis_size("head")
        self.me = self.head * 2 + self.sub
        self.partner = 1 - self.sub

    def head_at(self, step):
        return lax.rem(self.head + step, self.heads)

    def group_at(self, step):
        return lax.rem(self.group + step, self.groups)


def enter(at):
    barrier = pltpu.get_barrier_semaphore()

    def greet(**where):
        pl.semaphore_signal(barrier, inc=1, device_id=where, device_id_type=MESH)

    for step in range(1, at.heads):
        greet(head=at.head_at(step))
        greet(head=at.head_at(step), sub=at.partner)
    for step in range(1, at.groups):
        greet(groups=at.group_at(step))
    greet(sub=at.partner)

    @pl.when(at.seq > 0)
    def _():
        greet(seq=at.seq - 1)

    @pl.when(at.seq < at.seqs - 1)
    def _():
        greet(seq=at.seq + 1)

    count = 2 * (at.heads - 1) + at.groups
    count = count + jnp.where(at.seq > 0, 1, 0) + jnp.where(at.seq < at.seqs - 1, 1, 0)
    return lambda: pl.semaphore_wait(barrier, count)


class Spread:
    def __init__(self, at, buffer, rows, sems):
        self.at, self.buffer, self.rows = at, buffer, rows
        self.send, self.recv = sems

    def part(self, block, head):
        begin, count = self.rows
        if callable(begin):
            begin = begin(head)
        return self.buffer.at[block, pl.ds(begin, count)]

    def cross(self, step):
        block = self.part(self.at.me, self.at.head_at(step))
        return remote(
            block, block, self.send.at[step], self.recv.at[step], head=self.at.head_at(step)
        )

    def aside(self, step):
        source = self.at.head_at(self.at.heads - step) * 2 + self.at.sub
        block = self.part(source, self.at.head)
        slot = self.at.heads + step
        return remote(block, block, self.send.at[slot], self.recv.at[slot], sub=self.at.partner)

    def start(self):
        for step in range(1, self.at.heads):
            self.cross(step).start()
        self.aside(0).start()

    def relay(self):
        for step in range(1, self.at.heads):
            self.cross(step).wait_recv()
            self.aside(step).start()

    def finish(self):
        for step in range(self.at.heads):
            if step > 0:
                self.cross(step).wait_send()
            self.aside(step).wait()


class Weight:
    def __init__(self, at, own, full, sems):
        self.at, self.own, self.full = at, own, full
        self.send, self.recv, self.local = sems
        self.length = own.shape[0] // at.groups

    def piece(self, block, part):
        start = pl.multiple_of(part * self.length, 16)
        return self.full.at[block, pl.ds(start, self.length)]

    def source(self, step):
        return self.at.head_at(self.at.heads - step) * 2 + self.at.sub

    def cross(self, step):
        start = pl.multiple_of(self.at.group * self.length, 16)
        return remote(
            self.own.at[pl.ds(start, self.length)],
            self.piece(self.at.me, self.at.group),
            self.send.at[step],
            self.recv.at[step],
            head=self.at.head_at(step),
        )

    def over(self, step, turn):
        block = self.piece(self.source(step), self.at.group)
        slot = self.at.heads + (step - 1) * self.at.groups + turn
        return remote(
            block, block, self.send.at[slot], self.recv.at[slot], groups=self.at.group_at(turn)
        )

    def aside(self, step, turn):
        part = self.at.group_at(self.at.groups - turn)
        block = self.piece(self.source(step), part)
        slot = self.at.heads * (1 + self.at.groups) + (step - 1) * self.at.groups + turn
        return remote(block, block, self.send.at[slot], self.recv.at[slot], sub=self.at.partner)

    def mine(self):
        return remote(
            self.own, self.full.at[self.at.me], self.send.at[0], self.recv.at[0], sub=self.at.partner
        )

    def kept(self):
        return pltpu.make_async_copy(self.own, self.full.at[self.at.me], self.local.at[0])

    def start(self):
        for step in range(1, self.at.heads):
            self.cross(step).start()
        self.mine().start()
        self.kept().start()

    def relay_cross(self):
        for step in range(1, self.at.heads):
            self.cross(step).wait_recv()
            for turn in range(1, self.at.groups):
                self.over(step, turn).start()
            self.aside(step, 0).start()

    def relay_over(self):
        for step in range(1, self.at.heads):
            for turn in range(1, self.at.groups):
                self.over(step, turn).wait_recv()
                self.aside(step, turn).start()

    def finish(self):
        self.mine().wait()
        self.kept().wait()
        for step in range(1, self.at.heads):
            self.cross(step).wait_send()
            for turn in range(1, self.at.groups):
                self.over(step, turn).wait_send()
            for turn in range(self.at.groups):
                self.aside(step, turn).wait()


def weight_sems(heads, groups):
    count = heads * (1 + 2 * groups)
    return [
        pltpu.SemaphoreType.DMA((count,)),
        pltpu.SemaphoreType.DMA((count,)),
        pltpu.SemaphoreType.DMA((1,)),
    ]


def norm_rows(values):
    average = jnp.mean(values, axis=-1, keepdims=True)
    centered = values - average
    return centered * lax.rsqrt(jnp.mean(centered * centered, axis=-1, keepdims=True) + 1e-05)


PARTS = 4
WEIGHTS = 6


def up_to(value, unit):
    return -(-value // unit) * unit


def synthesis_constants(bin_count, fft_size, padded_bins, padded_hop):
    parts = fft_size // HOP
    samples = np.arange(fft_size)
    window = 0.5 - 0.5 * np.cos(2.0 * np.pi / fft_size * samples)
    bins = np.arange(bin_count)[:, None]
    angle = 2.0 * np.pi / fft_size * (bins * samples[None, :] % fft_size)
    edge = (bins == 0) | (bins == bin_count - 1)
    factor = np.where(edge, 1.0, 2.0) / fft_size
    cosine = factor * np.cos(angle) * window
    sine = np.where(edge, 0.0, -factor * np.sin(angle) * window)

    def spread(table, rows, fill):
        result = np.full((rows, parts, padded_hop), fill)
        result[: table.shape[0], :, :HOP] = table.reshape(-1, parts, HOP)
        return result.reshape(rows, parts * padded_hop)

    tables = np.concatenate([spread(cosine, padded_bins, 0.0), spread(sine, padded_bins, 0.0)])
    energy = spread((window * window)[None, :], 1, 1.0).reshape(parts, padded_hop)
    energy = np.pad(energy, ((0, -parts % 8), (0, 0)), constant_values=1.0)
    return jnp.asarray(tables, jnp.bfloat16), jnp.asarray(energy, jnp.float32)


def sine_cosine(angle):
    turns = jnp.round(angle * (2.0 / math.pi))
    rest = angle - turns * 1.5703125
    rest = rest - turns * 4.837512969970703125e-4
    rest = rest - turns * 7.549789948768648e-8
    square = rest * rest
    sine = rest + rest * square * (
        -1.6666654611e-1 + square * (8.3321608736e-3 + square * -1.9515295891e-4)
    )
    cosine = 1.0 - 0.5 * square + square * square * (
        4.166664568298827e-2 + square * (-1.388731625493765e-3 + square * 2.443315711809948e-5)
    )
    quadrant = turns.astype(jnp.int32) & 3
    odd = (quadrant & 1) == 1
    sine, cosine = jnp.where(odd, cosine, sine), jnp.where(odd, sine, cosine)
    sine = jnp.where(quadrant >= 2, -sine, sine)
    cosine = jnp.where((quadrant == 1) | (quadrant == 2), -cosine, cosine)
    return sine, cosine


def mix(parts, full):
    if parts[0].shape[1] % 128 == 0:
        return jnp.dot(
            jnp.concatenate(parts, axis=1),
            full[...].reshape(-1, full.shape[2]),
            preferred_element_type=jnp.float32,
        )
    result = 0.0
    for block, part in enumerate(parts):
        result = result + jnp.dot(part, full[block], preferred_element_type=jnp.float32)
    return result


def block_kernel(sizes, *refs):
    (used_ref, temp_ref, tokens_ref, masked_ref, mask_ref, bias_ref, env_ref, tables_hbm, attn_hbm,
     conv_in_hbm, conv_kernel_hbm, voc_kernel_hbm, dft_hbm) = refs[:13]
    owns_hbm = list(refs[13 : 13 + WEIGHTS])
    feat_hbm, wave_hbm = refs[13 + WEIGHTS : 15 + WEIGHTS]
    refs = refs[15 + WEIGHTS :]
    fulls = refs[:WEIGHTS]
    (tables_ref, attn_ref, conv_in, conv_kernel, voc_kernel, dft, head_raw, head_wide, head_own,
     tok, tokh, emb, att, kvbuf, q_scr, acc, l_acc, stream, gated, win, act, audio,
     feat_out, wave_out) = refs[
        WEIGHTS : WEIGHTS + 24
    ]
    (load_sems, tok_send, tok_recv, e_send, e_recv, a_send, a_recv, r_send, r_recv, l_send,
     l_recv, s_send, s_recv) = refs[WEIGHTS + 24 : WEIGHTS + 37]
    wsems = refs[WEIGHTS + 37 :]
    local_heads, head_size, bin_count, padded_bins, fft_size = sizes
    at = Place()
    blocks, total, columns = emb.shape
    rows = total - 2 * HALO
    width = q_scr.shape[2]
    codes = tables_ref.shape[1]
    slab = rows // blocks
    padded_hop = env_ref.shape[1]
    parts = fft_size // HOP
    half_voc = voc_kernel.shape[0] // 2
    rim = half_voc + parts // 2
    taps = conv_kernel.shape[0]
    span_rows = win.shape[1]

    tokh[...] = jnp.zeros_like(tokh)
    wait_for_peers = enter(at)
    loads = []

    def load(source, target):
        copy = pltpu.make_async_copy(source, target, load_sems.at[len(loads)])
        copy.start()
        loads.append(copy)
        return copy

    tables_load = load(tables_hbm, tables_ref)
    joined = width % 128 == 0
    attn_loads = [
        load(attn_hbm.at[p], attn_ref.at[0, :, pl.ds(p * width, width)] if joined else attn_ref.at[p])
        for p in range(3)
    ]
    head_load = load(owns_hbm[5], head_raw)
    conv_loads = [load(conv_in_hbm, conv_in), load(conv_kernel_hbm, conv_kernel)]
    late_loads = [load(voc_kernel_hbm, voc_kernel), load(dft_hbm, dft)]

    first, last = at.seq == 0, at.seq == at.seqs - 1

    def tokens_up():
        return remote(tok.at[:, pl.ds(rows - 128, 128)], tokh.at[0],
                      tok_send.at[0], tok_recv.at[0], seq=at.seq + 1)

    def tokens_down():
        return remote(tok.at[:, pl.ds(0, 128)], tokh.at[1],
                      tok_send.at[1], tok_recv.at[1], seq=at.seq - 1)

    owns = owns_hbm[:5] + [head_own]
    weights = [Weight(at, owns[w], fulls[w], wsems[3 * w : 3 * w + 3]) for w in range(WEIGHTS)]

    ids = lax.broadcasted_iota(jnp.int32, (1, codes), 1).astype(jnp.float32)
    mask_row = mask_ref[...].astype(jnp.float32).reshape(1, columns)

    def embed(token_rows):
        result = token_rows[:, 3:4] * mask_row
        for level in range(3):
            hot = jnp.where(token_rows[:, level : level + 1] == ids, 1.0, 0.0).astype(jnp.bfloat16)
            result = result + jnp.dot(hot, tables_ref[level], preferred_element_type=jnp.float32)
        return result.astype(jnp.bfloat16)

    part_rows = rows // PARTS
    sizes_of = [1] * PARTS
    PIECES = len(sizes_of)
    spans = [
        (sum(sizes_of[:p]) * part_rows, sizes_of[p] * part_rows) for p in range(PIECES)
    ] + [(rows, 2 * HALO)]
    spreads = [
        Spread(at, emb, span, (e_send.at[p], e_recv.at[p])) for p, span in enumerate(spans)
    ]
    is_masked = masked_ref[...].reshape(1, rows)
    tok[0:2] = tokens_ref[0:2].astype(jnp.float32)
    tok[2:3] = jnp.where(is_masked == 1, -1, tokens_ref[2:3]).astype(jnp.float32)
    tok[3:4] = is_masked.astype(jnp.float32)
    tok[4:8] = jnp.zeros((4, rows), jnp.float32)
    token_columns = tok[...].T
    tables_load.wait()
    for p in range(PIECES):
        emb[at.me, pl.ds(*spans[p])] = embed(token_columns[spans[p][0] : sum(spans[p])])
        if p == 0:
            wait_for_peers()
        spreads[p].start()
        if p == 0:

            @pl.when(jnp.logical_not(last))
            def _():
                tokens_up().start()

            @pl.when(jnp.logical_not(first))
            def _():
                tokens_down().start()

    @pl.when(jnp.logical_not(last))
    def _():
        tokens_up().wait_send()

    @pl.when(jnp.logical_not(first))
    def _():
        tokens_up().wait_recv()
        tokens_down().wait_send()

    @pl.when(jnp.logical_not(last))
    def _():
        tokens_down().wait_recv()

    halo_tokens = jnp.concatenate(
        [tokh[0].T[128 - HALO :], tokh[1].T[:HALO]], axis=0
    )
    emb[at.me, pl.ds(rows, 2 * HALO)] = embed(halo_tokens)
    spreads[PIECES].start()
    for weight in weights[:5]:
        weight.start()
    lanes = lax.broadcasted_iota(jnp.int32, (1, width), 1)
    in_head = [
        (lanes >= h * head_size) & (lanes < (h + 1) * head_size) for h in range(local_heads)
    ]

    def unit(projected):
        squares = projected * projected
        scale = jnp.zeros_like(projected)
        for h in range(local_heads):
            total_h = jnp.sum(jnp.where(in_head[h], squares, 0.0), axis=-1, keepdims=True)
            scale = jnp.where(in_head[h], lax.rsqrt(total_h + 1e-06), scale)
        return projected * scale

    def part_start(part):
        return part * part_rows if isinstance(part, int) else pl.multiple_of(part * part_rows, part_rows)

    def send_up(block, step, part):
        view = kvbuf.at[block, pl.ds(part_start(part), part_rows)]
        return remote(view, view, r_send.at[step, part], r_recv.at[step, part], seq=at.seq + 1)

    def send_down(block, step, part):
        view = kvbuf.at[block, pl.ds(part_start(part), part_rows)]
        return remote(view, view, l_send.at[step, part], l_recv.at[step, part], seq=at.seq - 1)

    for copy in attn_loads:
        copy.wait()
    for p, spread in enumerate(spreads):
        spread.relay()
        spread.finish()
        begin, count = spread.rows
        whole = jnp.concatenate([emb[block, pl.ds(begin, count)] for block in range(blocks)], axis=1)
        normed = norm_rows(whole.astype(jnp.float32)).astype(jnp.bfloat16)
        projected = [
            jnp.dot(normed, attn_ref[part], preferred_element_type=jnp.float32)
            for part in range(attn_ref.shape[0])
        ]
        if joined:
            projected = [projected[0][:, part * width : (part + 1) * width] for part in range(3)]
        query = unit(projected[0])
        for h in range(local_heads):
            q_scr[h, pl.ds(begin, count)] = jnp.where(in_head[h], query, 0.0).astype(jnp.bfloat16)
        if p < PIECES:
            kvbuf[at.seq, pl.ds(begin, count)] = jnp.concatenate(
                [unit(projected[1]).astype(jnp.bfloat16), projected[2].astype(jnp.bfloat16)], axis=1
            )
            for part in range(begin // part_rows, (begin + count) // part_rows):

                @pl.when(jnp.logical_not(last))
                def _():
                    send_up(at.seq, 0, part).start()

                @pl.when(jnp.logical_not(first))
                def _():
                    send_down(at.seq, 0, part).start()

    head_load.wait()
    head_wide[pl.ds(0, 2 * bin_count)] = head_raw[...].astype(jnp.float32)
    tail_rows = head_wide.shape[0] - 2 * bin_count
    head_wide[pl.ds(2 * bin_count, tail_rows)] = jnp.zeros((tail_rows, width), jnp.float32)
    head_own[pl.ds(0, padded_bins)] = head_wide[pl.ds(0, padded_bins)].astype(jnp.bfloat16)
    head_own[pl.ds(padded_bins, padded_bins)] = head_wide[pl.ds(bin_count, padded_bins)].astype(
        jnp.bfloat16
    )

    weights[5].start()
    acc[...] = jnp.zeros_like(acc)
    l_acc[...] = jnp.zeros_like(l_acc)
    tile = total // 3
    keys = rows // 2

    def attend(block, pair):
        frame = block * rows + pair * keys + lax.broadcasted_iota(jnp.int32, (1, keys), 1)
        live = frame < used_ref[0]
        sharps = [temp_ref[h] * 1.4426950408889634 for h in range(local_heads)]
        biases = [jnp.where(live, -sharp, -1e30) for sharp in sharps]
        held = pl.ds(pl.multiple_of(pair * keys, keys) if not isinstance(pair, int) else pair * keys, keys)
        key, value = kvbuf[block, held, :width], kvbuf[block, held, width:]
        for index in range(3):
            span = pl.ds(index * tile, tile)
            scores = lax.dot_general(
                jnp.concatenate([q_scr[h, span] for h in range(local_heads)]),
                key,
                (((1,), (1,)), ((), ())),
                preferred_element_type=jnp.float32,
            )
            chances = []
            for h in range(local_heads):
                chance = jnp.exp2(scores[h * tile : (h + 1) * tile] * sharps[h] + biases[h])
                part = chance[:, :128]
                for lane in range(128, keys, 128):
                    part = part + chance[:, lane : lane + 128]
                l_acc[h, span] += part
                chances.append(chance.astype(jnp.bfloat16))
            summed = jnp.dot(
                jnp.concatenate(chances), value, preferred_element_type=jnp.float32
            )
            for h in range(local_heads):
                acc[h, span] += summed[h * tile : (h + 1) * tile]

    order = [("cross", 0), ("cross", 1), ("cross", 2), ("over", 0), ("cross", 3), ("over", 1),
             ("cross", 4), ("over", 2)]
    stages = [0, 1, 2, 2, 4, 4, 5, 5]

    def relays(stage, later=False):
        for (kind, index), own_stage in zip(order, stages):
            if own_stage == stage or (later and own_stage > stage):
                if kind == "cross":
                    weights[index].relay_cross()
                else:
                    weights[index].relay_over()

    pairs_of = 2
    turns = PARTS // pairs_of
    rounds = pairs_of * (at.seqs - 1)

    def exchange(index, carry):
        step, pair = index // pairs_of, lax.rem(index, pairs_of)
        before = jnp.maximum(index - 1, 0)
        old_step, old_pair = before // pairs_of, lax.rem(before, pairs_of)
        arriving = index < rounds

        for turn in range(turns):
            part = turns * pair + turn

            @pl.when(arriving & (step < at.seq))
            def _():
                block = at.seq - 1 - step
                send_up(block, step, part).wait_recv()

                @pl.when(jnp.logical_not(last))
                def _():
                    send_up(block, step + 1, part).start()

            @pl.when(arriving & (step < at.seqs - 1 - at.seq))
            def _():
                block = at.seq + 1 + step
                send_down(block, step, part).wait_recv()

                @pl.when(jnp.logical_not(first))
                def _():
                    send_down(block, step + 1, part).start()

            if turn == turns // 2 - 1:

                @pl.when((index > 0) & (old_step < at.seq))
                def _():
                    attend(at.seq - 1 - old_step, old_pair)

            if turn == turns - 1:

                @pl.when((index > 0) & (old_step < at.seqs - 1 - at.seq))
                def _():
                    attend(at.seq + 1 + old_step, old_pair)

        @pl.when((index > 0) & (index <= pairs_of))
        def _():
            attend(at.seq, index - 1)

        for stage in range(min(6, rounds)):

            @pl.when(index == stage)
            def _():
                relays(stage)

        return carry

    lax.fori_loop(0, rounds + 1, exchange, 0)
    if rounds < 6:
        relays(rounds, later=True)

    early = at.heads == 2
    near = rows // 2 + HALO
    far = rows - near

    def near_at(head):
        return pl.multiple_of(jnp.where(head == 0, far, 0), HALO) if early else 0

    def far_at(head):
        return pl.multiple_of(jnp.where(head == 0, 0, near), HALO) if early else near

    tiles = [(near_at, near), (rows, 2 * HALO), (far_at, far)]
    gathers = [
        Spread(at, att, span, (a_send.at[p], a_recv.at[p])) for p, span in enumerate(tiles)
    ]

    def attended(begin, count):
        span = pl.ds(begin, count)
        value = jnp.zeros((count, width), jnp.float32)
        for h in range(local_heads):
            mean = acc[h, span] / jnp.sum(l_acc[h, span], axis=-1, keepdims=True)
            value = jnp.where(in_head[h], mean, value)
        att[at.me, span] = value.astype(jnp.bfloat16)

    other = at.head_at(1)
    attended(near_at(other), near)
    if early:
        gathers[0].cross(1).start()
    attended(rows, 2 * HALO)
    attended(far_at(other), far)
    if early:
        gathers[1].start()
        gathers[0].aside(0).start()
        gathers[2].start()
    else:
        for gather in gathers:
            gather.start()
    weights[5].relay_cross()

    def drain(step, carry):
        @pl.when(jnp.logical_not(last) & (step <= at.seq))
        def _():
            for part in range(PARTS):
                send_up(at.seq - step, step, part).wait_send()

        @pl.when(jnp.logical_not(first) & (step <= at.seqs - 1 - at.seq))
        def _():
            for part in range(PARTS):
                send_down(at.seq + step, step, part).wait_send()

        return carry

    lax.fori_loop(0, at.seqs - 1, drain, 0)
    for copy in conv_loads:
        copy.wait()
    weights[0].finish()
    weights[3].relay_over()
    channel_tiles = gated.shape[0]
    gated[:, pl.ds(total, gated.shape[1] - total)] = jnp.zeros(
        (channel_tiles, gated.shape[1] - total, 128), jnp.float32
    )
    zero_first = jnp.where(first, 0.0, 1.0)
    zero_last = jnp.where(last, 0.0, 1.0)

    def convolution_input(pieces):
        for piece_at in pieces:
            gathers[piece_at].relay()
            gathers[piece_at].finish()
        spans = [
            pl.ds(tiles[p][0](at.head) if callable(tiles[p][0]) else tiles[p][0], tiles[p][1])
            for p in pieces
        ]

        def gathered(buffer, block):
            return jnp.concatenate([buffer[block, span] for span in spans])

        base = jnp.concatenate([gathered(emb, block) for block in range(blocks)], axis=1)
        summed = base.astype(jnp.float32) + mix(
            [gathered(att, block) for block in range(blocks)], fulls[0]
        )
        body_rows = tiles[pieces[0]][1]
        targets = [(0, body_rows, pl.multiple_of(spans[0].start + HALO, HALO))]
        if len(pieces) > 1:
            summed = jnp.concatenate(
                [
                    summed[:body_rows],
                    summed[body_rows : body_rows + HALO] * zero_first,
                    summed[body_rows + HALO :] * zero_last,
                ]
            )
            targets += [(body_rows, HALO, 0), (body_rows + HALO, HALO, total - HALO)]
        normed = norm_rows(summed).astype(jnp.bfloat16)
        value = jnp.dot(normed, conv_in[0], preferred_element_type=jnp.float32)
        signal = jnp.dot(normed, conv_in[1], preferred_element_type=jnp.float32)
        gate = (value * jax.nn.sigmoid(signal)).astype(jnp.bfloat16).astype(jnp.float32)
        for low, length, start in targets:
            target = pl.ds(start, length)
            stream[target] = summed[low : low + length]
            for c in range(channel_tiles):
                gated[c, target] = gate[low : low + length, c * 128 : (c + 1) * 128]

    convolution_input([0, 1])
    if not early:
        convolution_input([2])
    first_tap = HALO - rim - taps // 2
    lead = first_tap % 8
    chunk = span_rows // 2

    def convolve(member):
        base_row = pl.multiple_of(member * slab + first_tap - lead, 8)
        outs = []
        for part in range(2):
            line = []
            for c in range(channel_tiles):
                kernel = conv_kernel[:, c * 128 : (c + 1) * 128]
                reach = up_to(chunk + taps + lead, 8)
                source = gated[c, pl.ds(base_row + part * chunk, reach)]
                result = jnp.zeros((chunk, 128), jnp.float32)
                for turn in range(8):
                    shifted = source[turn:] if turn else source
                    for k in range(taps):
                        offset = lead + k - turn
                        if offset % 8 == 0 and offset >= 0:
                            result = result + kernel[k : k + 1] * shifted[offset : offset + chunk]
                line.append((result * jax.nn.sigmoid(result)).astype(jnp.bfloat16))
            outs.append(jnp.concatenate(line, axis=1))
        return jnp.concatenate(outs)

    def swap(slot, step, other, source):
        head, sub = at.head_at(step), lax.rem(at.sub + other, 2)
        if source is None:
            block = at.head_at(at.heads - step) * 2 + sub
            view = win.at[head * 2 + sub], act.at[block]
        else:
            view = win.at[head * 2 + sub], act.at[source]
        return remote(*view, s_send.at[slot], s_recv.at[slot], head=head, sub=sub)

    peers = [(step, other) for step in range(1, at.heads) for other in range(2)] + [(0, 1)]
    for slot, (step, other) in enumerate(peers):
        if step == 0 and early:
            convolution_input([2])
        member = at.head_at(step) * 2 + lax.rem(at.sub + other, 2)
        win[member] = convolve(member)
        swap(slot, step, other, at.me).start()
    act[at.me] = convolve(at.me)

    weights[4].relay_over()
    weights[1].finish()
    for slot, (step, other) in enumerate(peers):
        swap(slot, step, other, at.me).wait_send()
        swap(slot, step, other, None).wait_recv()

    conv_sum = mix([act[block] for block in range(blocks)], fulls[1])
    window_at = HALO - rim
    slack = window_at % 8
    around = stream[pl.ds(pl.multiple_of(at.me * slab + window_at - slack, 8), span_rows + 8)]
    features = norm_rows(around[slack : slack + span_rows] + conv_sum)
    feat_out[...] = features[rim : rim + slab].astype(jnp.bfloat16)
    feat_store = load(feat_out, feat_hbm)
    first_frame = at.seq * rows + at.me * slab - rim
    frames = first_frame + lax.broadcasted_iota(jnp.int32, (span_rows, 1), 0)
    weights[5].relay_over()
    weights[2].finish()
    base_rows = jnp.dot(
        features.astype(jnp.bfloat16),
        fulls[2][...].reshape(-1, fulls[2].shape[2]),
        preferred_element_type=jnp.float32,
    )
    base_rows = norm_rows(jnp.where((frames >= 0) & (frames < used_ref[0]), base_rows, 0.0))
    for copy in late_loads:
        copy.wait()
    voc_rows = up_to(slab + parts, 8)
    vdepth = jnp.zeros((voc_rows, base_rows.shape[1]), jnp.float32)
    for k in range(2 * half_voc + 1):
        vdepth = vdepth + voc_kernel[k : k + 1] * base_rows[k : k + voc_rows]
    inner = norm_rows(vdepth).astype(jnp.bfloat16)
    weights[3].finish()
    hidden = jnp.dot(
        inner, fulls[3][...].reshape(-1, fulls[3].shape[2]), preferred_element_type=jnp.float32
    )
    hidden = (0.5 * hidden * (1.0 + lax.erf(hidden * math.sqrt(0.5)))).astype(jnp.bfloat16)
    weights[4].finish()
    refined = base_rows[half_voc : half_voc + voc_rows] + jnp.dot(
        hidden, fulls[4][...].reshape(-1, fulls[4].shape[2]), preferred_element_type=jnp.float32
    )
    head_input = norm_rows(refined).astype(jnp.bfloat16)
    weights[5].finish()

    bias_row = bias_ref[...].reshape(1, 2 * bin_count)
    biases = [
        bias_row[:, :padded_bins],
        jnp.concatenate(
            [bias_row[:, bin_count:], jnp.zeros((1, padded_bins - bin_count), jnp.float32)], axis=1
        ),
    ]

    def spectrum(index):
        parts_of = [
            fulls[5][block, pl.ds(index * padded_bins, padded_bins)] for block in range(blocks)
        ]
        inputs = [head_input]
        if width % 128 == 0:
            parts_of = [jnp.concatenate(parts_of, axis=1)]
        else:
            inputs = [head_input[:, block * width : (block + 1) * width] for block in range(blocks)]
        result = 0.0
        for one_input, part in zip(inputs, parts_of):
            result = result + lax.dot_general(
                one_input, part, (((1,), (1,)), ((), ())), preferred_element_type=jnp.float32
            )
        return result + biases[index]

    magnitude = jnp.minimum(jnp.exp(spectrum(0)), 100.0)
    sine, cosine = sine_cosine(spectrum(1))
    wave_frames = first_frame + half_voc + lax.broadcasted_iota(jnp.int32, (voc_rows, 1), 0)
    exists = (wave_frames >= 0) & (wave_frames < at.seqs * rows)
    magnitude = jnp.where(exists, magnitude, 0.0)
    waves = jnp.dot(
        (magnitude * cosine).astype(jnp.bfloat16),
        dft[pl.ds(0, padded_bins)],
        preferred_element_type=jnp.float32,
    ) + jnp.dot(
        (magnitude * sine).astype(jnp.bfloat16),
        dft[pl.ds(padded_bins, padded_bins)],
        preferred_element_type=jnp.float32,
    )
    there = jnp.where(exists, 1.0, 0.0)
    total_audio = jnp.zeros((slab, padded_hop), jnp.float32)
    energy = jnp.zeros((slab, padded_hop), jnp.float32)
    for quarter in range(parts):
        begin = parts - quarter
        total_audio = total_audio + waves[
            begin : begin + slab, quarter * padded_hop : (quarter + 1) * padded_hop
        ]
        energy = energy + there[begin : begin + slab] * env_ref[quarter : quarter + 1]
    total_audio = total_audio / energy
    for c in range(padded_hop // 128):
        audio[c] = total_audio[:, c * 128 : (c + 1) * 128]
    pairs = slab // 2
    group = 2 * HOP // 128
    low_lanes = lax.broadcasted_iota(jnp.int32, (1, 128), 1) < HOP % 128
    even = [audio[c, pl.ds(0, pairs, stride=2)] for c in range(padded_hop // 128)]
    odd = [
        pltpu.roll(audio[c, pl.ds(1, pairs, stride=2)], HOP % 128, 1)
        for c in range(padded_hop // 128)
    ]
    full_tiles = HOP // 128
    lines = even[:full_tiles] + [jnp.where(low_lanes, even[full_tiles], odd[0])]
    for c in range(full_tiles):
        lines.append(jnp.where(low_lanes, odd[c], odd[c + 1]))
    for index in range(group):
        wave_out[pl.ds(index, pairs, stride=group)] = lines[index]
    load(wave_out, wave_hbm).wait()
    feat_store.wait()


def hand_over(features, wave, features_out, wave_out, sems):
    copies = [
        pltpu.make_async_copy(features, features_out, sems.at[0]),
        pltpu.make_async_copy(wave, wave_out, sems.at[1]),
    ]
    for copy in copies:
        copy.start()
    for copy in copies:
        copy.wait()


def local(
    tokens,
    masked,
    used_frames,
    tables,
    mask_vec,
    attn_in,
    head_temp,
    attn_out,
    conv_in,
    conv_kernel,
    conv_out,
    voc_in,
    voc_kernel,
    voc_up,
    voc_down,
    voc_head,
    head_bias,
):
    groups, heads, seqs = (lax.axis_size(name) for name in ("groups", "head", "seq"))
    blocks = lax.axis_size(("head", "sub"))
    rows = tokens.shape[1]
    total = rows + 2 * HALO
    slab = rows // blocks
    columns = tables.shape[2]
    width = attn_in.shape[2]
    local_heads = head_temp.shape[0]
    bin_count = head_bias.shape[0] // 2
    fft_size = 2 * (bin_count - 1)
    parts = fft_size // HOP
    padded_bins = up_to(bin_count, 16)
    padded_hop = up_to(HOP, 128)
    rim = voc_kernel.shape[0] // 2 + parts // 2
    window_rows = up_to(slab + 2 * rim, 16)
    channels = conv_kernel.shape[1]
    dft, env = synthesis_constants(bin_count, fft_size, padded_bins, padded_hop)
    head_rows = voc_head.T
    owns = (attn_out, conv_out, voc_in, voc_up, voc_down, head_rows)
    vmem = pl.BlockSpec(memory_space=pltpu.VMEM)
    smem = pl.BlockSpec(memory_space=pltpu.SMEM)
    anywhere = pl.BlockSpec(memory_space=pl.ANY)
    dma = pltpu.SemaphoreType.DMA
    bf16, f32 = jnp.bfloat16, jnp.float32
    full_shapes = [(blocks,) + own.shape for own in owns[:5]] + [(blocks, 2 * padded_bins, width)]
    scratch = [pltpu.VMEM(shape, bf16) for shape in full_shapes]
    scratch += [
        pltpu.VMEM(tables.shape, bf16),
        pltpu.VMEM((1, attn_in.shape[1], 3 * width) if width % 128 == 0 else attn_in.shape, bf16),
        pltpu.VMEM(conv_in.shape, bf16),
        pltpu.VMEM(conv_kernel.shape, f32),
        pltpu.VMEM(voc_kernel.shape, f32),
        pltpu.VMEM(dft.shape, bf16),
        pltpu.VMEM(head_rows.shape, bf16),
        pltpu.VMEM((up_to(bin_count + padded_bins, 8), width), f32),
        pltpu.VMEM((2 * padded_bins, width), bf16),
        pltpu.VMEM((8, rows), f32),
        pltpu.VMEM((2, 8, 128), f32),
        pltpu.VMEM((blocks, total, columns), bf16),
        pltpu.VMEM((blocks, total, width), bf16),
        pltpu.VMEM((seqs, rows, 2 * width), bf16),
        pltpu.VMEM((local_heads, total, width), bf16),
        pltpu.VMEM((local_heads, total, width), f32),
        pltpu.VMEM((local_heads, total, 128), f32),
        pltpu.VMEM((total, columns * blocks), f32),
        pltpu.VMEM((channels // 128, total + 64, 128), f32),
        pltpu.VMEM((blocks, window_rows, channels), bf16),
        pltpu.VMEM((blocks, window_rows, channels), bf16),
        pltpu.VMEM((padded_hop // 128, slab, 128), f32),
        pltpu.VMEM((slab, columns * blocks), bf16),
        pltpu.VMEM((slab * HOP // 128, 128), f32),
        dma((11,)),
        dma((2,)),
        dma((2,)),
        dma((PARTS + 1, 2 * heads)),
        dma((PARTS + 1, 2 * heads)),
        dma((3, 2 * heads)),
        dma((3, 2 * heads)),
        dma((seqs, PARTS)),
        dma((seqs, PARTS)),
        dma((seqs, PARTS)),
        dma((seqs, PARTS)),
        dma((blocks,)),
        dma((blocks,)),
    ]
    for _ in owns:
        scratch += weight_sems(heads, groups)
    sizes = (local_heads, width // local_heads, bin_count, padded_bins, fft_size)
    features, wave = pl.pallas_call(
        functools.partial(block_kernel, sizes),
        out_shape=[
            jax.ShapeDtypeStruct((slab, columns * blocks), bf16),
            jax.ShapeDtypeStruct((slab * HOP // 128, 128), f32),
        ],
        in_specs=[smem] * 2 + [vmem] * 5 + [anywhere] * (6 + WEIGHTS),
        out_specs=[anywhere, anywhere],
        scratch_shapes=scratch,
        compiler_params=pltpu.CompilerParams(
            collective_id=0, has_side_effects=True, vmem_limit_bytes=60 * 1024 * 1024
        ),
    )(
        used_frames, head_temp, tokens, masked, mask_vec, head_bias, env, tables, attn_in, conv_in, conv_kernel, voc_kernel, dft, *owns)
    features, wave = pl.pallas_call(
        hand_over,
        out_shape=[jax.ShapeDtypeStruct(out.shape, out.dtype) for out in (features, wave)],
        in_specs=[vmem] * 2,
        out_specs=[anywhere] * 2,
        scratch_shapes=[dma((2,))],
    )(features, wave)
    return features, wave.reshape(slab * HOP)


def solution(mesh):
    in_specs = (
        P(None, ("groups", "seq")),
        P(("groups", "seq")),
        P("groups"),
        P(None, None, ("head", "sub")),
        P(("head", "sub")),
        P(None, None, ("head", "sub")),
        P(("head", "sub")),
        P(("head", "sub"), None),
        P(None, None, ("head", "sub")),
        P(None, ("head", "sub")),
        P(("head", "sub"), None),
        P(("head", "sub"), None),
        P(),
        P(("head", "sub"), None),
        P(("head", "sub"), None),
        P(("head", "sub"), None),
        P(),
    )
    out_specs = (P(("groups", "seq", "head", "sub"), None), P(("groups", "seq", "head", "sub")))
    return jax.shard_map(local, mesh=mesh, in_specs=in_specs, out_specs=out_specs, check_vma=False)
```

```python
import functools
import math

import jax
import jax.numpy as jnp
import numpy as np
from jax import lax
from jax.experimental import pallas as pl
from jax.experimental.pallas import tpu as pltpu
from jax.sharding import PartitionSpec as P

HOP = 320


MESH = pl.DeviceIdType.MESH
HALO = 32


def remote(src, dst, send_sem, recv_sem, **where):
    return pltpu.make_async_remote_copy(
        src_ref=src,
        dst_ref=dst,
        send_sem=send_sem,
        recv_sem=recv_sem,
        device_id=where,
        device_id_type=MESH,
    )


class Place:
    def __init__(self):
        self.group, self.seq = lax.axis_index("groups"), lax.axis_index("seq")
        self.head, self.sub = lax.axis_index("head"), lax.axis_index("sub")
        self.groups, self.seqs = lax.axis_size("groups"), lax.axis_size("seq")
        self.heads = lax.axis_size("head")
        self.me = self.head * 2 + self.sub
        self.partner = 1 - self.sub

    def head_at(self, step):
        return lax.rem(self.head + step, self.heads)

    def group_at(self, step):
        return lax.rem(self.group + step, self.groups)


def enter(at):
    barrier = pltpu.get_barrier_semaphore()

    def greet(**where):
        pl.semaphore_signal(barrier, inc=1, device_id=where, device_id_type=MESH)

    for step in range(1, at.heads):
        greet(head=at.head_at(step))
        greet(head=at.head_at(step), sub=at.partner)
    for step in range(1, at.groups):
        greet(groups=at.group_at(step))
    greet(sub=at.partner)

    @pl.when(at.seq > 0)
    def _():
        greet(seq=at.seq - 1)

    @pl.when(at.seq < at.seqs - 1)
    def _():
        greet(seq=at.seq + 1)

    count = 2 * (at.heads - 1) + at.groups
    count = count + jnp.where(at.seq > 0, 1, 0) + jnp.where(at.seq < at.seqs - 1, 1, 0)
    return lambda: pl.semaphore_wait(barrier, count)


class Spread:
    def __init__(self, at, buffer, rows, sems):
        self.at, self.buffer, self.rows = at, buffer, rows
        self.send, self.recv = sems

    def part(self, block, head):
        begin, count = self.rows
        if callable(begin):
            begin = begin(head)
        return self.buffer.at[block, pl.ds(begin, count)]

    def cross(self, step):
        block = self.part(self.at.me, self.at.head_at(step))
        return remote(
            block, block, self.send.at[step], self.recv.at[step], head=self.at.head_at(step)
        )

    def aside(self, step):
        source = self.at.head_at(self.at.heads - step) * 2 + self.at.sub
        block = self.part(source, self.at.head)
        slot = self.at.heads + step
        return remote(block, block, self.send.at[slot], self.recv.at[slot], sub=self.at.partner)

    def start(self):
        for step in range(1, self.at.heads):
            self.cross(step).start()
        self.aside(0).start()

    def relay(self):
        for step in range(1, self.at.heads):
            self.cross(step).wait_recv()
            self.aside(step).start()

    def finish(self):
        for step in range(self.at.heads):
            if step > 0:
                self.cross(step).wait_send()
            self.aside(step).wait()


class Weight:
    def __init__(self, at, own, full, sems):
        self.at, self.own, self.full = at, own, full
        self.send, self.recv, self.local = sems
        self.length = own.shape[0] // at.groups

    def piece(self, block, part):
        start = pl.multiple_of(part * self.length, 16)
        return self.full.at[block, pl.ds(start, self.length)]

    def source(self, step):
        return self.at.head_at(self.at.heads - step) * 2 + self.at.sub

    def cross(self, step):
        start = pl.multiple_of(self.at.group * self.length, 16)
        return remote(
            self.own.at[pl.ds(start, self.length)],
            self.piece(self.at.me, self.at.group),
            self.send.at[step],
            self.recv.at[step],
            head=self.at.head_at(step),
        )

    def over(self, step, turn):
        block = self.piece(self.source(step), self.at.group)
        slot = self.at.heads + (step - 1) * self.at.groups + turn
        return remote(
            block, block, self.send.at[slot], self.recv.at[slot], groups=self.at.group_at(turn)
        )

    def aside(self, step, turn):
        part = self.at.group_at(self.at.groups - turn)
        block = self.piece(self.source(step), part)
        slot = self.at.heads * (1 + self.at.groups) + (step - 1) * self.at.groups + turn
        return remote(block, block, self.send.at[slot], self.recv.at[slot], sub=self.at.partner)

    def mine(self):
        return remote(
            self.own, self.full.at[self.at.me], self.send.at[0], self.recv.at[0], sub=self.at.partner
        )

    def kept(self):
        return pltpu.make_async_copy(self.own, self.full.at[self.at.me], self.local.at[0])

    def start(self):
        for step in range(1, self.at.heads):
            self.cross(step).start()
        self.mine().start()
        self.kept().start()

    def relay_cross(self):
        for step in range(1, self.at.heads):
            self.cross(step).wait_recv()
            for turn in range(1, self.at.groups):
                self.over(step, turn).start()
            self.aside(step, 0).start()

    def relay_over(self):
        for step in range(1, self.at.heads):
            for turn in range(1, self.at.groups):
                self.over(step, turn).wait_recv()
                self.aside(step, turn).start()

    def finish(self):
        self.mine().wait()
        self.kept().wait()
        for step in range(1, self.at.heads):
            self.cross(step).wait_send()
            for turn in range(1, self.at.groups):
                self.over(step, turn).wait_send()
            for turn in range(self.at.groups):
                self.aside(step, turn).wait()


def weight_sems(heads, groups):
    count = heads * (1 + 2 * groups)
    return [
        pltpu.SemaphoreType.DMA((count,)),
        pltpu.SemaphoreType.DMA((count,)),
        pltpu.SemaphoreType.DMA((1,)),
    ]


def norm_rows(values):
    average = jnp.mean(values, axis=-1, keepdims=True)
    centered = values - average
    return centered * lax.rsqrt(jnp.mean(centered * centered, axis=-1, keepdims=True) + 1e-05)


PARTS = 4
WEIGHTS = 6


def up_to(value, unit):
    return -(-value // unit) * unit


def synthesis_constants(bin_count, fft_size, padded_bins, padded_hop):
    parts = fft_size // HOP
    samples = np.arange(fft_size)
    window = 0.5 - 0.5 * np.cos(2.0 * np.pi / fft_size * samples)
    bins = np.arange(bin_count)[:, None]
    angle = 2.0 * np.pi / fft_size * (bins * samples[None, :] % fft_size)
    edge = (bins == 0) | (bins == bin_count - 1)
    factor = np.where(edge, 1.0, 2.0) / fft_size
    cosine = factor * np.cos(angle) * window
    sine = np.where(edge, 0.0, -factor * np.sin(angle) * window)

    def spread(table, rows, fill):
        result = np.full((rows, parts, padded_hop), fill)
        result[: table.shape[0], :, :HOP] = table.reshape(-1, parts, HOP)
        return result.reshape(rows, parts * padded_hop)

    tables = np.concatenate([spread(cosine, padded_bins, 0.0), spread(sine, padded_bins, 0.0)])
    energy = spread((window * window)[None, :], 1, 1.0).reshape(parts, padded_hop)
    energy = np.pad(energy, ((0, -parts % 8), (0, 0)), constant_values=1.0)
    return jnp.asarray(tables, jnp.bfloat16), jnp.asarray(energy, jnp.float32)


def sine_cosine(angle):
    turns = jnp.round(angle * (2.0 / math.pi))
    rest = angle - turns * 1.5703125
    rest = rest - turns * 4.837512969970703125e-4
    rest = rest - turns * 7.549789948768648e-8
    square = rest * rest
    sine = rest + rest * square * (
        -1.6666654611e-1 + square * (8.3321608736e-3 + square * -1.9515295891e-4)
    )
    cosine = 1.0 - 0.5 * square + square * square * (
        4.166664568298827e-2 + square * (-1.388731625493765e-3 + square * 2.443315711809948e-5)
    )
    quadrant = turns.astype(jnp.int32) & 3
    odd = (quadrant & 1) == 1
    sine, cosine = jnp.where(odd, cosine, sine), jnp.where(odd, sine, cosine)
    sine = jnp.where(quadrant >= 2, -sine, sine)
    cosine = jnp.where((quadrant == 1) | (quadrant == 2), -cosine, cosine)
    return sine, cosine


def mix(parts, full):
    if parts[0].shape[1] % 128 == 0:
        return jnp.dot(
            jnp.concatenate(parts, axis=1),
            full[...].reshape(-1, full.shape[2]),
            preferred_element_type=jnp.float32,
        )
    result = 0.0
    for block, part in enumerate(parts):
        result = result + jnp.dot(part, full[block], preferred_element_type=jnp.float32)
    return result


def block_kernel(sizes, *refs):
    (used_ref, temp_ref, tokens_ref, masked_ref, mask_ref, bias_ref, env_ref, tables_hbm, attn_hbm,
     conv_in_hbm, conv_kernel_hbm, voc_kernel_hbm, dft_hbm) = refs[:13]
    owns_hbm = list(refs[13 : 13 + WEIGHTS])
    feat_hbm, wave_hbm = refs[13 + WEIGHTS : 15 + WEIGHTS]
    refs = refs[15 + WEIGHTS :]
    fulls = refs[:WEIGHTS]
    (tables_ref, attn_ref, conv_in, conv_kernel, voc_kernel, dft, head_raw, head_wide, head_own,
     tok, tokh, emb, att, kvbuf, q_scr, acc, l_acc, stream, gated, win, act, audio,
     feat_out, wave_out) = refs[
        WEIGHTS : WEIGHTS + 24
    ]
    (load_sems, tok_send, tok_recv, e_send, e_recv, a_send, a_recv, r_send, r_recv, l_send,
     l_recv, s_send, s_recv) = refs[WEIGHTS + 24 : WEIGHTS + 37]
    wsems = refs[WEIGHTS + 37 :]
    local_heads, head_size, bin_count, padded_bins, fft_size = sizes
    at = Place()
    blocks, total, columns = emb.shape
    rows = total - 2 * HALO
    width = q_scr.shape[2]
    codes = tables_ref.shape[1]
    slab = rows // blocks
    padded_hop = env_ref.shape[1]
    parts = fft_size // HOP
    half_voc = voc_kernel.shape[0] // 2
    rim = half_voc + parts // 2
    taps = conv_kernel.shape[0]
    span_rows = win.shape[1]

    tokh[...] = jnp.zeros_like(tokh)
    wait_for_peers = enter(at)
    loads = []

    def load(source, target):
        copy = pltpu.make_async_copy(source, target, load_sems.at[len(loads)])
        copy.start()
        loads.append(copy)
        return copy

    tables_load = load(tables_hbm, tables_ref)
    joined = width % 128 == 0
    attn_loads = [
        load(attn_hbm.at[p], attn_ref.at[0, :, pl.ds(p * width, width)] if joined else attn_ref.at[p])
        for p in range(3)
    ]
    head_load = load(owns_hbm[5], head_raw)
    conv_loads = [load(conv_in_hbm, conv_in), load(conv_kernel_hbm, conv_kernel)]
    late_loads = [load(voc_kernel_hbm, voc_kernel), load(dft_hbm, dft)]

    first, last = at.seq == 0, at.seq == at.seqs - 1

    def tokens_up():
        return remote(tok.at[:, pl.ds(rows - 128, 128)], tokh.at[0],
                      tok_send.at[0], tok_recv.at[0], seq=at.seq + 1)

    def tokens_down():
        return remote(tok.at[:, pl.ds(0, 128)], tokh.at[1],
                      tok_send.at[1], tok_recv.at[1], seq=at.seq - 1)

    owns = owns_hbm[:5] + [head_own]
    weights = [Weight(at, owns[w], fulls[w], wsems[3 * w : 3 * w + 3]) for w in range(WEIGHTS)]

    ids = lax.broadcasted_iota(jnp.int32, (1, codes), 1).astype(jnp.float32)
    mask_row = mask_ref[...].astype(jnp.float32).reshape(1, columns)

    def embed(token_rows):
        result = token_rows[:, 3:4] * mask_row
        for level in range(3):
            hot = jnp.where(token_rows[:, level : level + 1] == ids, 1.0, 0.0).astype(jnp.bfloat16)
            result = result + jnp.dot(hot, tables_ref[level], preferred_element_type=jnp.float32)
        return result.astype(jnp.bfloat16)

    part_rows = rows // PARTS
    sizes_of = [1] * PARTS
    PIECES = len(sizes_of)
    spans = [
        (sum(sizes_of[:p]) * part_rows, sizes_of[p] * part_rows) for p in range(PIECES)
    ] + [(rows, 2 * HALO)]
    spreads = [
        Spread(at, emb, span, (e_send.at[p], e_recv.at[p])) for p, span in enumerate(spans)
    ]
    is_masked = masked_ref[...].reshape(1, rows)
    tok[0:2] = tokens_ref[0:2].astype(jnp.float32)
    tok[2:3] = jnp.where(is_masked == 1, -1, tokens_ref[2:3]).astype(jnp.float32)
    tok[3:4] = is_masked.astype(jnp.float32)
    tok[4:8] = jnp.zeros((4, rows), jnp.float32)
    token_columns = tok[...].T
    tables_load.wait()
    for p in range(PIECES):
        emb[at.me, pl.ds(*spans[p])] = embed(token_columns[spans[p][0] : sum(spans[p])])
        if p == 0:
            wait_for_peers()
        spreads[p].start()
        if p == 0:

            @pl.when(jnp.logical_not(last))
            def _():
                tokens_up().start()

            @pl.when(jnp.logical_not(first))
            def _():
                tokens_down().start()

    @pl.when(jnp.logical_not(last))
    def _():
        tokens_up().wait_send()

    @pl.when(jnp.logical_not(first))
    def _():
        tokens_up().wait_recv()
        tokens_down().wait_send()

    @pl.when(jnp.logical_not(last))
    def _():
        tokens_down().wait_recv()

    halo_tokens = jnp.concatenate(
        [tokh[0].T[128 - HALO :], tokh[1].T[:HALO]], axis=0
    )
    emb[at.me, pl.ds(rows, 2 * HALO)] = embed(halo_tokens)
    spreads[PIECES].start()
    for weight in weights[:5]:
        weight.start()
    lanes = lax.broadcasted_iota(jnp.int32, (1, width), 1)
    in_head = [
        (lanes >= h * head_size) & (lanes < (h + 1) * head_size) for h in range(local_heads)
    ]

    def unit(projected):
        squares = projected * projected
        scale = jnp.zeros_like(projected)
        for h in range(local_heads):
            total_h = jnp.sum(jnp.where(in_head[h], squares, 0.0), axis=-1, keepdims=True)
            scale = jnp.where(in_head[h], lax.rsqrt(total_h + 1e-06), scale)
        return projected * scale

    def part_start(part):
        return part * part_rows if isinstance(part, int) else pl.multiple_of(part * part_rows, part_rows)

    def send_up(block, step, part):
        view = kvbuf.at[block, pl.ds(part_start(part), part_rows)]
        return remote(view, view, r_send.at[step, part], r_recv.at[step, part], seq=at.seq + 1)

    def send_down(block, step, part):
        view = kvbuf.at[block, pl.ds(part_start(part), part_rows)]
        return remote(view, view, l_send.at[step, part], l_recv.at[step, part], seq=at.seq - 1)

    for copy in attn_loads:
        copy.wait()
    for p, spread in enumerate(spreads):
        spread.relay()
        spread.finish()
        begin, count = spread.rows
        whole = jnp.concatenate([emb[block, pl.ds(begin, count)] for block in range(blocks)], axis=1)
        normed = norm_rows(whole.astype(jnp.float32)).astype(jnp.bfloat16)
        projected = [
            jnp.dot(normed, attn_ref[part], preferred_element_type=jnp.float32)
            for part in range(attn_ref.shape[0])
        ]
        if joined:
            projected = [projected[0][:, part * width : (part + 1) * width] for part in range(3)]
        query = unit(projected[0])
        for h in range(local_heads):
            q_scr[h, pl.ds(begin, count)] = jnp.where(in_head[h], query, 0.0).astype(jnp.bfloat16)
        if p < PIECES:
            kvbuf[at.seq, pl.ds(begin, count)] = jnp.concatenate(
                [unit(projected[1]).astype(jnp.bfloat16), projected[2].astype(jnp.bfloat16)], axis=1
            )
            for part in range(begin // part_rows, (begin + count) // part_rows):

                @pl.when(jnp.logical_not(last))
                def _():
                    send_up(at.seq, 0, part).start()

                @pl.when(jnp.logical_not(first))
                def _():
                    send_down(at.seq, 0, part).start()

    head_load.wait()
    head_wide[pl.ds(0, 2 * bin_count)] = head_raw[...].astype(jnp.float32)
    tail_rows = head_wide.shape[0] - 2 * bin_count
    head_wide[pl.ds(2 * bin_count, tail_rows)] = jnp.zeros((tail_rows, width), jnp.float32)
    head_own[pl.ds(0, padded_bins)] = head_wide[pl.ds(0, padded_bins)].astype(jnp.bfloat16)
    head_own[pl.ds(padded_bins, padded_bins)] = head_wide[pl.ds(bin_count, padded_bins)].astype(
        jnp.bfloat16
    )

    weights[5].start()
    acc[...] = jnp.zeros_like(acc)
    l_acc[...] = jnp.zeros_like(l_acc)
    tile = total // 3
    keys = rows // 2

    def attend(block, pair):
        frame = block * rows + pair * keys + lax.broadcasted_iota(jnp.int32, (1, keys), 1)
        live = frame < used_ref[0]
        sharps = [temp_ref[h] * 1.4426950408889634 for h in range(local_heads)]
        biases = [jnp.where(live, -sharp, -1e30) for sharp in sharps]
        held = pl.ds(pl.multiple_of(pair * keys, keys) if not isinstance(pair, int) else pair * keys, keys)
        key, value = kvbuf[block, held, :width], kvbuf[block, held, width:]
        for index in range(3):
            span = pl.ds(index * tile, tile)
            scores = lax.dot_general(
                jnp.concatenate([q_scr[h, span] for h in range(local_heads)]),
                key,
                (((1,), (1,)), ((), ())),
                preferred_element_type=jnp.float32,
            )
            chances = []
            for h in range(local_heads):
                chance = jnp.exp2(scores[h * tile : (h + 1) * tile] * sharps[h] + biases[h])
                part = chance[:, :128]
                for lane in range(128, keys, 128):
                    part = part + chance[:, lane : lane + 128]
                l_acc[h, span] += part
                chances.append(chance.astype(jnp.bfloat16))
            summed = jnp.dot(
                jnp.concatenate(chances), value, preferred_element_type=jnp.float32
            )
            for h in range(local_heads):
                acc[h, span] += summed[h * tile : (h + 1) * tile]

    order = [("cross", 0), ("cross", 1), ("cross", 2), ("over", 0), ("cross", 3), ("over", 1),
             ("cross", 4), ("over", 2)]
    stages = [0, 1, 2, 2, 4, 4, 5, 5]

    def relays(stage, later=False):
        for (kind, index), own_stage in zip(order, stages):
            if own_stage == stage or (later and own_stage > stage):
                if kind == "cross":
                    weights[index].relay_cross()
                else:
                    weights[index].relay_over()

    pairs_of = 2
    turns = PARTS // pairs_of
    rounds = pairs_of * (at.seqs - 1)

    def exchange(index, carry):
        step, pair = index // pairs_of, lax.rem(index, pairs_of)
        before = jnp.maximum(index - 1, 0)
        old_step, old_pair = before // pairs_of, lax.rem(before, pairs_of)
        arriving = index < rounds

        for turn in range(turns):
            part = turns * pair + turn

            @pl.when(arriving & (step < at.seq))
            def _():
                block = at.seq - 1 - step
                send_up(block, step, part).wait_recv()

                @pl.when(jnp.logical_not(last))
                def _():
                    send_up(block, step + 1, part).start()

            @pl.when(arriving & (step < at.seqs - 1 - at.seq))
            def _():
                block = at.seq + 1 + step
                send_down(block, step, part).wait_recv()

                @pl.when(jnp.logical_not(first))
                def _():
                    send_down(block, step + 1, part).start()

            if turn == turns // 2 - 1:

                @pl.when((index > 0) & (old_step < at.seq))
                def _():
                    attend(at.seq - 1 - old_step, old_pair)

            if turn == turns - 1:

                @pl.when((index > 0) & (old_step < at.seqs - 1 - at.seq))
                def _():
                    attend(at.seq + 1 + old_step, old_pair)

        @pl.when((index > 0) & (index <= pairs_of))
        def _():
            attend(at.seq, index - 1)

        for stage in range(min(6, rounds)):

            @pl.when(index == stage)
            def _():
                relays(stage)

        return carry

    lax.fori_loop(0, rounds + 1, exchange, 0)
    if rounds < 6:
        relays(rounds, later=True)

    early = at.heads == 2
    near = rows // 2 + HALO
    far = rows - near

    def near_at(head):
        return pl.multiple_of(jnp.where(head == 0, far, 0), HALO) if early else 0

    def far_at(head):
        return pl.multiple_of(jnp.where(head == 0, 0, near), HALO) if early else near

    tiles = [(near_at, near), (rows, 2 * HALO), (far_at, far)]
    gathers = [
        Spread(at, att, span, (a_send.at[p], a_recv.at[p])) for p, span in enumerate(tiles)
    ]

    def attended(begin, count):
        span = pl.ds(begin, count)
        value = jnp.zeros((count, width), jnp.float32)
        for h in range(local_heads):
            mean = acc[h, span] / jnp.sum(l_acc[h, span], axis=-1, keepdims=True)
            value = jnp.where(in_head[h], mean, value)
        att[at.me, span] = value.astype(jnp.bfloat16)

    other = at.head_at(1)
    attended(near_at(other), near)
    if early:
        gathers[0].cross(1).start()
    attended(rows, 2 * HALO)
    attended(far_at(other), far)
    if early:
        gathers[1].start()
        gathers[0].aside(0).start()
        gathers[2].start()
    else:
        for gather in gathers:
            gather.start()
    weights[5].relay_cross()

    def drain(step, carry):
        @pl.when(jnp.logical_not(last) & (step <= at.seq))
        def _():
            for part in range(PARTS):
                send_up(at.seq - step, step, part).wait_send()

        @pl.when(jnp.logical_not(first) & (step <= at.seqs - 1 - at.seq))
        def _():
            for part in range(PARTS):
                send_down(at.seq + step, step, part).wait_send()

        return carry

    lax.fori_loop(0, at.seqs - 1, drain, 0)
    for copy in conv_loads:
        copy.wait()
    weights[0].finish()
    weights[3].relay_over()
    channel_tiles = gated.shape[0]
    gated[:, pl.ds(total, gated.shape[1] - total)] = jnp.zeros(
        (channel_tiles, gated.shape[1] - total, 128), jnp.float32
    )
    zero_first = jnp.where(first, 0.0, 1.0)
    zero_last = jnp.where(last, 0.0, 1.0)

    def convolution_input(pieces):
        for piece_at in pieces:
            gathers[piece_at].relay()
            gathers[piece_at].finish()
        spans = [
            pl.ds(tiles[p][0](at.head) if callable(tiles[p][0]) else tiles[p][0], tiles[p][1])
            for p in pieces
        ]

        def gathered(buffer, block):
            return jnp.concatenate([buffer[block, span] for span in spans])

        base = jnp.concatenate([gathered(emb, block) for block in range(blocks)], axis=1)
        summed = base.astype(jnp.float32) + mix(
            [gathered(att, block) for block in range(blocks)], fulls[0]
        )
        body_rows = tiles[pieces[0]][1]
        targets = [(0, body_rows, pl.multiple_of(spans[0].start + HALO, HALO))]
        if len(pieces) > 1:
            summed = jnp.concatenate(
                [
                    summed[:body_rows],
                    summed[body_rows : body_rows + HALO] * zero_first,
                    summed[body_rows + HALO :] * zero_last,
                ]
            )
            targets += [(body_rows, HALO, 0), (body_rows + HALO, HALO, total - HALO)]
        normed = norm_rows(summed).astype(jnp.bfloat16)
        value = jnp.dot(normed, conv_in[0], preferred_element_type=jnp.float32)
        signal = jnp.dot(normed, conv_in[1], preferred_element_type=jnp.float32)
        gate = (value * jax.nn.sigmoid(signal)).astype(jnp.bfloat16).astype(jnp.float32)
        for low, length, start in targets:
            target = pl.ds(start, length)
            stream[target] = summed[low : low + length]
            for c in range(channel_tiles):
                gated[c, target] = gate[low : low + length, c * 128 : (c + 1) * 128]

    convolution_input([0, 1])
    if not early:
        convolution_input([2])
    first_tap = HALO - rim - taps // 2
    lead = first_tap % 8
    chunk = span_rows // 2

    def convolve(member):
        base_row = pl.multiple_of(member * slab + first_tap - lead, 8)
        outs = []
        for part in range(2):
            line = []
            for c in range(channel_tiles):
                kernel = conv_kernel[:, c * 128 : (c + 1) * 128]
                reach = up_to(chunk + taps + lead, 8)
                source = gated[c, pl.ds(base_row + part * chunk, reach)]
                result = jnp.zeros((chunk, 128), jnp.float32)
                for turn in range(8):
                    shifted = source[turn:] if turn else source
                    for k in range(taps):
                        offset = lead + k - turn
                        if offset % 8 == 0 and offset >= 0:
                            result = result + kernel[k : k + 1] * shifted[offset : offset + chunk]
                line.append((result * jax.nn.sigmoid(result)).astype(jnp.bfloat16))
            outs.append(jnp.concatenate(line, axis=1))
        return jnp.concatenate(outs)

    def swap(slot, step, other, source):
        head, sub = at.head_at(step), lax.rem(at.sub + other, 2)
        if source is None:
            block = at.head_at(at.heads - step) * 2 + sub
            view = win.at[head * 2 + sub], act.at[block]
        else:
            view = win.at[head * 2 + sub], act.at[source]
        return remote(*view, s_send.at[slot], s_recv.at[slot], head=head, sub=sub)

    peers = [(step, other) for step in range(1, at.heads) for other in range(2)] + [(0, 1)]
    for slot, (step, other) in enumerate(peers):
        if step == 0 and early:
            convolution_input([2])
        member = at.head_at(step) * 2 + lax.rem(at.sub + other, 2)
        win[member] = convolve(member)
        swap(slot, step, other, at.me).start()
    act[at.me] = convolve(at.me)

    weights[4].relay_over()
    weights[1].finish()
    def received(step):
        for slot, peer in enumerate(peers):
            if peer[0] == step:
                swap(slot, *peer, at.me).wait_send()
                swap(slot, *peer, None).wait_recv()
        pair_at = at.head_at(at.heads - step) * 2
        return jnp.dot(
            jnp.concatenate([act[pair_at], act[pair_at + 1]], axis=1),
            fulls[1][pl.ds(pair_at, 2)].reshape(-1, fulls[1].shape[2]),
            preferred_element_type=jnp.float32,
        )

    conv_sum = received(0)
    for step in range(1, at.heads):
        conv_sum = conv_sum + received(step)

    window_at = HALO - rim
    slack = window_at % 8
    around = stream[pl.ds(pl.multiple_of(at.me * slab + window_at - slack, 8), span_rows + 8)]
    features = norm_rows(around[slack : slack + span_rows] + conv_sum)
    feat_out[...] = features[rim : rim + slab].astype(jnp.bfloat16)
    feat_store = load(feat_out, feat_hbm)
    first_frame = at.seq * rows + at.me * slab - rim
    frames = first_frame + lax.broadcasted_iota(jnp.int32, (span_rows, 1), 0)
    weights[5].relay_over()
    weights[2].finish()
    base_rows = jnp.dot(
        features.astype(jnp.bfloat16),
        fulls[2][...].reshape(-1, fulls[2].shape[2]),
        preferred_element_type=jnp.float32,
    )
    base_rows = norm_rows(jnp.where((frames >= 0) & (frames < used_ref[0]), base_rows, 0.0))
    for copy in late_loads:
        copy.wait()
    voc_rows = up_to(slab + parts, 8)
    vdepth = jnp.zeros((voc_rows, base_rows.shape[1]), jnp.float32)
    for k in range(2 * half_voc + 1):
        vdepth = vdepth + voc_kernel[k : k + 1] * base_rows[k : k + voc_rows]
    inner = norm_rows(vdepth).astype(jnp.bfloat16)
    weights[3].finish()
    hidden = jnp.dot(
        inner, fulls[3][...].reshape(-1, fulls[3].shape[2]), preferred_element_type=jnp.float32
    )
    hidden = (0.5 * hidden * (1.0 + lax.erf(hidden * math.sqrt(0.5)))).astype(jnp.bfloat16)
    weights[4].finish()
    refined = base_rows[half_voc : half_voc + voc_rows] + jnp.dot(
        hidden, fulls[4][...].reshape(-1, fulls[4].shape[2]), preferred_element_type=jnp.float32
    )
    head_input = norm_rows(refined).astype(jnp.bfloat16)
    weights[5].finish()

    bias_row = bias_ref[...].reshape(1, 2 * bin_count)
    biases = [
        bias_row[:, :padded_bins],
        jnp.concatenate(
            [bias_row[:, bin_count:], jnp.zeros((1, padded_bins - bin_count), jnp.float32)], axis=1
        ),
    ]

    def spectrum(index):
        parts_of = [
            fulls[5][block, pl.ds(index * padded_bins, padded_bins)] for block in range(blocks)
        ]
        inputs = [head_input]
        if width % 128 == 0:
            parts_of = [jnp.concatenate(parts_of, axis=1)]
        else:
            inputs = [head_input[:, block * width : (block + 1) * width] for block in range(blocks)]
        result = 0.0
        for one_input, part in zip(inputs, parts_of):
            result = result + lax.dot_general(
                one_input, part, (((1,), (1,)), ((), ())), preferred_element_type=jnp.float32
            )
        return result + biases[index]

    magnitude = jnp.minimum(jnp.exp(spectrum(0)), 100.0)
    sine, cosine = sine_cosine(spectrum(1))
    wave_frames = first_frame + half_voc + lax.broadcasted_iota(jnp.int32, (voc_rows, 1), 0)
    exists = (wave_frames >= 0) & (wave_frames < at.seqs * rows)
    magnitude = jnp.where(exists, magnitude, 0.0)
    waves = jnp.dot(
        (magnitude * cosine).astype(jnp.bfloat16),
        dft[pl.ds(0, padded_bins)],
        preferred_element_type=jnp.float32,
    ) + jnp.dot(
        (magnitude * sine).astype(jnp.bfloat16),
        dft[pl.ds(padded_bins, padded_bins)],
        preferred_element_type=jnp.float32,
    )
    there = jnp.where(exists, 1.0, 0.0)
    total_audio = jnp.zeros((slab, padded_hop), jnp.float32)
    energy = jnp.zeros((slab, padded_hop), jnp.float32)
    for quarter in range(parts):
        begin = parts - quarter
        total_audio = total_audio + waves[
            begin : begin + slab, quarter * padded_hop : (quarter + 1) * padded_hop
        ]
        energy = energy + there[begin : begin + slab] * env_ref[quarter : quarter + 1]
    total_audio = total_audio / energy
    for c in range(padded_hop // 128):
        audio[c] = total_audio[:, c * 128 : (c + 1) * 128]
    pairs = slab // 2
    group = 2 * HOP // 128
    low_lanes = lax.broadcasted_iota(jnp.int32, (1, 128), 1) < HOP % 128
    even = [audio[c, pl.ds(0, pairs, stride=2)] for c in range(padded_hop // 128)]
    odd = [
        pltpu.roll(audio[c, pl.ds(1, pairs, stride=2)], HOP % 128, 1)
        for c in range(padded_hop // 128)
    ]
    full_tiles = HOP // 128
    lines = even[:full_tiles] + [jnp.where(low_lanes, even[full_tiles], odd[0])]
    for c in range(full_tiles):
        lines.append(jnp.where(low_lanes, odd[c], odd[c + 1]))
    for index in range(group):
        wave_out[pl.ds(index, pairs, stride=group)] = lines[index]
    load(wave_out, wave_hbm).wait()
    feat_store.wait()


def hand_over(features, wave, features_out, wave_out, sems):
    copies = [
        pltpu.make_async_copy(features, features_out, sems.at[0]),
        pltpu.make_async_copy(wave, wave_out, sems.at[1]),
    ]
    for copy in copies:
        copy.start()
    for copy in copies:
        copy.wait()


def local(
    tokens,
    masked,
    used_frames,
    tables,
    mask_vec,
    attn_in,
    head_temp,
    attn_out,
    conv_in,
    conv_kernel,
    conv_out,
    voc_in,
    voc_kernel,
    voc_up,
    voc_down,
    voc_head,
    head_bias,
):
    groups, heads, seqs = (lax.axis_size(name) for name in ("groups", "head", "seq"))
    blocks = lax.axis_size(("head", "sub"))
    rows = tokens.shape[1]
    total = rows + 2 * HALO
    slab = rows // blocks
    columns = tables.shape[2]
    width = attn_in.shape[2]
    local_heads = head_temp.shape[0]
    bin_count = head_bias.shape[0] // 2
    fft_size = 2 * (bin_count - 1)
    parts = fft_size // HOP
    padded_bins = up_to(bin_count, 16)
    padded_hop = up_to(HOP, 128)
    rim = voc_kernel.shape[0] // 2 + parts // 2
    window_rows = up_to(slab + 2 * rim, 16)
    channels = conv_kernel.shape[1]
    dft, env = synthesis_constants(bin_count, fft_size, padded_bins, padded_hop)
    head_rows = voc_head.T
    owns = (attn_out, conv_out, voc_in, voc_up, voc_down, head_rows)
    vmem = pl.BlockSpec(memory_space=pltpu.VMEM)
    smem = pl.BlockSpec(memory_space=pltpu.SMEM)
    anywhere = pl.BlockSpec(memory_space=pl.ANY)
    dma = pltpu.SemaphoreType.DMA
    bf16, f32 = jnp.bfloat16, jnp.float32
    full_shapes = [(blocks,) + own.shape for own in owns[:5]] + [(blocks, 2 * padded_bins, width)]
    scratch = [pltpu.VMEM(shape, bf16) for shape in full_shapes]
    scratch += [
        pltpu.VMEM(tables.shape, bf16),
        pltpu.VMEM((1, attn_in.shape[1], 3 * width) if width % 128 == 0 else attn_in.shape, bf16),
        pltpu.VMEM(conv_in.shape, bf16),
        pltpu.VMEM(conv_kernel.shape, f32),
        pltpu.VMEM(voc_kernel.shape, f32),
        pltpu.VMEM(dft.shape, bf16),
        pltpu.VMEM(head_rows.shape, bf16),
        pltpu.VMEM((up_to(bin_count + padded_bins, 8), width), f32),
        pltpu.VMEM((2 * padded_bins, width), bf16),
        pltpu.VMEM((8, rows), f32),
        pltpu.VMEM((2, 8, 128), f32),
        pltpu.VMEM((blocks, total, columns), bf16),
        pltpu.VMEM((blocks, total, width), bf16),
        pltpu.VMEM((seqs, rows, 2 * width), bf16),
        pltpu.VMEM((local_heads, total, width), bf16),
        pltpu.VMEM((local_heads, total, width), f32),
        pltpu.VMEM((local_heads, total, 128), f32),
        pltpu.VMEM((total, columns * blocks), f32),
        pltpu.VMEM((channels // 128, total + 64, 128), f32),
        pltpu.VMEM((blocks, window_rows, channels), bf16),
        pltpu.VMEM((blocks, window_rows, channels), bf16),
        pltpu.VMEM((padded_hop // 128, slab, 128), f32),
        pltpu.VMEM((slab, columns * blocks), bf16),
        pltpu.VMEM((slab * HOP // 128, 128), f32),
        dma((11,)),
        dma((2,)),
        dma((2,)),
        dma((PARTS + 1, 2 * heads)),
        dma((PARTS + 1, 2 * heads)),
        dma((3, 2 * heads)),
        dma((3, 2 * heads)),
        dma((seqs, PARTS)),
        dma((seqs, PARTS)),
        dma((seqs, PARTS)),
        dma((seqs, PARTS)),
        dma((blocks,)),
        dma((blocks,)),
    ]
    for _ in owns:
        scratch += weight_sems(heads, groups)
    sizes = (local_heads, width // local_heads, bin_count, padded_bins, fft_size)
    features, wave = pl.pallas_call(
        functools.partial(block_kernel, sizes),
        out_shape=[
            jax.ShapeDtypeStruct((slab, columns * blocks), bf16),
            jax.ShapeDtypeStruct((slab * HOP // 128, 128), f32),
        ],
        in_specs=[smem] * 2 + [vmem] * 5 + [anywhere] * (6 + WEIGHTS),
        out_specs=[anywhere, anywhere],
        scratch_shapes=scratch,
        compiler_params=pltpu.CompilerParams(
            collective_id=0, has_side_effects=True, vmem_limit_bytes=60 * 1024 * 1024
        ),
    )(
        used_frames, head_temp, tokens, masked, mask_vec, head_bias, env, tables, attn_in, conv_in, conv_kernel, voc_kernel, dft, *owns)
    features, wave = pl.pallas_call(
        hand_over,
        out_shape=[jax.ShapeDtypeStruct(out.shape, out.dtype) for out in (features, wave)],
        in_specs=[vmem] * 2,
        out_specs=[anywhere] * 2,
        scratch_shapes=[dma((2,))],
    )(features, wave)
    return features, wave.reshape(slab * HOP)


def solution(mesh):
    in_specs = (
        P(None, ("groups", "seq")),
        P(("groups", "seq")),
        P("groups"),
        P(None, None, ("head", "sub")),
        P(("head", "sub")),
        P(None, None, ("head", "sub")),
        P(("head", "sub")),
        P(("head", "sub"), None),
        P(None, None, ("head", "sub")),
        P(None, ("head", "sub")),
        P(("head", "sub"), None),
        P(("head", "sub"), None),
        P(),
        P(("head", "sub"), None),
        P(("head", "sub"), None),
        P(("head", "sub"), None),
        P(),
    )
    out_specs = (P(("groups", "seq", "head", "sub"), None), P(("groups", "seq", "head", "sub")))
    return jax.shard_map(local, mesh=mesh, in_specs=in_specs, out_specs=out_specs, check_vma=False)
```
